512 devices in a mesh: vec: 4 (over y_lo, core), row: 8 (over x, y_hi), col: 16 (over z).
Axes of the slice: x: 4, y: 4 (y_hi: 2, y_lo: 2; y = y_hi * 2 + y_lo), z: 16, core: 2. Of those that a mesh axis runs over, the one named last changes fastest.
Arguments:
- checkpoints: float32 [2, 2, 16, 256, 2048], P(None, None, 'vec', 'row', 'col'), may hold values from -6 to 6
- adjoints_in: float32 [2, 16, 256, 2048], P(None, 'vec', 'row', 'col'), may hold values from -4 to 4
- vector_bits: int32 [16, 256, 2048], P('vec', 'row', 'col'), may hold values 0 or 1
- potential_int: int32 [256, 2048], P('row', 'col'), may hold values from -32767 to 32767
- pot_scale: float32 [1], replicated, may hold values from 1.5e-05 to 9e-05
- energies: float32 [16], replicated, may hold values from -0.9 to 0.9
- residual: float32 [16, 256, 2048], P(None, 'row', 'col'), may hold values from -6 to 6
- first_segment: int32 [1], replicated, may hold values from 0 to 62
Outputs:
- potential_grad: float32 [256, 2048], P('row', 'col')
- adjoint_out: float32 [2, 16, 256, 2048], P(None, 'vec', 'row', 'col')
The draws below stay inside these ranges and needn't reach their ends.
All inputs are finite; a program needn't handle non-finite values. No bound on the sum of `vector_bits` on one device may be relied on, other than what follows from the above.
Results may differ from the reference program's by a relative error of at most 0.0003.
Values sent between devices are 32-bit elements; how exact they have to be, the bound alone decides.
No kernel may reach another device: no remote copies, remote signals or barrier semaphores. Data moves between devices by JAX's collectives and lax.ppermute only.
A program may use at most 64 MiB of HBM per device.

```python
import math
import jax
import jax.numpy as jnp
from jax import lax

VEC_DEV = 4
SEG = 16
MOMENTS = 1024
ENERGIES = 16
QMAX = 32767
NR = 256
NC = 2048
NVEC = 16


def plant(result, stream_key, least, largest):
    index_at = [jax.random.randint(jax.random.fold_in(stream_key, axis), (), 0, length) for axis, length in enumerate(result.shape)]
    longest = result.shape.index(max(result.shape))
    next_to = index_at[:longest] + [(index_at[longest] + 1) % result.shape[longest]] + index_at[longest + 1:]
    return result.at[tuple(index_at)].set(least).at[tuple(next_to)].set(largest)


def levels(stream_key, extent, pieces, low, high):
    gain, own = 1.0, jax.random.fold_in(stream_key, 6)
    for axis_at, parts in pieces:
        draws = jnp.exp(jax.random.uniform(jax.random.fold_in(own, axis_at), (parts,), jnp.float32, low / len(pieces), high / len(pieces)))
        gain = gain * jnp.repeat(draws, extent[axis_at] // parts).reshape([-1 if axis == axis_at else 1 for axis in range(len(extent))])
    return gain


def scatter_about(stream_key, shape, width, limit, shards=(), kind=jnp.bfloat16):
    gain = levels(stream_key, shape, shards, -0.22, 0.18) if shards else 1.0
    array = jax.random.normal(stream_key, shape, jnp.float32) * width * gain
    return jnp.minimum(jnp.maximum(array, -limit), limit).astype(kind)


def setup_inputs(seed: int = 0) -> dict:
    key_list = jax.random.split(jax.random.key(seed), 9)
    return {
        "checkpoints": scatter_about(key_list[0], (2, 2, NVEC, NR, NC), 1.0, 6.0, ((2, 4), (3, 8), (4, 16)), jnp.float32),
        "adjoints_in": scatter_about(key_list[1], (2, NVEC, NR, NC), 0.3, 4.0, ((1, 4), (2, 8), (3, 16)), jnp.float32),
        "vector_bits": plant((jax.random.randint(key_list[2], (NVEC, NR, NC), 0, 2) < 1).astype(jnp.int32), jax.random.fold_in(key_list[2], 1), 0, 1),
        "potential_int": plant(jax.random.randint(key_list[3], (NR, NC), -QMAX, QMAX + 1), jax.random.fold_in(key_list[3], 1), -QMAX, QMAX).astype(jnp.int32),
        "pot_scale": jnp.clip(jnp.exp(jax.random.uniform(key_list[4], (1,), jnp.float32, math.log(1.4999999621068127e-05), math.log(9.000000136438757e-05))), 1.4999999621068127e-05, 9.000000136438757e-05),
        "energies": jnp.clip(jax.random.uniform(key_list[5], (ENERGIES,), jnp.float32, -0.9, 0.9), -0.9, 0.9),
        "residual": scatter_about(key_list[6], (ENERGIES, NR, NC), 1.0, 6.0, ((1, 8), (2, 16)), jnp.float32),
        "first_segment": jax.random.randint(key_list[7], (1,), 0, MOMENTS // SEG - 1).astype(jnp.int32),
    }


def window_coefs(first_segment, energies):
    moment_order = first_segment[0] * SEG + jnp.arange(2 * SEG, dtype=jnp.int32)
    degree = moment_order.astype(jnp.float32)
    kernel_norm = float(MOMENTS + 1)
    angle_step = math.pi / kernel_norm
    jackson = ((kernel_norm - degree) * jnp.cos(angle_step * degree) + jnp.sin(angle_step * degree) * (math.cos(angle_step) / math.sin(angle_step))) / kernel_norm
    factor = jnp.where(moment_order == 0, 1.0, 2.0).astype(jnp.float32)
    angles = jnp.arccos(energies)
    cosines = jnp.cos(degree[:, None] * angles[None, :])
    return (jackson * factor)[:, None] * cosines / (math.pi * jnp.sin(angles))[None, :]


def apply_operator(values, onsite, inv_span):
    beside = jnp.roll(values, 1, -2) + jnp.roll(values, -1, -2) + jnp.roll(values, 1, -1) + jnp.roll(values, -1, -1)
    return inv_span * (onsite * values - beside)


def reference(checkpoints, adjoints_in, vector_bits, potential_int, pot_scale, energies, residual, first_segment):
    pot_factor = pot_scale[0]
    inv_span = 1.0 / (4.5 + QMAX * pot_factor)
    onsite = potential_int.astype(jnp.float32) * pot_factor
    coefficients = window_coefs(first_segment, energies)
    weights = jnp.einsum("ne,eij->nij", coefficients, residual, precision=lax.Precision.HIGHEST)
    inv_count = 1.0 / NVEC
    gradient = jnp.zeros((NR, NC), jnp.float32)
    adjoint_blocks = []
    for first_vec in range(0, NVEC, VEC_DEV):
        saved = checkpoints[:, :, first_vec:first_vec + VEC_DEV]
        sign_weights = (2 * vector_bits[first_vec:first_vec + VEC_DEV] - 1).astype(jnp.float32) * inv_count
        states = []
        for segment in range(2):
            earlier = saved[segment, 0]
            current = saved[segment, 1]
            states.extend([earlier, current])
            for offset in range(2, SEG):
                advanced = 2.0 * apply_operator(current, onsite, inv_span) - earlier
                states.append(advanced)
                earlier, current = current, advanced
        after_one = adjoints_in[0, first_vec:first_vec + VEC_DEV]
        after_two = adjoints_in[1, first_vec:first_vec + VEC_DEV]
        for offset in range(2 * SEG - 1, -1, -1):
            gradient = gradient + jnp.sum(after_one * states[offset], axis=0)
            advanced = weights[offset] * sign_weights + 2.0 * apply_operator(after_one, onsite, inv_span) - after_two
            after_two, after_one = after_one, advanced
        adjoint_blocks.append(jnp.stack([after_one, after_two]))
    return gradient * (2.0 * inv_span), jnp.concatenate(adjoint_blocks, axis=1)
```

```python
import functools
import math

import jax
import jax.numpy as jnp
from jax import lax
from jax.experimental import pallas as pl
from jax.experimental.pallas import tpu as pltpu
from jax.sharding import PartitionSpec as P

SEG = 16
MOMENTS = 1024
QMAX = 32767
TERMS = 2 * SEG

ADJ, SGN, RES, ONS = 0, 8, 12, 28
PLANES = 29
ROWS = 32
HALO = 32
EXT = ROWS + 2 * HALO
FHALO = 16
FEXT = ROWS + 2 * FHALO
LANES = 128
FPLANES = 16
MAIN = PLANES * ROWS
G_ADJ = 7 * EXT
G_ONS = EXT // 4
G_ROWS = G_ADJ + G_ONS + 2 * FEXT


def window_coefs(first_segment, energies):
    moment_order = first_segment[0] * SEG + jnp.arange(TERMS, dtype=jnp.int32)
    degree = moment_order.astype(jnp.float32)
    kernel_norm = float(MOMENTS + 1)
    angle_step = math.pi / kernel_norm
    jackson = (
        (kernel_norm - degree) * jnp.cos(angle_step * degree)
        + jnp.sin(angle_step * degree) * (math.cos(angle_step) / math.sin(angle_step))
    ) / kernel_norm
    factor = jnp.where(moment_order == 0, 1.0, 2.0).astype(jnp.float32)
    angles = jnp.arccos(energies)
    cosines = jnp.cos(degree[:, None] * angles[None, :])
    return (jackson * factor)[:, None] * cosines / (math.pi * jnp.sin(angles))[None, :]


def lane_iota():
    return lax.broadcasted_iota(jnp.int32, (8, LANES), 1)


def sub_iota():
    return lax.broadcasted_iota(jnp.int32, (8, LANES), 0)


def tile(ref, row):
    return ref[pl.ds(row, 8), :]


def main_tile(own, above, below, plane, t):
    section = (above, own, below)[t // 4]
    return tile(section, plane * ROWS + (t % 4) * 8)


def fwd_tile(chk, above, below, plane, t):
    if t < 2:
        return tile(above, MAIN + plane * FHALO + t * 8)
    if t < 6:
        return tile(chk, plane * ROWS + (t - 2) * 8)
    return tile(below, MAIN + plane * FHALO + (t - 6) * 8)


def pack_kernel(own, chk, above, below, to_left, to_right):
    lane = lane_iota()

    def pack(tiles, row):
        count = len(tiles)
        width = LANES // count
        group = lane // width
        left = right = None
        for j, value in enumerate(tiles):
            rolled = pltpu.roll(value, width * j, 1) if j else value
            left = rolled if j == 0 else jnp.where(group == j, rolled, left)
            right = rolled if j == 0 else jnp.where(group == (j + count - 1) % count, rolled, right)
        to_left[pl.ds(row, 8), :] = left
        to_right[pl.ds(row, 8), :] = right

    for g in range(7):
        for t in range(EXT // 8):
            pack([main_tile(own, above, below, 4 * g + j, t) for j in range(4)], g * EXT + t * 8)
    for m in range(3):
        pack([main_tile(own, above, below, ONS, 3 * j + m) for j in range(4)], G_ADJ + m * 8)
    for g in range(2):
        for t in range(FEXT // 8):
            pack(
                [fwd_tile(chk, above, below, 8 * g + j, t) for j in range(8)],
                G_ADJ + G_ONS + g * FEXT + t * 8,
            )


def main_kernel(
    coef, scale, own, chk, above, below, from_right, from_left,
    adj_out, grad_out,
    xc, xh, sgc, sgh, rsc, rsh, onc, onh, fc, fh, vs,
):
    lane = lane_iota()
    sub = sub_iota()
    first_lane, last_lane = lane == 0, lane == LANES - 1
    first_sub, last_sub = sub == 0, sub == 7
    s = scale[0]

    def strip(row, j, count):
        width = LANES // count
        mixed = jnp.where(lane // width == j, tile(from_right, row), tile(from_left, row))
        return pltpu.roll(mixed, (LANES - width * j) % LANES, 1) if j else mixed

    for t in range(EXT // 8):
        for plane in range(8):
            xc[plane, pl.ds(t * 8, 8), :] = main_tile(own, above, below, plane, t)
            xh[plane, pl.ds(t * 8, 8), :] = strip((plane // 4) * EXT + t * 8, plane % 4, 4)
        for v in range(4):
            sgc[v, pl.ds(t * 8, 8), :] = main_tile(own, above, below, SGN + v, t)
            sgh[v, pl.ds(t * 8, 8), :] = strip(2 * EXT + t * 8, v, 4)
        for e in range(16):
            rsc[e, pl.ds(t * 8, 8), :] = main_tile(own, above, below, RES + e, t)
            rsh[e, pl.ds(t * 8, 8), :] = strip((3 + e // 4) * EXT + t * 8, e % 4, 4)
        onc[pl.ds(t * 8, 8), :] = main_tile(own, above, below, ONS, t) * s
        onh[pl.ds(t * 8, 8), :] = strip(G_ADJ + (t % 3) * 8, t // 3, 4) * s
    for t in range(FEXT // 8):
        for plane in range(FPLANES):
            fc[plane, pl.ds(t * 8, 8), :] = fwd_tile(chk, above, below, plane, t)
            fh[plane, pl.ds(t * 8, 8), :] = strip(
                G_ADJ + G_ONS + (plane // 8) * FEXT + t * 8, plane % 8, 8
            )
    for segment in range(2):
        for which in range(2):
            for v in range(4):
                for i in range(4):
                    vs[segment * SEG + which, v, pl.ds(i * 8, 8), :] = tile(
                        chk, (segment * 8 + which * 4 + v) * ROWS + i * 8
                    )

    def neighbours(cref, href, plane, lo, hi, count):
        def load(t):
            c, h = cref[plane, pl.ds(t * 8, 8), :], href[plane, pl.ds(t * 8, 8), :]
            return c, h

        def rolled(pair, shift):
            return tuple(pltpu.roll(p, shift, 0) for p in pair)

        here = load(lo)
        prev_up = rolled(load(lo - 1) if lo > 0 else here, 1)
        here_up = rolled(here, 1)
        here_down = rolled(here, 7)
        for t in range(lo, hi):
            after = load(t + 1) if t + 1 < count else here
            after_up, after_down = rolled(after, 1), rolled(after, 7)
            c, h = here
            cl, cr = pltpu.roll(c, 1, 1), pltpu.roll(c, LANES - 1, 1)
            hl, hr = pltpu.roll(h, 1, 1), pltpu.roll(h, LANES - 1, 1)
            side_c = jnp.where(first_lane, hl, cl) + jnp.where(last_lane, hr, cr)
            side_h = jnp.where(first_lane, cl, hl) + jnp.where(last_lane, cr, hr)
            vert = [
                jnp.where(first_sub, prev_up[k], here_up[k])
                + jnp.where(last_sub, after_down[k], here_down[k])
                for k in range(2)
            ]
            yield t, c, h, side_c + vert[0], side_h + vert[1]
            here, prev_up, here_up, here_down = after, here_up, after_up, after_down

    def forward(k, new, old, lo, hi):
        for segment in range(2):
            for v in range(4):
                p_new = segment * 8 + new * 4 + v
                p_old = segment * 8 + old * 4 + v
                for t, c, h, nc, nh in neighbours(fc, fh, p_new, lo, hi, FEXT // 8):
                    row = pl.ds(t * 8, 8)
                    on = pl.ds(t * 8 + HALO - FHALO, 8)
                    out_c = onc[on, :] * c - s * nc - fc[p_old, row, :]
                    out_h = onh[on, :] * h - s * nh - fh[p_old, row, :]
                    fc[p_old, row, :] = out_c
                    fh[p_old, row, :] = out_h
                    if 2 <= t < 6:
                        vs[segment * SEG + k, v, pl.ds((t - 2) * 8, 8), :] = out_c

    for start, stop, lo, hi in ((1, 4, 0, 8), (4, 8, 1, 7)):
        def body(i, carry, lo=lo, hi=hi):
            forward(2 * i, 1, 0, lo, hi)
            forward(2 * i + 1, 0, 1, lo, hi)
            return carry
        lax.fori_loop(start, stop, body, 0)

    def adjoint(t_term, new, old, lo, hi, grads):
        grads = list(grads)
        weights = {}
        for t in range(lo, hi):
            wc = wh = None
            row = pl.ds(t * 8, 8)
            for e in range(16):
                q = coef[t_term, e]
                pc, phh = rsc[e, row, :] * q, rsh[e, row, :] * q
                wc, wh = (pc, phh) if wc is None else (wc + pc, wh + phh)
            wcr[row, :] = wc
            whr[row, :] = wh
        for v in range(4):
            p_new, p_old = new * 4 + v, old * 4 + v
            for t, c, h, nc, nh in neighbours(xc, xh, p_new, lo, hi, EXT // 8):
                row = pl.ds(t * 8, 8)
                if 4 <= t < 8:
                    grads[t - 4] = grads[t - 4] + c * vs[t_term, v, pl.ds((t - 4) * 8, 8), :]
                xc[p_old, row, :] = wcr[row, :] * sgc[v, row, :] + (onc[row, :] * c - s * nc) - xc[p_old, row, :]
                xh[p_old, row, :] = whr[row, :] * sgh[v, row, :] + (onh[row, :] * h - s * nh) - xh[p_old, row, :]
        return tuple(grads)

    def run(wc_ref, wh_ref):
        nonlocal wcr, whr
        wcr, whr = wc_ref, wh_ref
        grads = tuple(jnp.zeros((8, LANES), jnp.float32) for _ in range(4))
        for phase in range(4):
            def body(i, carry, phase=phase):
                t_term = TERMS - 1 - 8 * phase - 2 * i
                carry = adjoint(t_term, 0, 1, phase, EXT // 8 - phase, carry)
                return adjoint(t_term - 1, 1, 0, phase, EXT // 8 - phase, carry)
            grads = lax.fori_loop(0, 4, body, grads)
        for i in range(4):
            grad_out[pl.ds(i * 8, 8), :] = grads[i] * s

    wcr = whr = None
    pl.run_scoped(run, pltpu.VMEM((EXT, LANES), jnp.float32), pltpu.VMEM((EXT, LANES), jnp.float32))
    for which in range(2):
        for v in range(4):
            for i in range(4):
                adj_out[which, v, pl.ds(i * 8, 8), :] = xc[which * 4 + v, pl.ds(HALO + i * 8, 8), :]


VMEM_SPEC = pl.BlockSpec(memory_space=pltpu.VMEM)
SMEM_SPEC = pl.BlockSpec(memory_space=pltpu.SMEM)
F32 = jnp.float32


def per_device(
    checkpoints,
    adjoints_in,
    vector_bits,
    potential_int,
    pot_scale,
    energies,
    residual,
    first_segment,
):
    pot_factor = pot_scale[0]
    inv_span = 1.0 / (4.5 + QMAX * pot_factor)
    onsite = potential_int.astype(F32) * pot_factor
    coefs = window_coefs(first_segment, energies)
    vector_count = lax.axis_size("vec") * vector_bits.shape[0]
    signs = (2 * vector_bits - 1).astype(F32) * (1.0 / vector_count)

    own = jnp.concatenate(
        [adjoints_in.reshape(8, ROWS, LANES), signs, residual, onsite[None]], axis=0
    ).reshape(MAIN, LANES)
    chk = checkpoints.reshape(FPLANES, ROWS, LANES)
    to_below = jnp.concatenate([own, chk[:, ROWS - FHALO :].reshape(-1, LANES)], axis=0)
    to_above = jnp.concatenate([own, chk[:, :FHALO].reshape(-1, LANES)], axis=0)
    chk = chk.reshape(FPLANES * ROWS, LANES)

    def shift(value, axis, step):
        n = lax.axis_size(axis)
        return lax.ppermute(value, axis, [(i, (i + step) % n) for i in range(n)])

    above = shift(to_below, "row", 1)
    below = shift(to_above, "row", -1)

    strips = jax.ShapeDtypeStruct((G_ROWS, LANES), F32)
    to_left, to_right = pl.pallas_call(
        pack_kernel,
        out_shape=(strips, strips),
        in_specs=[VMEM_SPEC] * 4,
        out_specs=(VMEM_SPEC, VMEM_SPEC),
        name="pack_columns",
    )(own, chk, above, below)
    from_left = shift(to_right, "col", 1)
    from_right = shift(to_left, "col", -1)

    ext = (EXT, LANES)
    adjoint_out, grad = pl.pallas_call(
        main_kernel,
        out_shape=(
            jax.ShapeDtypeStruct((2, 4, ROWS, LANES), F32),
            jax.ShapeDtypeStruct((ROWS, LANES), F32),
        ),
        in_specs=[SMEM_SPEC, SMEM_SPEC] + [VMEM_SPEC] * 6,
        out_specs=(VMEM_SPEC, VMEM_SPEC),
        scratch_shapes=[
            pltpu.VMEM((8, *ext), F32), pltpu.VMEM((8, *ext), F32),
            pltpu.VMEM((4, *ext), F32), pltpu.VMEM((4, *ext), F32),
            pltpu.VMEM((16, *ext), F32), pltpu.VMEM((16, *ext), F32),
            pltpu.VMEM(ext, F32), pltpu.VMEM(ext, F32),
            pltpu.VMEM((FPLANES, FEXT, LANES), F32), pltpu.VMEM((FPLANES, FEXT, LANES), F32),
            pltpu.VMEM((TERMS, 4, ROWS, LANES), F32),
        ],
        compiler_params=pltpu.CompilerParams(vmem_limit_bytes=40 * 1024 * 1024),
        name="window",
    )(coefs, (2.0 * inv_span)[None], own, chk, above, below, from_right, from_left)

    grad = grad + lax.ppermute(grad, "vec", [(0, 1), (1, 0), (2, 3), (3, 2)])
    grad = grad + lax.ppermute(grad, "vec", [(0, 2), (2, 0), (1, 3), (3, 1)])
    return grad, adjoint_out


def solution(mesh):
    return jax.shard_map(
        per_device,
        mesh=mesh,
        in_specs=(
            P(None, None, "vec", "row", "col"),
            P(None, "vec", "row", "col"),
            P("vec", "row", "col"),
            P("row", "col"),
            P(),
            P(),
            P(None, "row", "col"),
            P(),
        ),
        out_specs=(P("row", "col"), P(None, "vec", "row", "col")),
        check_vma=False,
    )
```

```python
import functools
import math

import jax
import jax.numpy as jnp
from jax import lax
from jax.experimental import pallas as pl
from jax.experimental.pallas import tpu as pltpu
from jax.sharding import PartitionSpec as P

SEG = 16
MOMENTS = 1024
QMAX = 32767
TERMS = 2 * SEG
NVEC = 16
F32 = jnp.float32

ADJ, SGN, RES, ONS = 0, 8, 12, 28
PLANES = 29
ROWS = 32
HALO = 32
EXT = ROWS + 2 * HALO
FHALO = 16
FEXT = ROWS + 2 * FHALO
LANES = 128
FPLANES = 16
MAIN = PLANES * ROWS
G_ADJ = 7 * EXT
G_ONS = EXT // 4
G_ROWS = G_ADJ + G_ONS + 2 * FEXT


def window_coefs(first_segment, energies):
    moment_order = first_segment[0] * SEG + jnp.arange(TERMS, dtype=jnp.int32)
    degree = moment_order.astype(jnp.float32)
    kernel_norm = float(MOMENTS + 1)
    angle_step = math.pi / kernel_norm
    jackson = (
        (kernel_norm - degree) * jnp.cos(angle_step * degree)
        + jnp.sin(angle_step * degree) * (math.cos(angle_step) / math.sin(angle_step))
    ) / kernel_norm
    factor = jnp.where(moment_order == 0, 1.0, 2.0).astype(jnp.float32)
    angles = jnp.arccos(energies)
    cosines = jnp.cos(degree[:, None] * angles[None, :])
    return (jackson * factor)[:, None] * cosines / (math.pi * jnp.sin(angles))[None, :]


def lane_iota():
    return lax.broadcasted_iota(jnp.int32, (8, LANES), 1)


def sub_iota():
    return lax.broadcasted_iota(jnp.int32, (8, LANES), 0)


def tile(ref, row):
    return ref[pl.ds(row, 8), :]


def main_tile(own, above, below, plane, t):
    section = (above, own, below)[t // 4]
    return tile(section, plane * ROWS + (t % 4) * 8)


def fwd_tile(chk, above, below, plane, t):
    if t < 2:
        return tile(above, MAIN + plane * FHALO + t * 8)
    if t < 6:
        return tile(chk, plane * ROWS + (t - 2) * 8)
    return tile(below, MAIN + plane * FHALO + (t - 6) * 8)


def prepare_kernel(factor, adj, bits, pot, res, chk, to_below, to_above, bits_v, pot_v, sems):
    copies = []

    def start(src, dst):
        copy = pltpu.make_async_copy(src, dst, sems.at[len(copies)])
        copy.start()
        copies.append(copy)

    start(bits, bits_v)
    start(pot, pot_v)
    for out, first in ((to_below, ROWS - FHALO), (to_above, 0)):
        start(adj, out.at[pl.ds(ADJ * ROWS, 8 * ROWS)])
        start(res, out.at[pl.ds(RES * ROWS, 16 * ROWS)])
        for plane in range(FPLANES):
            start(
                chk.at[pl.ds(plane * ROWS + first, FHALO)],
                out.at[pl.ds(MAIN + plane * FHALO, FHALO)],
            )
    copies[0].wait()
    signs = (2 * bits_v[...] - 1).astype(F32) * (1.0 / NVEC)
    copies[1].wait()
    onsite = pot_v[...].astype(F32) * factor[0]
    for out in (to_below, to_above):
        out[pl.ds(SGN * ROWS, 4 * ROWS), :] = signs
        out[pl.ds(ONS * ROWS, ROWS), :] = onsite
    for copy in copies[2:]:
        copy.wait()


def pack_kernel(own, chk, above, below, to_left, to_right):
    lane = lane_iota()

    def pack(tiles, row):
        count = len(tiles)
        width = LANES // count
        group = lane // width
        left = right = None
        for j, value in enumerate(tiles):
            rolled = pltpu.roll(value, width * j, 1) if j else value
            left = rolled if j == 0 else jnp.where(group == j, rolled, left)
            right = rolled if j == 0 else jnp.where(group == (j + count - 1) % count, rolled, right)
        to_left[pl.ds(row, 8), :] = left
        to_right[pl.ds(row, 8), :] = right

    for g in range(7):
        for t in range(EXT // 8):
            pack([main_tile(own, above, below, 4 * g + j, t) for j in range(4)], g * EXT + t * 8)
    for m in range(3):
        pack([main_tile(own, above, below, ONS, 3 * j + m) for j in range(4)], G_ADJ + m * 8)
    for g in range(2):
        for t in range(FEXT // 8):
            pack(
                [fwd_tile(chk, above, below, 8 * g + j, t) for j in range(8)],
                G_ADJ + G_ONS + g * FEXT + t * 8,
            )


def main_kernel(
    coef, scale, own, chk, above, below, from_right, from_left,
    adj_out, grad_out,
    xc, xh, sgc, sgh, rsc, rsh, onc, onh, fc, fh, vs,
):
    lane = lane_iota()
    sub = sub_iota()
    first_lane, last_lane = lane == 0, lane == LANES - 1
    first_sub, last_sub = sub == 0, sub == 7
    s = scale[0]

    def strip(row, j, count):
        width = LANES // count
        mixed = jnp.where(lane // width == j, tile(from_right, row), tile(from_left, row))
        return pltpu.roll(mixed, (LANES - width * j) % LANES, 1) if j else mixed

    for t in range(EXT // 8):
        for plane in range(8):
            xc[plane, pl.ds(t * 8, 8), :] = main_tile(own, above, below, plane, t)
            xh[plane, pl.ds(t * 8, 8), :] = strip((plane // 4) * EXT + t * 8, plane % 4, 4)
        for v in range(4):
            sgc[v, pl.ds(t * 8, 8), :] = main_tile(own, above, below, SGN + v, t)
            sgh[v, pl.ds(t * 8, 8), :] = strip(2 * EXT + t * 8, v, 4)
        for e in range(16):
            rsc[e, pl.ds(t * 8, 8), :] = main_tile(own, above, below, RES + e, t)
            rsh[e, pl.ds(t * 8, 8), :] = strip((3 + e // 4) * EXT + t * 8, e % 4, 4)
        onc[pl.ds(t * 8, 8), :] = main_tile(own, above, below, ONS, t)
        onh[pl.ds(t * 8, 8), :] = strip(G_ADJ + (t % 3) * 8, t // 3, 4)
    for t in range(FEXT // 8):
        for plane in range(FPLANES):
            fc[plane, pl.ds(t * 8, 8), :] = fwd_tile(chk, above, below, plane, t)
            fh[plane, pl.ds(t * 8, 8), :] = strip(
                G_ADJ + G_ONS + (plane // 8) * FEXT + t * 8, plane % 8, 8
            )
    for segment in range(2):
        for which in range(2):
            for v in range(4):
                for i in range(4):
                    vs[segment * SEG + which, v, pl.ds(i * 8, 8), :] = tile(
                        chk, (segment * 8 + which * 4 + v) * ROWS + i * 8
                    )

    def neighbours(cref, href, plane, lo, hi, count):
        def load(t):
            c, h = cref[plane, pl.ds(t * 8, 8), :], href[plane, pl.ds(t * 8, 8), :]
            return c, h

        def rolled(pair, shift):
            return tuple(pltpu.roll(p, shift, 0) for p in pair)

        here = load(lo)
        prev_up = rolled(load(lo - 1) if lo > 0 else here, 1)
        here_up = rolled(here, 1)
        here_down = rolled(here, 7)
        for t in range(lo, hi):
            after = load(t + 1) if t + 1 < count else here
            after_up, after_down = rolled(after, 1), rolled(after, 7)
            c, h = here
            cl, cr = pltpu.roll(c, 1, 1), pltpu.roll(c, LANES - 1, 1)
            hl, hr = pltpu.roll(h, 1, 1), pltpu.roll(h, LANES - 1, 1)
            side_c = jnp.where(first_lane, hl, cl) + jnp.where(last_lane, hr, cr)
            side_h = jnp.where(first_lane, cl, hl) + jnp.where(last_lane, cr, hr)
            vert = [
                jnp.where(first_sub, prev_up[k], here_up[k])
                + jnp.where(last_sub, after_down[k], here_down[k])
                for k in range(2)
            ]
            yield t, c, h, side_c + vert[0], side_h + vert[1]
            here, prev_up, here_up, here_down = after, here_up, after_up, after_down

    def forward(k, new, old, lo, hi):
        for segment in range(2):
            for v in range(4):
                p_new = segment * 8 + new * 4 + v
                p_old = segment * 8 + old * 4 + v
                for t, c, h, nc, nh in neighbours(fc, fh, p_new, lo, hi, FEXT // 8):
                    row = pl.ds(t * 8, 8)
                    on = pl.ds(t * 8 + HALO - FHALO, 8)
                    out_c = onc[on, :] * c - s * nc - fc[p_old, row, :]
                    out_h = onh[on, :] * h - s * nh - fh[p_old, row, :]
                    fc[p_old, row, :] = out_c
                    fh[p_old, row, :] = out_h
                    if 2 <= t < 6:
                        vs[segment * SEG + k, v, pl.ds((t - 2) * 8, 8), :] = out_c

    for start, stop, lo, hi in ((1, 4, 0, 8), (4, 8, 1, 7)):
        def body(i, carry, lo=lo, hi=hi):
            forward(2 * i, 1, 0, lo, hi)
            forward(2 * i + 1, 0, 1, lo, hi)
            return carry
        lax.fori_loop(start, stop, body, 0)

    def adjoint(t_term, new, old, lo, hi, grads):
        grads = list(grads)
        weights = {}
        for t in range(lo, hi):
            wc = wh = None
            row = pl.ds(t * 8, 8)
            for e in range(16):
                q = coef[t_term, e]
                pc, phh = rsc[e, row, :] * q, rsh[e, row, :] * q
                wc, wh = (pc, phh) if wc is None else (wc + pc, wh + phh)
            wcr[row, :] = wc
            whr[row, :] = wh
        for v in range(4):
            p_new, p_old = new * 4 + v, old * 4 + v
            for t, c, h, nc, nh in neighbours(xc, xh, p_new, lo, hi, EXT // 8):
                row = pl.ds(t * 8, 8)
                if 4 <= t < 8:
                    grads[t - 4] = grads[t - 4] + c * vs[t_term, v, pl.ds((t - 4) * 8, 8), :]
                xc[p_old, row, :] = wcr[row, :] * sgc[v, row, :] + (onc[row, :] * c - s * nc) - xc[p_old, row, :]
                xh[p_old, row, :] = whr[row, :] * sgh[v, row, :] + (onh[row, :] * h - s * nh) - xh[p_old, row, :]
        return tuple(grads)

    def run(wc_ref, wh_ref):
        nonlocal wcr, whr
        wcr, whr = wc_ref, wh_ref
        grads = tuple(jnp.zeros((8, LANES), jnp.float32) for _ in range(4))
        for phase in range(4):
            def body(i, carry, phase=phase):
                t_term = TERMS - 1 - 8 * phase - 2 * i
                carry = adjoint(t_term, 0, 1, phase, EXT // 8 - phase, carry)
                return adjoint(t_term - 1, 1, 0, phase, EXT // 8 - phase, carry)
            grads = lax.fori_loop(0, 4, body, grads)
        for i in range(4):
            grad_out[pl.ds(i * 8, 8), :] = grads[i] * s

    wcr = whr = None
    pl.run_scoped(run, pltpu.VMEM((EXT, LANES), jnp.float32), pltpu.VMEM((EXT, LANES), jnp.float32))
    for which in range(2):
        for v in range(4):
            for i in range(4):
                adj_out[which, v, pl.ds(i * 8, 8), :] = xc[which * 4 + v, pl.ds(HALO + i * 8, 8), :]


VMEM_SPEC = pl.BlockSpec(memory_space=pltpu.VMEM)
SMEM_SPEC = pl.BlockSpec(memory_space=pltpu.SMEM)
HBM_SPEC = pl.BlockSpec(memory_space=pltpu.HBM)


def per_device(
    checkpoints,
    adjoints_in,
    vector_bits,
    potential_int,
    pot_scale,
    energies,
    residual,
    first_segment,
):
    pot_factor = pot_scale[0]
    inv_span = 1.0 / (4.5 + QMAX * pot_factor)
    coefs = window_coefs(first_segment, energies)
    chk = checkpoints.reshape(FPLANES * ROWS, LANES)
    send = jax.ShapeDtypeStruct((MAIN + FPLANES * FHALO, LANES), F32)
    own, to_above = pl.pallas_call(
        prepare_kernel,
        out_shape=(send, send),
        in_specs=[SMEM_SPEC] + [HBM_SPEC] * 5,
        out_specs=(VMEM_SPEC, VMEM_SPEC),
        scratch_shapes=[
            pltpu.VMEM((4 * ROWS, LANES), jnp.int32),
            pltpu.VMEM((ROWS, LANES), jnp.int32),
            pltpu.SemaphoreType.DMA((2 + 2 * (2 + FPLANES),)),
        ],
        compiler_params=pltpu.CompilerParams(vmem_limit_bytes=4 * 1024 * 1024),
        name="prepare",
    )(
        (pot_factor * 2.0 * inv_span)[None],
        *(
            pltpu.with_memory_space_constraint(value, pltpu.HBM)
            for value in (
                adjoints_in.reshape(8 * ROWS, LANES),
                vector_bits.reshape(4 * ROWS, LANES),
                potential_int,
                residual.reshape(16 * ROWS, LANES),
                chk,
            )
        ),
    )

    def shift(value, axis, step):
        n = lax.axis_size(axis)
        return lax.ppermute(value, axis, [(i, (i + step) % n) for i in range(n)])

    above = shift(own, "row", 1)
    below = shift(to_above, "row", -1)

    strips = jax.ShapeDtypeStruct((G_ROWS, LANES), F32)
    to_left, to_right = pl.pallas_call(
        pack_kernel,
        out_shape=(strips, strips),
        in_specs=[VMEM_SPEC] * 4,
        out_specs=(VMEM_SPEC, VMEM_SPEC),
        compiler_params=pltpu.CompilerParams(vmem_limit_bytes=6 * 1024 * 1024),
        name="pack_columns",
    )(own, chk, above, below)
    from_left = shift(to_right, "col", 1)
    from_right = shift(to_left, "col", -1)

    ext = (EXT, LANES)
    adjoint_out, grad = pl.pallas_call(
        main_kernel,
        out_shape=(
            jax.ShapeDtypeStruct((2, 4, ROWS, LANES), F32),
            jax.ShapeDtypeStruct((ROWS, LANES), F32),
        ),
        in_specs=[SMEM_SPEC, SMEM_SPEC] + [VMEM_SPEC] * 6,
        out_specs=(VMEM_SPEC, VMEM_SPEC),
        scratch_shapes=[
            pltpu.VMEM((8, *ext), F32), pltpu.VMEM((8, *ext), F32),
            pltpu.VMEM((4, *ext), F32), pltpu.VMEM((4, *ext), F32),
            pltpu.VMEM((16, *ext), F32), pltpu.VMEM((16, *ext), F32),
            pltpu.VMEM(ext, F32), pltpu.VMEM(ext, F32),
            pltpu.VMEM((FPLANES, FEXT, LANES), F32), pltpu.VMEM((FPLANES, FEXT, LANES), F32),
            pltpu.VMEM((TERMS, 4, ROWS, LANES), F32),
        ],
        compiler_params=pltpu.CompilerParams(vmem_limit_bytes=14 * 1024 * 1024),
        name="window",
    )(coefs, (2.0 * inv_span)[None], own, chk, above, below, from_right, from_left)

    grad = jnp.sum(lax.all_gather(grad, "vec"), axis=0)
    return grad, adjoint_out


def solution(mesh):
    return jax.shard_map(
        per_device,
        mesh=mesh,
        in_specs=(
            P(None, None, "vec", "row", "col"),
            P(None, "vec", "row", "col"),
            P("vec", "row", "col"),
            P("row", "col"),
            P(),
            P(),
            P(None, "row", "col"),
            P(),
        ),
        out_specs=(P("row", "col"), P(None, "vec", "row", "col")),
        check_vma=False,
    )
```

```python
import functools
import math

import jax
import jax.numpy as jnp
from jax import lax
from jax.experimental import pallas as pl
from jax.experimental.pallas import tpu as pltpu
from jax.sharding import PartitionSpec as P

SEG = 16
MOMENTS = 1024
QMAX = 32767
TERMS = 2 * SEG
NVEC = 16
F32 = jnp.float32

ADJ, SGN, RES, ONS = 0, 8, 12, 20
PLANES = 21
HALF = 8
ROWS = 32
HALO = 32
EXT = ROWS + 2 * HALO
FHALO = 16
FEXT = ROWS + 2 * FHALO
LANES = 128
FPLANES = 16
MAIN = PLANES * ROWS
GROUPS = 5
G_RES = 3 * EXT
G_ADJ = GROUPS * EXT
G_ONS = EXT // 4
G_ROWS = G_ADJ + G_ONS + 2 * FEXT


def window_coefs(first_segment, energies):
    moment_order = first_segment[0] * SEG + jnp.arange(TERMS, dtype=jnp.int32)
    degree = moment_order.astype(jnp.float32)
    kernel_norm = float(MOMENTS + 1)
    angle_step = math.pi / kernel_norm
    jackson = (
        (kernel_norm - degree) * jnp.cos(angle_step * degree)
        + jnp.sin(angle_step * degree) * (math.cos(angle_step) / math.sin(angle_step))
    ) / kernel_norm
    factor = jnp.where(moment_order == 0, 1.0, 2.0).astype(jnp.float32)
    angles = jnp.arccos(energies)
    cosines = jnp.cos(degree[:, None] * angles[None, :])
    return (jackson * factor)[:, None] * cosines / (math.pi * jnp.sin(angles))[None, :]


def lane_iota():
    return lax.broadcasted_iota(jnp.int32, (8, LANES), 1)


def tile(ref, row):
    return ref[pl.ds(row, 8), :]


def main_tile(own, above, below, plane, t):
    section = (above, own, below)[t // 4]
    return tile(section, plane * ROWS + (t % 4) * 8)


def fwd_tile(chk, above, below, plane, t):
    if t < 2:
        return tile(above, MAIN + plane * FHALO + t * 8)
    if t < 6:
        return tile(chk, plane * ROWS + (t - 2) * 8)
    return tile(below, MAIN + plane * FHALO + (t - 6) * 8)


def prepare_kernel(
    factor, core, adj, bits, pot, res, chk, to_below, to_above, chk_v, bits_v, pot_v, sems
):
    copies = []

    def start(src, dst):
        copy = pltpu.make_async_copy(src, dst, sems.at[len(copies)])
        copy.start()
        copies.append(copy)

    first_res = pl.multiple_of(core[0] * (HALF * ROWS), HALF * ROWS)
    start(bits, bits_v)
    start(pot, pot_v)
    for out, first in ((to_below, ROWS - FHALO), (to_above, 0)):
        start(adj, out.at[pl.ds(ADJ * ROWS, 8 * ROWS)])
        start(res.at[pl.ds(first_res, HALF * ROWS)], out.at[pl.ds(RES * ROWS, HALF * ROWS)])
        for plane in range(FPLANES):
            start(
                chk.at[pl.ds(plane * ROWS + first, FHALO)],
                out.at[pl.ds(MAIN + plane * FHALO, FHALO)],
            )
    start(chk, chk_v)
    copies[0].wait()
    signs = (2 * bits_v[...] - 1).astype(F32) * (1.0 / NVEC)
    copies[1].wait()
    onsite = pot_v[...].astype(F32) * factor[0]
    for out in (to_below, to_above):
        out[pl.ds(SGN * ROWS, 4 * ROWS), :] = signs
        out[pl.ds(ONS * ROWS, ROWS), :] = onsite
    for copy in copies[2:]:
        copy.wait()


def pack_kernel(own, chk, above, below, to_left, to_right, to_core):
    lane = lane_iota()

    def pack(tiles, row):
        count = len(tiles)
        width = LANES // count
        group = lane // width
        left = right = None
        for j, value in enumerate(tiles):
            rolled = pltpu.roll(value, width * j, 1) if j else value
            left = rolled if j == 0 else jnp.where(group == j, rolled, left)
            right = rolled if j == 0 else jnp.where(group == (j + count - 1) % count, rolled, right)
        to_left[pl.ds(row, 8), :] = left
        to_right[pl.ds(row, 8), :] = right

    for g in range(GROUPS):
        for t in range(EXT // 8):
            pack([main_tile(own, above, below, 4 * g + j, t) for j in range(4)], g * EXT + t * 8)
    for m in range(3):
        pack([main_tile(own, above, below, ONS, 3 * j + m) for j in range(4)], G_ADJ + m * 8)
    for g in range(2):
        for t in range(FEXT // 8):
            pack(
                [fwd_tile(chk, above, below, 8 * g + j, t) for j in range(8)],
                G_ADJ + G_ONS + g * FEXT + t * 8,
            )
    size = HALF * ROWS
    to_core[pl.ds(0, size), :] = above[pl.ds(RES * ROWS, size), :]
    to_core[pl.ds(size, size), :] = below[pl.ds(RES * ROWS, size), :]


def unpack_strip(from_right, from_left, lane, right_row, left_row, j, count):
    width = LANES // count
    mixed = jnp.where(lane // width == j, tile(from_right, right_row), tile(from_left, left_row))
    return pltpu.roll(mixed, (LANES - width * j) % LANES, 1) if j else mixed


def weigh(coef, t_term, planes):
    total = None
    for e, value in enumerate(planes):
        term = value * coef[t_term, e]
        total = term if total is None else total + term
    return total


def phase_tiles(phase):
    return phase, EXT // 8 - phase


def weights_kernel(coef, core, own, res, above, below, swapped, out):
    other = (1 - core[0]) * (HALF * ROWS)
    for t in range(EXT // 8):
        def body(t_term, carry, t=t):
            planes = [main_tile(own, above, below, RES + e, t) for e in range(HALF)]
            for e in range(HALF):
                if t < 4:
                    planes.append(tile(swapped, e * ROWS + t * 8))
                elif t < 8:
                    row = pl.multiple_of(other + e * ROWS + (t - 4) * 8, 8)
                    planes.append(tile(res, row))
                else:
                    planes.append(tile(swapped, (HALF + e) * ROWS + (t - 8) * 8))
            out[t_term, pl.ds(t * 8, 8), :] = weigh(coef, t_term, planes)
            return carry
        phase = min(t, EXT // 8 - 1 - t, 3)
        lax.fori_loop(TERMS - 8 * (phase + 1), TERMS, body, 0, unroll=4)


class Stencil:
    def __init__(self):
        lane, sub = lane_iota(), lax.broadcasted_iota(jnp.int32, (8, LANES), 0)
        self.lane = lane
        self.first_lane, self.last_lane = lane == 0, lane == LANES - 1
        self.first_sub, self.last_sub = sub == 0, sub == 7

    def tiles(self, cref, href, plane, lo, hi, count):
        def load(t):
            return cref[plane, pl.ds(t * 8, 8), :], href[plane, pl.ds(t * 8, 8), :]

        def rolled(pair, shift):
            return tuple(pltpu.roll(p, shift, 0) for p in pair)

        here = load(lo)
        here_up, here_down = rolled(here, 1), rolled(here, 7)
        prev_up = rolled(load(lo - 1), 1) if lo > 0 else here_up
        for t in range(lo, hi):
            after = load(t + 1) if t + 1 < count else here
            after_up, after_down = rolled(after, 1), rolled(after, 7)
            c, h = here
            cl, cr = pltpu.roll(c, 1, 1), pltpu.roll(c, LANES - 1, 1)
            hl, hr = pltpu.roll(h, 1, 1), pltpu.roll(h, LANES - 1, 1)
            side_c = jnp.where(self.first_lane, hl, cl) + jnp.where(self.last_lane, hr, cr)
            side_h = jnp.where(self.first_lane, cl, hl) + jnp.where(self.last_lane, cr, hr)
            vert = [
                jnp.where(self.first_sub, prev_up[k], here_up[k])
                + jnp.where(self.last_sub, after_down[k], here_down[k])
                for k in range(2)
            ]
            yield t, c, h, side_c + vert[0], side_h + vert[1]
            here, prev_up, here_up, here_down = after, here_up, after_up, after_down


def forward_kernel(scale, own, chk, above, below, from_right, from_left, vs, fc, fh, onc, onh):
    stencil = Stencil()
    lane = stencil.lane
    s = scale[0]
    for t in range(FEXT // 8):
        row = pl.ds(t * 8, 8)
        for plane in range(FPLANES):
            at = G_ADJ + G_ONS + (plane // 8) * FEXT + t * 8
            fc[plane, row, :] = fwd_tile(chk, above, below, plane, t)
            fh[plane, row, :] = unpack_strip(from_right, from_left, lane, at, at, plane % 8, 8)
        e = t + (HALO - FHALO) // 8
        at = G_ADJ + (e % 3) * 8
        onc[row, :] = main_tile(own, above, below, ONS, e)
        onh[row, :] = unpack_strip(from_right, from_left, lane, at, at, e // 3, 4)
    for segment in range(2):
        for which in range(2):
            for v in range(4):
                for i in range(4):
                    vs[segment * SEG + which, v, pl.ds(i * 8, 8), :] = tile(
                        chk, (segment * 8 + which * 4 + v) * ROWS + i * 8
                    )

    def forward(k, new, old, lo, hi):
        for segment in range(2):
            for v in range(4):
                p_new = segment * 8 + new * 4 + v
                p_old = segment * 8 + old * 4 + v
                for t, c, h, nc, nh in stencil.tiles(fc, fh, p_new, lo, hi, FEXT // 8):
                    row = pl.ds(t * 8, 8)
                    out_c = onc[row, :] * c - s * nc - fc[p_old, row, :]
                    out_h = onh[row, :] * h - s * nh - fh[p_old, row, :]
                    fc[p_old, row, :] = out_c
                    fh[p_old, row, :] = out_h
                    if 2 <= t < 6:
                        vs[segment * SEG + k, v, pl.ds((t - 2) * 8, 8), :] = out_c

    for start, stop, lo, hi in ((1, 4, 0, 8), (4, 8, 1, 7)):
        def body(i, carry, lo=lo, hi=hi):
            forward(2 * i, 1, 0, lo, hi)
            forward(2 * i + 1, 0, 1, lo, hi)
            return carry
        lax.fori_loop(start, stop, body, 0)


def adjoint_kernel(
    coef, scale, own, above, below, from_right, from_left, swapped, vs, wcs,
    adj_out, grad_out,
    xc, xh, sgc, sgh, rsh, onc, onh, whr,
):
    stencil = Stencil()
    lane = stencil.lane
    s = scale[0]

    def strip(row, j, count):
        return unpack_strip(from_right, from_left, lane, row, row, j, count)

    for t in range(EXT // 8):
        row = pl.ds(t * 8, 8)
        for plane in range(8):
            xc[plane, row, :] = main_tile(own, above, below, plane, t)
            xh[plane, row, :] = strip((plane // 4) * EXT + t * 8, plane % 4, 4)
        for v in range(4):
            sgc[v, row, :] = main_tile(own, above, below, SGN + v, t)
            sgh[v, row, :] = strip(2 * EXT + t * 8, v, 4)
        for e in range(HALF):
            at = (e // 4) * EXT + t * 8
            rsh[e, row, :] = strip(G_RES + at, e % 4, 4)
            rsh[HALF + e, row, :] = unpack_strip(
                swapped, swapped, lane, at, 2 * EXT + at, e % 4, 4
            )
        onc[row, :] = main_tile(own, above, below, ONS, t)
        onh[row, :] = strip(G_ADJ + (t % 3) * 8, t // 3, 4)

    def adjoint(t_term, new, old, lo, hi, grads):
        grads = list(grads)
        for t in range(lo, hi):
            row = pl.ds(t * 8, 8)
            whr[row, :] = weigh(coef, t_term, [rsh[e, row, :] for e in range(2 * HALF)])
        for v in range(4):
            p_new, p_old = new * 4 + v, old * 4 + v
            for t, c, h, nc, nh in stencil.tiles(xc, xh, p_new, lo, hi, EXT // 8):
                row = pl.ds(t * 8, 8)
                if 4 <= t < 8:
                    grads[t - 4] = grads[t - 4] + c * vs[t_term, v, pl.ds((t - 4) * 8, 8), :]
                xc[p_old, row, :] = (
                    wcs[t_term, row, :] * sgc[v, row, :]
                    + (onc[row, :] * c - s * nc)
                    - xc[p_old, row, :]
                )
                xh[p_old, row, :] = (
                    whr[row, :] * sgh[v, row, :]
                    + (onh[row, :] * h - s * nh)
                    - xh[p_old, row, :]
                )
        return tuple(grads)

    grads = tuple(jnp.zeros((8, LANES), F32) for _ in range(4))
    for phase in range(4):
        lo, hi = phase_tiles(phase)
        def body(i, carry, phase=phase, lo=lo, hi=hi):
            t_term = TERMS - 1 - 8 * phase - 2 * i
            carry = adjoint(t_term, 0, 1, lo, hi, carry)
            return adjoint(t_term - 1, 1, 0, lo, hi, carry)
        grads = lax.fori_loop(0, 4, body, grads)
    for i in range(4):
        grad_out[pl.ds(i * 8, 8), :] = grads[i] * s
    for which in range(2):
        for v in range(4):
            for i in range(4):
                adj_out[which, v, pl.ds(i * 8, 8), :] = xc[which * 4 + v, pl.ds(HALO + i * 8, 8), :]


VMEM_SPEC = pl.BlockSpec(memory_space=pltpu.VMEM)
SMEM_SPEC = pl.BlockSpec(memory_space=pltpu.SMEM)
HBM_SPEC = pl.BlockSpec(memory_space=pltpu.HBM)


def params(mib):
    return pltpu.CompilerParams(vmem_limit_bytes=mib * 1024 * 1024)


def per_device(
    checkpoints,
    adjoints_in,
    vector_bits,
    potential_int,
    pot_scale,
    energies,
    residual,
    first_segment,
):
    pot_factor = pot_scale[0]
    inv_span = 1.0 / (4.5 + QMAX * pot_factor)
    core = lax.axis_index("vec") % 2
    coefs = window_coefs(first_segment, energies)
    coefs = jnp.where(core == 0, coefs, jnp.roll(coefs, HALF, axis=1))
    core = core[None]
    chk = checkpoints.reshape(FPLANES * ROWS, LANES)
    res = residual.reshape(2 * HALF * ROWS, LANES)
    scale = (2.0 * inv_span)[None]
    send = jax.ShapeDtypeStruct((MAIN + FPLANES * FHALO, LANES), F32)
    own, to_above, chk = pl.pallas_call(
        prepare_kernel,
        out_shape=(send, send, jax.ShapeDtypeStruct((FPLANES * ROWS, LANES), F32)),
        in_specs=[SMEM_SPEC] * 2 + [HBM_SPEC] * 5,
        out_specs=(VMEM_SPEC,) * 3,
        scratch_shapes=[
            pltpu.VMEM((4 * ROWS, LANES), jnp.int32),
            pltpu.VMEM((ROWS, LANES), jnp.int32),
            pltpu.SemaphoreType.DMA((3 + 2 * (2 + FPLANES),)),
        ],
        compiler_params=params(4),
        name="prepare",
    )(
        pot_factor * scale,
        core,
        *(
            pltpu.with_memory_space_constraint(value, pltpu.HBM)
            for value in (
                adjoints_in.reshape(8 * ROWS, LANES),
                vector_bits.reshape(4 * ROWS, LANES),
                potential_int,
                res,
                chk,
            )
        ),
    )

    def shift(value, axis, step):
        n = lax.axis_size(axis)
        return lax.ppermute(value, axis, [(i, (i + step) % n) for i in range(n)])

    def swap_cores(value):
        return lax.ppermute(value, "vec", [(0, 1), (1, 0), (2, 3), (3, 2)])

    above = shift(own, "row", 1)
    below = shift(to_above, "row", -1)

    strips = jax.ShapeDtypeStruct((G_ROWS, LANES), F32)
    to_left, to_right, to_core = pl.pallas_call(
        pack_kernel,
        out_shape=(strips, strips, jax.ShapeDtypeStruct((2 * HALF * ROWS, LANES), F32)),
        in_specs=[VMEM_SPEC] * 4,
        out_specs=(VMEM_SPEC,) * 3,
        compiler_params=params(6),
        name="pack_columns",
    )(own, chk, above, below)
    from_left = shift(to_right, "col", 1)
    from_right = shift(to_left, "col", -1)
    swapped_rows = swap_cores(to_core)
    weights = pl.pallas_call(
        weights_kernel,
        out_shape=jax.ShapeDtypeStruct((TERMS, EXT, LANES), F32),
        in_specs=[SMEM_SPEC] * 2 + [VMEM_SPEC] * 5,
        out_specs=VMEM_SPEC,
        compiler_params=params(6),
        cost_estimate=pl.CostEstimate(flops=12_000_000, bytes_accessed=4_000_000, transcendentals=0),
        name="weights",
    )(coefs, core, own, res, above, below, swapped_rows)

    weights, from_right, from_left = lax.optimization_barrier((weights, from_right, from_left))
    strip_rows = slice(G_RES, G_RES + 2 * EXT)
    swapped_strips = swap_cores(
        jnp.concatenate([from_right[strip_rows], from_left[strip_rows]], axis=0)
    )
    frame = (FPLANES, FEXT, LANES)
    states = pl.pallas_call(
        forward_kernel,
        out_shape=jax.ShapeDtypeStruct((TERMS, 4, ROWS, LANES), F32),
        in_specs=[SMEM_SPEC] + [VMEM_SPEC] * 6,
        out_specs=VMEM_SPEC,
        scratch_shapes=[
            pltpu.VMEM(frame, F32), pltpu.VMEM(frame, F32),
            pltpu.VMEM(frame[1:], F32), pltpu.VMEM(frame[1:], F32),
        ],
        compiler_params=params(8),
        cost_estimate=pl.CostEstimate(flops=20_000_000, bytes_accessed=6_000_000, transcendentals=0),
        name="forward",
    )(scale, own, chk, above, below, from_right, from_left)

    ext = (EXT, LANES)
    adjoint_out, grad = pl.pallas_call(
        adjoint_kernel,
        out_shape=(
            jax.ShapeDtypeStruct((2, 4, ROWS, LANES), F32),
            jax.ShapeDtypeStruct((ROWS, LANES), F32),
        ),
        in_specs=[SMEM_SPEC, SMEM_SPEC] + [VMEM_SPEC] * 8,
        out_specs=(VMEM_SPEC, VMEM_SPEC),
        scratch_shapes=[
            pltpu.VMEM((8, *ext), F32), pltpu.VMEM((8, *ext), F32),
            pltpu.VMEM((4, *ext), F32), pltpu.VMEM((4, *ext), F32),
            pltpu.VMEM((2 * HALF, *ext), F32),
            pltpu.VMEM(ext, F32), pltpu.VMEM(ext, F32), pltpu.VMEM(ext, F32),
        ],
        compiler_params=params(10),
        name="adjoint",
    )(coefs, scale, own, above, below, from_right, from_left, swapped_strips, states, weights)

    grad = jnp.sum(lax.all_gather(grad, "vec"), axis=0)
    return grad, adjoint_out


def solution(mesh):
    return jax.shard_map(
        per_device,
        mesh=mesh,
        in_specs=(
            P(None, None, "vec", "row", "col"),
            P(None, "vec", "row", "col"),
            P("vec", "row", "col"),
            P("row", "col"),
            P(),
            P(),
            P(None, "row", "col"),
            P(),
        ),
        out_specs=(P("row", "col"), P(None, "vec", "row", "col")),
        check_vma=False,
    )
```

```python
import functools
import math

import jax
import jax.numpy as jnp
from jax import lax
from jax.experimental import pallas as pl
from jax.experimental.pallas import tpu as pltpu
from jax.sharding import PartitionSpec as P

SEG = 16
MOMENTS = 1024
QMAX = 32767
TERMS = 2 * SEG
NVEC = 16
F32 = jnp.float32

ADJ, SGN, RES, ONS = 0, 8, 12, 20
PLANES = 21
HALF = 8
ROWS = 32
HALO = 32
EXT = ROWS + 2 * HALO
FHALO = 16
FEXT = ROWS + 2 * FHALO
LANES = 128
FPLANES = 16
MAIN = PLANES * ROWS
WIDE = EXT // 8
GROUPS = 5
G_RES = 3 * EXT
G_ADJ = GROUPS * EXT
G_ONS = EXT // 4
G_ROWS = G_ADJ + G_ONS + 2 * FEXT


def window_coefs(first_segment, energies):
    moment_order = first_segment[0] * SEG + jnp.arange(TERMS, dtype=jnp.int32)
    degree = moment_order.astype(jnp.float32)
    kernel_norm = float(MOMENTS + 1)
    angle_step = math.pi / kernel_norm
    jackson = (
        (kernel_norm - degree) * jnp.cos(angle_step * degree)
        + jnp.sin(angle_step * degree) * (math.cos(angle_step) / math.sin(angle_step))
    ) / kernel_norm
    factor = jnp.where(moment_order == 0, 1.0, 2.0).astype(jnp.float32)
    angles = jnp.arccos(energies)
    cosines = jnp.cos(degree[:, None] * angles[None, :])
    return (jackson * factor)[:, None] * cosines / (math.pi * jnp.sin(angles))[None, :]


def lane_iota():
    return lax.broadcasted_iota(jnp.int32, (8, LANES), 1)


def tile(ref, row):
    return ref[pl.ds(row, 8), :]


def main_tile(own, above, below, plane, t):
    section = (above, own, below)[t // 4]
    return tile(section, plane * ROWS + (t % 4) * 8)


def fwd_tile(chk, above, below, plane, t):
    if t < 2:
        return tile(above, MAIN + plane * FHALO + t * 8)
    if t < 6:
        return tile(chk, plane * ROWS + (t - 2) * 8)
    return tile(below, MAIN + plane * FHALO + (t - 6) * 8)


def prepare_kernel(
    core, scalar, adj, bits, pot, res, chk,
    to_below, to_above, chk_v, res_v, scale_v, bits_v, pot_v, sems
):
    copies = []

    def start(src, dst):
        copy = pltpu.make_async_copy(src, dst, sems.at[len(copies)])
        copy.start()
        copies.append(copy)

    first_res = pl.multiple_of(core[0] * (HALF * ROWS), HALF * ROWS)
    start(bits, bits_v)
    start(pot, pot_v)
    for out, first in ((to_below, ROWS - FHALO), (to_above, 0)):
        start(adj, out.at[pl.ds(ADJ * ROWS, 8 * ROWS)])
        start(res.at[pl.ds(first_res, HALF * ROWS)], out.at[pl.ds(RES * ROWS, HALF * ROWS)])
        for plane in range(FPLANES):
            start(
                chk.at[pl.ds(plane * ROWS + first, FHALO)],
                out.at[pl.ds(MAIN + plane * FHALO, FHALO)],
            )
    start(chk, chk_v)
    start(res.at[pl.ds(pl.multiple_of(HALF * ROWS - first_res, HALF * ROWS), HALF * ROWS)], res_v)
    copies[0].wait()
    signs = (2 * bits_v[...] - 1).astype(F32) * (1.0 / NVEC)
    copies[1].wait()
    pot_factor = scalar[0]
    scale = 2.0 / (4.5 + QMAX * pot_factor)
    scale_v[0] = scale
    onsite = pot_v[...].astype(F32) * (pot_factor * scale)
    for out in (to_below, to_above):
        out[pl.ds(SGN * ROWS, 4 * ROWS), :] = signs
        out[pl.ds(ONS * ROWS, ROWS), :] = onsite
    for copy in copies[2:]:
        copy.wait()


def pack_kernel(own, chk, above, below, to_left, to_right):
    lane = lane_iota()

    def pack(tiles, row):
        count = len(tiles)
        width = LANES // count
        group = lane // width
        left = right = None
        for j, value in enumerate(tiles):
            rolled = pltpu.roll(value, width * j, 1) if j else value
            left = rolled if j == 0 else jnp.where(group == j, rolled, left)
            right = rolled if j == 0 else jnp.where(group == (j + count - 1) % count, rolled, right)
        to_left[pl.ds(row, 8), :] = left
        to_right[pl.ds(row, 8), :] = right

    for g in range(GROUPS):
        for t in range(EXT // 8):
            pack([main_tile(own, above, below, 4 * g + j, t) for j in range(4)], g * EXT + t * 8)
    for m in range(3):
        pack([main_tile(own, above, below, ONS, 3 * j + m) for j in range(4)], G_ADJ + m * 8)
    for g in range(2):
        for t in range(FEXT // 8):
            pack(
                [fwd_tile(chk, above, below, 8 * g + j, t) for j in range(8)],
                G_ADJ + G_ONS + g * FEXT + t * 8,
            )


def unpack_strip(from_right, from_left, lane, right_row, left_row, j, count):
    width = LANES // count
    mixed = jnp.where(lane // width == j, tile(from_right, right_row), tile(from_left, left_row))
    return pltpu.roll(mixed, (LANES - width * j) % LANES, 1) if j else mixed


def splats(coef, t_term):
    return [jnp.full((8, LANES), coef[t_term, e], F32) for e in range(2 * HALF)]


def weigh(factors, planes):
    terms = [value * factor for value, factor in zip(planes, factors)]
    while len(terms) > 1:
        terms = [x + y for x, y in zip(terms[::2], terms[1::2])]
    return terms[0]


def phase_tiles(phase):
    return phase, EXT // 8 - phase


def weights_kernel(coef, own, res_other, above, below, swapped, out):
    def residuals(t):
        planes = [main_tile(own, above, below, RES + e, t) for e in range(HALF)]
        for e in range(HALF):
            if t < 4:
                planes.append(tile(swapped, e * ROWS + t * 8))
            elif t < 8:
                planes.append(tile(res_other, e * ROWS + (t - 4) * 8))
            else:
                planes.append(tile(swapped, (HALF + e) * ROWS + (t - 8) * 8))
        return planes

    for phase in range(4):
        lo, hi = phase_tiles(phase)

        def body(i, carry, phase=phase, lo=lo, hi=hi):
            t_term = TERMS - 8 * (phase + 1) + i
            factors = splats(coef, t_term)
            for t in range(lo, hi):
                out[t_term, pl.ds(t * 8, 8), :] = weigh(factors, residuals(t))
            return carry

        lax.fori_loop(0, 8, body, 0)


class Stencil:
    def __init__(self):
        lane, sub = lane_iota(), lax.broadcasted_iota(jnp.int32, (8, LANES), 0)
        self.lane = lane
        self.first_lane, self.last_lane = lane == 0, lane == LANES - 1
        self.first_sub, self.last_sub = sub == 0, sub == 7

    def tiles(self, cref, href, plane, lo, hi, count):
        def load(t):
            return cref[plane, pl.ds(t * 8, 8), :], href[plane, pl.ds(t * 8, 8), :]

        def rolled(pair, shift):
            return tuple(pltpu.roll(p, shift, 0) for p in pair)

        here = load(lo)
        here_up, here_down = rolled(here, 1), rolled(here, 7)
        prev_up = rolled(load(lo - 1), 1) if lo > 0 else here_up
        for t in range(lo, hi):
            after = load(t + 1) if t + 1 < count else here
            after_up, after_down = rolled(after, 1), rolled(after, 7)
            c, h = here
            cl, cr = pltpu.roll(c, 1, 1), pltpu.roll(c, LANES - 1, 1)
            hl, hr = pltpu.roll(h, 1, 1), pltpu.roll(h, LANES - 1, 1)
            side_c = jnp.where(self.first_lane, hl, cl) + jnp.where(self.last_lane, hr, cr)
            side_h = jnp.where(self.first_lane, cl, hl) + jnp.where(self.last_lane, cr, hr)
            vert = [
                jnp.where(self.first_sub, prev_up[k], here_up[k])
                + jnp.where(self.last_sub, after_down[k], here_down[k])
                for k in range(2)
            ]
            yield t, c, h, side_c + vert[0], side_h + vert[1]
            here, prev_up, here_up, here_down = after, here_up, after_up, after_down


def forward_kernel(scale, own, chk, above, below, from_right, from_left, vs, fc, fh, onc, onh):
    stencil = Stencil()
    lane = stencil.lane
    s = jnp.full((8, LANES), scale[0], F32)
    for t in range(FEXT // 8):
        row = pl.ds(t * 8, 8)
        for plane in range(FPLANES):
            at = G_ADJ + G_ONS + (plane // 8) * FEXT + t * 8
            fc[plane, row, :] = fwd_tile(chk, above, below, plane, t)
            fh[plane, row, :] = unpack_strip(from_right, from_left, lane, at, at, plane % 8, 8)
        e = t + (HALO - FHALO) // 8
        at = G_ADJ + (e % 3) * 8
        onc[row, :] = main_tile(own, above, below, ONS, e)
        onh[row, :] = unpack_strip(from_right, from_left, lane, at, at, e // 3, 4)
    for segment in range(2):
        for which in range(2):
            for v in range(4):
                for i in range(4):
                    vs[segment * SEG + which, v, pl.ds(i * 8, 8), :] = tile(
                        chk, (segment * 8 + which * 4 + v) * ROWS + i * 8
                    )

    def forward(k, new, old, lo, hi):
        for segment in range(2):
            for v in range(4):
                p_new = segment * 8 + new * 4 + v
                p_old = segment * 8 + old * 4 + v
                for t, c, h, nc, nh in stencil.tiles(fc, fh, p_new, lo, hi, FEXT // 8):
                    row = pl.ds(t * 8, 8)
                    out_c = onc[row, :] * c - s * nc - fc[p_old, row, :]
                    out_h = onh[row, :] * h - s * nh - fh[p_old, row, :]
                    fc[p_old, row, :] = out_c
                    fh[p_old, row, :] = out_h
                    if 2 <= t < 6:
                        vs[segment * SEG + k, v, pl.ds((t - 2) * 8, 8), :] = out_c

    for start, stop, lo, hi in ((1, 4, 0, 8), (4, 8, 1, 7)):
        def body(i, carry, lo=lo, hi=hi):
            forward(2 * i, 1, 0, lo, hi)
            forward(2 * i + 1, 0, 1, lo, hi)
            return carry
        lax.fori_loop(start, stop, body, 0)


def adjoint_kernel(
    coef, scale, own, above, below, from_right, from_left, swapped, vs, wcs,
    adj_out, grad_out,
    xc, xh, sgc, sgh, rsh, onc, onh, whr,
):
    stencil = Stencil()
    lane = stencil.lane
    s = jnp.full((8, LANES), scale[0], F32)

    def strip(row, j, count):
        return unpack_strip(from_right, from_left, lane, row, row, j, count)

    for t in range(EXT // 8):
        row = pl.ds(t * 8, 8)
        for plane in range(8):
            xc[plane, row, :] = main_tile(own, above, below, plane, t)
            xh[plane, row, :] = strip((plane // 4) * EXT + t * 8, plane % 4, 4)
        for v in range(4):
            sgc[v, row, :] = main_tile(own, above, below, SGN + v, t)
            sgh[v, row, :] = strip(2 * EXT + t * 8, v, 4)
        for e in range(HALF):
            at = (e // 4) * EXT + t * 8
            rsh[e, row, :] = strip(G_RES + at, e % 4, 4)
            rsh[HALF + e, row, :] = unpack_strip(
                swapped, swapped, lane, at, 2 * EXT + at, e % 4, 4
            )
        onc[row, :] = main_tile(own, above, below, ONS, t)
        onh[row, :] = strip(G_ADJ + (t % 3) * 8, t // 3, 4)

    def adjoint(t_term, new, old, lo, hi, grads):
        grads = list(grads)
        factors = splats(coef, t_term)
        for t in range(lo, hi):
            row = pl.ds(t * 8, 8)
            whr[row, :] = weigh(factors, [rsh[e, row, :] for e in range(2 * HALF)])
        for v in range(4):
            p_new, p_old = new * 4 + v, old * 4 + v
            for t, c, h, nc, nh in stencil.tiles(xc, xh, p_new, lo, hi, EXT // 8):
                row = pl.ds(t * 8, 8)
                if 4 <= t < 8:
                    grads[t - 4] = grads[t - 4] + c * vs[t_term, v, pl.ds((t - 4) * 8, 8), :]
                xc[p_old, row, :] = (
                    wcs[t_term, row, :] * sgc[v, row, :]
                    + (onc[row, :] * c - s * nc)
                    - xc[p_old, row, :]
                )
                xh[p_old, row, :] = (
                    whr[row, :] * sgh[v, row, :]
                    + (onh[row, :] * h - s * nh)
                    - xh[p_old, row, :]
                )
        return tuple(grads)

    grads = tuple(jnp.zeros((8, LANES), F32) for _ in range(4))
    for phase in range(4):
        lo, hi = phase_tiles(phase)
        def body(i, carry, phase=phase, lo=lo, hi=hi):
            t_term = TERMS - 1 - 8 * phase - 2 * i
            carry = adjoint(t_term, 0, 1, lo, hi, carry)
            return adjoint(t_term - 1, 1, 0, lo, hi, carry)
        grads = lax.fori_loop(0, 4, body, grads)
    for i in range(4):
        grad_out[pl.ds(i * 8, 8), :] = grads[i] * s
    for which in range(2):
        for v in range(4):
            for i in range(4):
                adj_out[which, v, pl.ds(i * 8, 8), :] = xc[which * 4 + v, pl.ds(HALO + i * 8, 8), :]


VMEM_SPEC = pl.BlockSpec(memory_space=pltpu.VMEM)
SMEM_SPEC = pl.BlockSpec(memory_space=pltpu.SMEM)
HBM_SPEC = pl.BlockSpec(memory_space=pltpu.HBM)


def params(mib):
    return pltpu.CompilerParams(vmem_limit_bytes=mib * 1024 * 1024)


def per_device(
    checkpoints,
    adjoints_in,
    vector_bits,
    potential_int,
    pot_scale,
    energies,
    residual,
    first_segment,
):
    core = lax.axis_index("vec") % 2
    coefs = window_coefs(first_segment, energies)
    coefs = jnp.where(core == 0, coefs, jnp.roll(coefs, HALF, axis=1))
    core = core[None]
    chk = checkpoints.reshape(FPLANES * ROWS, LANES)
    res = residual.reshape(2 * HALF * ROWS, LANES)
    send = jax.ShapeDtypeStruct((MAIN + FPLANES * FHALO, LANES), F32)
    own, to_above, chk, res_other, scale = pl.pallas_call(
        prepare_kernel,
        out_shape=(
            send,
            send,
            jax.ShapeDtypeStruct((FPLANES * ROWS, LANES), F32),
            jax.ShapeDtypeStruct((HALF * ROWS, LANES), F32),
            jax.ShapeDtypeStruct((1,), F32),
        ),
        in_specs=[SMEM_SPEC] * 2 + [HBM_SPEC] * 5,
        out_specs=(VMEM_SPEC,) * 4 + (SMEM_SPEC,),
        scratch_shapes=[
            pltpu.VMEM((4 * ROWS, LANES), jnp.int32),
            pltpu.VMEM((ROWS, LANES), jnp.int32),
            pltpu.SemaphoreType.DMA((4 + 2 * (2 + FPLANES),)),
        ],
        compiler_params=params(4),
        name="prepare",
    )(
        core,
        pot_scale,
        *(
            pltpu.with_memory_space_constraint(value, pltpu.HBM)
            for value in (
                adjoints_in.reshape(8 * ROWS, LANES),
                vector_bits.reshape(4 * ROWS, LANES),
                potential_int,
                res,
                chk,
            )
        ),
    )

    def shift(value, axis, step):
        n = lax.axis_size(axis)
        return lax.ppermute(value, axis, [(i, (i + step) % n) for i in range(n)])

    def swap_cores(value):
        return lax.ppermute(value, "vec", [(0, 1), (1, 0), (2, 3), (3, 2)])

    above = shift(own, "row", 1)
    below = shift(to_above, "row", -1)

    strips = jax.ShapeDtypeStruct((G_ROWS, LANES), F32)
    to_left, to_right = pl.pallas_call(
        pack_kernel,
        out_shape=(strips, strips),
        in_specs=[VMEM_SPEC] * 4,
        out_specs=(VMEM_SPEC,) * 2,
        compiler_params=params(6),
        name="pack_columns",
    )(own, chk, above, below)
    to_left, res_above, res_below = lax.optimization_barrier((to_left, above, below))
    from_left = shift(to_right, "col", 1)
    from_right = shift(to_left, "col", -1)
    res_rows = slice(RES * ROWS, (RES + HALF) * ROWS)
    swapped_rows = swap_cores(jnp.concatenate([res_above[res_rows], res_below[res_rows]], axis=0))
    weights = pl.pallas_call(
        weights_kernel,
        out_shape=jax.ShapeDtypeStruct((TERMS, EXT, LANES), F32),
        in_specs=[SMEM_SPEC] + [VMEM_SPEC] * 5,
        out_specs=VMEM_SPEC,
        compiler_params=params(6),
        cost_estimate=pl.CostEstimate(flops=12_000_000, bytes_accessed=4_000_000, transcendentals=0),
        name="weights",
    )(coefs, own, res_other, above, below, swapped_rows)

    weights, from_right, from_left = lax.optimization_barrier((weights, from_right, from_left))
    strip_rows = slice(G_RES, G_RES + 2 * EXT)
    swapped_strips = swap_cores(
        jnp.concatenate([from_right[strip_rows], from_left[strip_rows]], axis=0)
    )
    frame = (FPLANES, FEXT, LANES)
    states = pl.pallas_call(
        forward_kernel,
        out_shape=jax.ShapeDtypeStruct((TERMS, 4, ROWS, LANES), F32),
        in_specs=[SMEM_SPEC] + [VMEM_SPEC] * 6,
        out_specs=VMEM_SPEC,
        scratch_shapes=[
            pltpu.VMEM(frame, F32), pltpu.VMEM(frame, F32),
            pltpu.VMEM(frame[1:], F32), pltpu.VMEM(frame[1:], F32),
        ],
        compiler_params=params(8),
        cost_estimate=pl.CostEstimate(flops=20_000_000, bytes_accessed=6_000_000, transcendentals=0),
        name="forward",
    )(scale, own, chk, above, below, from_right, from_left)

    ext = (EXT, LANES)
    adjoint_out, grad = pl.pallas_call(
        adjoint_kernel,
        out_shape=(
            jax.ShapeDtypeStruct((2, 4, ROWS, LANES), F32),
            jax.ShapeDtypeStruct((ROWS, LANES), F32),
        ),
        in_specs=[SMEM_SPEC, SMEM_SPEC] + [VMEM_SPEC] * 8,
        out_specs=(VMEM_SPEC, VMEM_SPEC),
        scratch_shapes=[
            pltpu.VMEM((8, *ext), F32), pltpu.VMEM((8, *ext), F32),
            pltpu.VMEM((4, *ext), F32), pltpu.VMEM((4, *ext), F32),
            pltpu.VMEM((2 * HALF, *ext), F32),
            pltpu.VMEM(ext, F32), pltpu.VMEM(ext, F32), pltpu.VMEM(ext, F32),
        ],
        compiler_params=params(10),
        name="adjoint",
    )(coefs, scale, own, above, below, from_right, from_left, swapped_strips, states, weights)

    grad = jnp.sum(lax.all_gather(grad, "vec"), axis=0)
    return grad, adjoint_out


def solution(mesh):
    return jax.shard_map(
        per_device,
        mesh=mesh,
        in_specs=(
            P(None, None, "vec", "row", "col"),
            P(None, "vec", "row", "col"),
            P("vec", "row", "col"),
            P("row", "col"),
            P(),
            P(),
            P(None, "row", "col"),
            P(),
        ),
        out_specs=(P("row", "col"), P(None, "vec", "row", "col")),
        check_vma=False,
    )
```

```python
import functools
import math

import jax
import jax.numpy as jnp
from jax import lax
from jax.experimental import pallas as pl
from jax.experimental.pallas import tpu as pltpu
from jax.sharding import PartitionSpec as P

SEG = 16
MOMENTS = 1024
QMAX = 32767
TERMS = 2 * SEG
NVEC = 16
F32 = jnp.float32

ADJ, SGN, RES, ONS = 0, 8, 12, 20
PLANES = 21
HALF = 8
ROWS = 32
HALO = 32
EXT = ROWS + 2 * HALO
FHALO = 16
FEXT = ROWS + 2 * FHALO
LANES = 128
FPLANES = 16
MAIN = PLANES * ROWS
WIDE = EXT // 8
GROUPS = 5
G_RES = 3 * EXT
G_ADJ = GROUPS * EXT
G_ONS = EXT // 4
G_ROWS = G_ADJ + G_ONS + 2 * FEXT


def window_coefs(first_segment, energies):
    moment_order = first_segment[0] * SEG + jnp.arange(TERMS, dtype=jnp.int32)
    degree = moment_order.astype(jnp.float32)
    kernel_norm = float(MOMENTS + 1)
    angle_step = math.pi / kernel_norm
    jackson = (
        (kernel_norm - degree) * jnp.cos(angle_step * degree)
        + jnp.sin(angle_step * degree) * (math.cos(angle_step) / math.sin(angle_step))
    ) / kernel_norm
    factor = jnp.where(moment_order == 0, 1.0, 2.0).astype(jnp.float32)
    angles = jnp.arccos(energies)
    cosines = jnp.cos(degree[:, None] * angles[None, :])
    return (jackson * factor)[:, None] * cosines / (math.pi * jnp.sin(angles))[None, :]


def lane_iota():
    return lax.broadcasted_iota(jnp.int32, (8, LANES), 1)


def tile(ref, row):
    return ref[pl.ds(row, 8), :]


def main_tile(own, above, below, plane, t):
    section = (above, own, below)[t // 4]
    return tile(section, plane * ROWS + (t % 4) * 8)


def fwd_tile(chk, above, below, plane, t):
    if t < 2:
        return tile(above, MAIN + plane * FHALO + t * 8)
    if t < 6:
        return tile(chk, plane * ROWS + (t - 2) * 8)
    return tile(below, MAIN + plane * FHALO + (t - 6) * 8)


def prepare_kernel(
    core, scalar, adj, bits, pot, res, chk,
    to_below, to_above, chk_v, res_v, bits_v, pot_v, sems
):
    copies = []

    def start(src, dst):
        copy = pltpu.make_async_copy(src, dst, sems.at[len(copies)])
        copy.start()
        copies.append(copy)

    first_res = pl.multiple_of(core[0] * (HALF * ROWS), HALF * ROWS)
    start(bits, bits_v)
    start(pot, pot_v)
    for out, first in ((to_below, ROWS - FHALO), (to_above, 0)):
        start(adj, out.at[pl.ds(ADJ * ROWS, 8 * ROWS)])
        start(res.at[pl.ds(first_res, HALF * ROWS)], out.at[pl.ds(RES * ROWS, HALF * ROWS)])
        for plane in range(FPLANES):
            start(
                chk.at[pl.ds(plane * ROWS + first, FHALO)],
                out.at[pl.ds(MAIN + plane * FHALO, FHALO)],
            )
    start(chk, chk_v)
    start(res.at[pl.ds(pl.multiple_of(HALF * ROWS - first_res, HALF * ROWS), HALF * ROWS)], res_v)
    copies[0].wait()
    signs = (2 * bits_v[...] - 1).astype(F32) * (1.0 / NVEC)
    copies[1].wait()
    pot_factor = scalar[0]
    scale = 2.0 / (4.5 + QMAX * pot_factor)
    onsite = pot_v[...].astype(F32) * (pot_factor * scale)
    for out in (to_below, to_above):
        out[pl.ds(SGN * ROWS, 4 * ROWS), :] = signs
        out[pl.ds(ONS * ROWS, ROWS), :] = onsite
    for copy in copies[2:]:
        copy.wait()


def pack_kernel(own, chk, above, below, to_left, to_right):
    lane = lane_iota()

    def pack(tiles, row):
        count = len(tiles)
        width = LANES // count
        group = lane // width
        left = right = None
        for j, value in enumerate(tiles):
            rolled = pltpu.roll(value, width * j, 1) if j else value
            left = rolled if j == 0 else jnp.where(group == j, rolled, left)
            right = rolled if j == 0 else jnp.where(group == (j + count - 1) % count, rolled, right)
        to_left[pl.ds(row, 8), :] = left
        to_right[pl.ds(row, 8), :] = right

    for g in range(GROUPS):
        for t in range(EXT // 8):
            pack([main_tile(own, above, below, 4 * g + j, t) for j in range(4)], g * EXT + t * 8)
    for m in range(3):
        pack([main_tile(own, above, below, ONS, 3 * j + m) for j in range(4)], G_ADJ + m * 8)
    for g in range(2):
        for t in range(FEXT // 8):
            pack(
                [fwd_tile(chk, above, below, 8 * g + j, t) for j in range(8)],
                G_ADJ + G_ONS + g * FEXT + t * 8,
            )


def unpack_strip(from_right, from_left, lane, right_row, left_row, j, count):
    width = LANES // count
    mixed = jnp.where(lane // width == j, tile(from_right, right_row), tile(from_left, left_row))
    return pltpu.roll(mixed, (LANES - width * j) % LANES, 1) if j else mixed


def splats(coef, t_term):
    return [jnp.full((8, LANES), coef[t_term, e], F32) for e in range(2 * HALF)]


def weigh(factors, planes):
    terms = [value * factor for value, factor in zip(planes, factors)]
    while len(terms) > 1:
        terms = [x + y for x, y in zip(terms[::2], terms[1::2])]
    return terms[0]


def phase_tiles(phase):
    return phase, EXT // 8 - phase


def weights_kernel(coef, own, res_other, above, below, out):
    def residuals(t):
        planes = [main_tile(own, above, below, RES + e, t) for e in range(HALF)]
        if 4 <= t < 8:
            planes += [tile(res_other, e * ROWS + (t - 4) * 8) for e in range(HALF)]
        return planes

    for phase in range(4):
        lo, hi = phase_tiles(phase)

        def body(i, carry, phase=phase, lo=lo, hi=hi):
            t_term = TERMS - 8 * (phase + 1) + i
            factors = splats(coef, t_term)
            for t in range(lo, hi):
                out[t_term, pl.ds(t * 8, 8), :] = weigh(factors, residuals(t))
            return carry

        lax.fori_loop(0, 8, body, 0)


class Stencil:
    def __init__(self):
        lane, sub = lane_iota(), lax.broadcasted_iota(jnp.int32, (8, LANES), 0)
        self.lane = lane
        self.first_lane, self.last_lane = lane == 0, lane == LANES - 1
        self.first_sub, self.last_sub = sub == 0, sub == 7

    def tiles(self, cref, href, plane, lo, hi, count):
        def load(t):
            return cref[plane, pl.ds(t * 8, 8), :], href[plane, pl.ds(t * 8, 8), :]

        def rolled(pair, shift):
            return tuple(pltpu.roll(p, shift, 0) for p in pair)

        here = load(lo)
        here_up, here_down = rolled(here, 1), rolled(here, 7)
        prev_up = rolled(load(lo - 1), 1) if lo > 0 else here_up
        for t in range(lo, hi):
            after = load(t + 1) if t + 1 < count else here
            after_up, after_down = rolled(after, 1), rolled(after, 7)
            c, h = here
            cl, cr = pltpu.roll(c, 1, 1), pltpu.roll(c, LANES - 1, 1)
            hl, hr = pltpu.roll(h, 1, 1), pltpu.roll(h, LANES - 1, 1)
            side_c = jnp.where(self.first_lane, hl, cl) + jnp.where(self.last_lane, hr, cr)
            side_h = jnp.where(self.first_lane, cl, hl) + jnp.where(self.last_lane, cr, hr)
            vert = [
                jnp.where(self.first_sub, prev_up[k], here_up[k])
                + jnp.where(self.last_sub, after_down[k], here_down[k])
                for k in range(2)
            ]
            yield t, c, h, side_c + vert[0], side_h + vert[1]
            here, prev_up, here_up, here_down = after, here_up, after_up, after_down


def forward_kernel(scale, own, chk, above, below, from_right, from_left, vs, fc, fh, onc, onh):
    stencil = Stencil()
    lane = stencil.lane
    s = jnp.full((8, LANES), scale[0], F32)
    for t in range(FEXT // 8):
        row = pl.ds(t * 8, 8)
        for plane in range(FPLANES):
            at = G_ADJ + G_ONS + (plane // 8) * FEXT + t * 8
            fc[plane, row, :] = fwd_tile(chk, above, below, plane, t)
            fh[plane, row, :] = unpack_strip(from_right, from_left, lane, at, at, plane % 8, 8)
        e = t + (HALO - FHALO) // 8
        at = G_ADJ + (e % 3) * 8
        onc[row, :] = main_tile(own, above, below, ONS, e)
        onh[row, :] = unpack_strip(from_right, from_left, lane, at, at, e // 3, 4)
    for segment in range(2):
        for which in range(2):
            for v in range(4):
                for i in range(4):
                    vs[segment * SEG + which, v, pl.ds(i * 8, 8), :] = tile(
                        chk, (segment * 8 + which * 4 + v) * ROWS + i * 8
                    )

    def forward(k, new, old, lo, hi):
        for segment in range(2):
            for v in range(4):
                p_new = segment * 8 + new * 4 + v
                p_old = segment * 8 + old * 4 + v
                for t, c, h, nc, nh in stencil.tiles(fc, fh, p_new, lo, hi, FEXT // 8):
                    row = pl.ds(t * 8, 8)
                    out_c = onc[row, :] * c - s * nc - fc[p_old, row, :]
                    out_h = onh[row, :] * h - s * nh - fh[p_old, row, :]
                    fc[p_old, row, :] = out_c
                    fh[p_old, row, :] = out_h
                    if 2 <= t < 6:
                        vs[segment * SEG + k, v, pl.ds((t - 2) * 8, 8), :] = out_c

    for start, stop, lo, hi in ((1, 4, 0, 8), (4, 8, 1, 7)):
        def body(i, carry, lo=lo, hi=hi):
            forward(2 * i, 1, 0, lo, hi)
            forward(2 * i + 1, 0, 1, lo, hi)
            return carry
        lax.fori_loop(start, stop, body, 0)


def adjoint_kernel(
    coef, scale, own, above, below, from_right, from_left, swapped, vs, wcs,
    adj_out, grad_out,
    xc, xh, sgc, sgh, rsh, onc, onh, whr, wcr,
):
    stencil = Stencil()
    lane = stencil.lane
    s = jnp.full((8, LANES), scale[0], F32)

    def strip(row, j, count):
        return unpack_strip(from_right, from_left, lane, row, row, j, count)

    for t in range(EXT // 8):
        row = pl.ds(t * 8, 8)
        for plane in range(8):
            xc[plane, row, :] = main_tile(own, above, below, plane, t)
            xh[plane, row, :] = strip((plane // 4) * EXT + t * 8, plane % 4, 4)
        for v in range(4):
            sgc[v, row, :] = main_tile(own, above, below, SGN + v, t)
            sgh[v, row, :] = strip(2 * EXT + t * 8, v, 4)
        for e in range(HALF):
            at = (e // 4) * EXT + t * 8
            rsh[e, row, :] = strip(G_RES + at, e % 4, 4)
            rsh[HALF + e, row, :] = unpack_strip(
                swapped, swapped, lane, at, 2 * EXT + at, e % 4, 4
            )
        onc[row, :] = main_tile(own, above, below, ONS, t)
        onh[row, :] = strip(G_ADJ + (t % 3) * 8, t // 3, 4)

    def adjoint(t_term, new, old, lo, hi, grads):
        grads = list(grads)
        factors = splats(coef, t_term)
        for t in range(lo, hi):
            row = pl.ds(t * 8, 8)
            whr[row, :] = weigh(factors, [rsh[e, row, :] for e in range(2 * HALF)])
            if not 4 <= t < 8:
                at = 4 * EXT + t * 8 + (0 if t < 4 else (HALF - 2) * ROWS)
                planes = [tile(swapped, at + e * ROWS) for e in range(HALF)]
                wcr[row, :] = wcs[t_term, row, :] + weigh(factors[HALF:], planes)
        for v in range(4):
            p_new, p_old = new * 4 + v, old * 4 + v
            for t, c, h, nc, nh in stencil.tiles(xc, xh, p_new, lo, hi, EXT // 8):
                row = pl.ds(t * 8, 8)
                if 4 <= t < 8:
                    grads[t - 4] = grads[t - 4] + c * vs[t_term, v, pl.ds((t - 4) * 8, 8), :]
                xc[p_old, row, :] = (
                    (wcs[t_term, row, :] if 4 <= t < 8 else wcr[row, :]) * sgc[v, row, :]
                    + (onc[row, :] * c - s * nc)
                    - xc[p_old, row, :]
                )
                xh[p_old, row, :] = (
                    whr[row, :] * sgh[v, row, :]
                    + (onh[row, :] * h - s * nh)
                    - xh[p_old, row, :]
                )
        return tuple(grads)

    grads = tuple(jnp.zeros((8, LANES), F32) for _ in range(4))
    for phase in range(4):
        lo, hi = phase_tiles(phase)
        def body(i, carry, phase=phase, lo=lo, hi=hi):
            t_term = TERMS - 1 - 8 * phase - 2 * i
            carry = adjoint(t_term, 0, 1, lo, hi, carry)
            return adjoint(t_term - 1, 1, 0, lo, hi, carry)
        grads = lax.fori_loop(0, 4, body, grads)
    for i in range(4):
        grad_out[pl.ds(i * 8, 8), :] = grads[i] * s
    for which in range(2):
        for v in range(4):
            for i in range(4):
                adj_out[which, v, pl.ds(i * 8, 8), :] = xc[which * 4 + v, pl.ds(HALO + i * 8, 8), :]


VMEM_SPEC = pl.BlockSpec(memory_space=pltpu.VMEM)
SMEM_SPEC = pl.BlockSpec(memory_space=pltpu.SMEM)
HBM_SPEC = pl.BlockSpec(memory_space=pltpu.HBM)


def params(mib):
    return pltpu.CompilerParams(vmem_limit_bytes=mib * 1024 * 1024)


def per_device(
    checkpoints,
    adjoints_in,
    vector_bits,
    potential_int,
    pot_scale,
    energies,
    residual,
    first_segment,
):
    core = lax.axis_index("vec") % 2
    coefs = window_coefs(first_segment, energies)
    coefs = jnp.where(core == 0, coefs, jnp.roll(coefs, HALF, axis=1))
    core = core[None]
    scale = 2.0 / (4.5 + QMAX * pot_scale)
    chk = checkpoints.reshape(FPLANES * ROWS, LANES)
    res = residual.reshape(2 * HALF * ROWS, LANES)
    send = jax.ShapeDtypeStruct((MAIN + FPLANES * FHALO, LANES), F32)
    own, to_above, chk, res_other = pl.pallas_call(
        prepare_kernel,
        out_shape=(
            send,
            send,
            jax.ShapeDtypeStruct((FPLANES * ROWS, LANES), F32),
            jax.ShapeDtypeStruct((HALF * ROWS, LANES), F32),
        ),
        in_specs=[SMEM_SPEC] * 2 + [HBM_SPEC] * 5,
        out_specs=(VMEM_SPEC,) * 4,
        scratch_shapes=[
            pltpu.VMEM((4 * ROWS, LANES), jnp.int32),
            pltpu.VMEM((ROWS, LANES), jnp.int32),
            pltpu.SemaphoreType.DMA((4 + 2 * (2 + FPLANES),)),
        ],
        compiler_params=params(4),
        name="prepare",
    )(
        core,
        pot_scale,
        *(
            pltpu.with_memory_space_constraint(value, pltpu.HBM)
            for value in (
                adjoints_in.reshape(8 * ROWS, LANES),
                vector_bits.reshape(4 * ROWS, LANES),
                potential_int,
                res,
                chk,
            )
        ),
    )

    def shift(value, axis, step):
        n = lax.axis_size(axis)
        return lax.ppermute(value, axis, [(i, (i + step) % n) for i in range(n)])

    def swap_cores(value):
        return lax.ppermute(value, "vec", [(0, 1), (1, 0), (2, 3), (3, 2)])

    above = shift(own, "row", 1)
    below = shift(to_above, "row", -1)

    strips = jax.ShapeDtypeStruct((G_ROWS, LANES), F32)
    to_left, to_right = pl.pallas_call(
        pack_kernel,
        out_shape=(strips, strips),
        in_specs=[VMEM_SPEC] * 4,
        out_specs=(VMEM_SPEC,) * 2,
        compiler_params=params(6),
        name="pack_columns",
    )(own, chk, above, below)
    from_left = shift(to_right, "col", 1)
    from_right = shift(to_left, "col", -1)
    weights = pl.pallas_call(
        weights_kernel,
        out_shape=jax.ShapeDtypeStruct((TERMS, EXT, LANES), F32),
        in_specs=[SMEM_SPEC] + [VMEM_SPEC] * 4,
        out_specs=VMEM_SPEC,
        compiler_params=params(6),
        cost_estimate=pl.CostEstimate(flops=12_000_000, bytes_accessed=4_000_000, transcendentals=0),
        name="weights",
    )(coefs, own, res_other, above, below)

    weights, from_right, from_left = lax.optimization_barrier((weights, from_right, from_left))
    strip_rows = slice(G_RES, G_RES + 2 * EXT)
    res_rows = slice(RES * ROWS, (RES + HALF) * ROWS)
    swapped = swap_cores(
        jnp.concatenate(
            [from_right[strip_rows], from_left[strip_rows], above[res_rows], below[res_rows]], axis=0
        )
    )
    frame = (FPLANES, FEXT, LANES)
    states = pl.pallas_call(
        forward_kernel,
        out_shape=jax.ShapeDtypeStruct((TERMS, 4, ROWS, LANES), F32),
        in_specs=[SMEM_SPEC] + [VMEM_SPEC] * 6,
        out_specs=VMEM_SPEC,
        scratch_shapes=[
            pltpu.VMEM(frame, F32), pltpu.VMEM(frame, F32),
            pltpu.VMEM(frame[1:], F32), pltpu.VMEM(frame[1:], F32),
        ],
        compiler_params=params(8),
        cost_estimate=pl.CostEstimate(flops=20_000_000, bytes_accessed=6_000_000, transcendentals=0),
        name="forward",
    )(scale, own, chk, above, below, from_right, from_left)

    ext = (EXT, LANES)
    adjoint_out, grad = pl.pallas_call(
        adjoint_kernel,
        out_shape=(
            jax.ShapeDtypeStruct((2, 4, ROWS, LANES), F32),
            jax.ShapeDtypeStruct((ROWS, LANES), F32),
        ),
        in_specs=[SMEM_SPEC, SMEM_SPEC] + [VMEM_SPEC] * 8,
        out_specs=(VMEM_SPEC, VMEM_SPEC),
        scratch_shapes=[
            pltpu.VMEM((8, *ext), F32), pltpu.VMEM((8, *ext), F32),
            pltpu.VMEM((4, *ext), F32), pltpu.VMEM((4, *ext), F32),
            pltpu.VMEM((2 * HALF, *ext), F32),
            pltpu.VMEM(ext, F32), pltpu.VMEM(ext, F32), pltpu.VMEM(ext, F32), pltpu.VMEM(ext, F32),
        ],
        compiler_params=params(10),
        name="adjoint",
    )(coefs, scale, own, above, below, from_right, from_left, swapped, states, weights)

    grad = jnp.sum(lax.all_gather(grad, "vec"), axis=0)
    return grad, adjoint_out


def solution(mesh):
    return jax.shard_map(
        per_device,
        mesh=mesh,
        in_specs=(
            P(None, None, "vec", "row", "col"),
            P(None, "vec", "row", "col"),
            P("vec", "row", "col"),
            P("row", "col"),
            P(),
            P(),
            P(None, "row", "col"),
            P(),
        ),
        out_specs=(P("row", "col"), P(None, "vec", "row", "col")),
        check_vma=False,
    )
```

```python
import functools
import math

import jax
import jax.numpy as jnp
from jax import lax
from jax.experimental import pallas as pl
from jax.experimental.pallas import tpu as pltpu
from jax.sharding import PartitionSpec as P

SEG = 16
MOMENTS = 1024
QMAX = 32767
TERMS = 2 * SEG
NVEC = 16
F32 = jnp.float32

ADJ, SGN, RES, ONS = 0, 8, 12, 20
PLANES = 21
HALF = 8
ROWS = 32
HALO = 32
EXT = ROWS + 2 * HALO
FHALO = 16
FEXT = ROWS + 2 * FHALO
LANES = 128
FPLANES = 16
MAIN = PLANES * ROWS
WIDE = EXT // 8
GROUPS = 5
RES_GROUP = 3
OWN_ONS = GROUPS * ROWS
OWN_CHK = OWN_ONS + 8
OWN_ROWS = OWN_CHK + 2 * ROWS
EDGE_ONS = GROUPS * 2 * HALO
EDGE_CHK = EDGE_ONS + 16
EDGE_ROWS = EDGE_CHK + 4 * FHALO


def window_coefs(first_segment, energies):
    moment_order = first_segment[0] * SEG + jnp.arange(TERMS, dtype=jnp.int32)
    degree = moment_order.astype(jnp.float32)
    kernel_norm = float(MOMENTS + 1)
    angle_step = math.pi / kernel_norm
    jackson = (
        (kernel_norm - degree) * jnp.cos(angle_step * degree)
        + jnp.sin(angle_step * degree) * (math.cos(angle_step) / math.sin(angle_step))
    ) / kernel_norm
    factor = jnp.where(moment_order == 0, 1.0, 2.0).astype(jnp.float32)
    angles = jnp.arccos(energies)
    cosines = jnp.cos(degree[:, None] * angles[None, :])
    return (jackson * factor)[:, None] * cosines / (math.pi * jnp.sin(angles))[None, :]


def lane_iota():
    return lax.broadcasted_iota(jnp.int32, (8, LANES), 1)


def tile(ref, row):
    return ref[pl.ds(row, 8), :]


def main_tile(own, above, below, plane, t):
    section = (above, own, below)[t // 4]
    return tile(section, plane * ROWS + (t % 4) * 8)


def fwd_tile(chk, above, below, plane, t):
    if t < 2:
        return tile(above, MAIN + plane * FHALO + t * 8)
    if t < 6:
        return tile(chk, plane * ROWS + (t - 2) * 8)
    return tile(below, MAIN + plane * FHALO + (t - 6) * 8)


def prepare_kernel(
    core, scalar, adj, bits, pot, res, chk,
    to_below, to_above, chk_v, res_v, bits_v, pot_v, sems
):
    copies = []

    def start(src, dst):
        copy = pltpu.make_async_copy(src, dst, sems.at[len(copies)])
        copy.start()
        copies.append(copy)

    first_res = pl.multiple_of(core[0] * (HALF * ROWS), HALF * ROWS)
    start(bits, bits_v)
    start(pot, pot_v)
    for out, first in ((to_below, ROWS - FHALO), (to_above, 0)):
        start(adj, out.at[pl.ds(ADJ * ROWS, 8 * ROWS)])
        start(res.at[pl.ds(first_res, HALF * ROWS)], out.at[pl.ds(RES * ROWS, HALF * ROWS)])
        for plane in range(FPLANES):
            start(
                chk.at[pl.ds(plane * ROWS + first, FHALO)],
                out.at[pl.ds(MAIN + plane * FHALO, FHALO)],
            )
    start(chk, chk_v)
    start(res.at[pl.ds(pl.multiple_of(HALF * ROWS - first_res, HALF * ROWS), HALF * ROWS)], res_v)
    copies[0].wait()
    signs = (2 * bits_v[...] - 1).astype(F32) * (1.0 / NVEC)
    copies[1].wait()
    pot_factor = scalar[0]
    scale = 2.0 / (4.5 + QMAX * pot_factor)
    onsite = pot_v[...].astype(F32) * (pot_factor * scale)
    for out in (to_below, to_above):
        out[pl.ds(SGN * ROWS, 4 * ROWS), :] = signs
        out[pl.ds(ONS * ROWS, ROWS), :] = onsite
    for copy in copies[2:]:
        copy.wait()


def pack(tiles, row, to_left, to_right):
    lane = lane_iota()
    count = len(tiles)
    width = LANES // count
    group = lane // width
    left = right = None
    for j, value in enumerate(tiles):
        rolled = pltpu.roll(value, width * j, 1) if j else value
        left = rolled if j == 0 else jnp.where(group == j, rolled, left)
        right = rolled if j == 0 else jnp.where(group == (j + count - 1) % count, rolled, right)
    to_left[pl.ds(row, 8), :] = left
    to_right[pl.ds(row, 8), :] = right


def pack_own_kernel(own, chk, to_left, to_right):
    for g in range(GROUPS):
        for i in range(4):
            tiles = [tile(own, (4 * g + j) * ROWS + i * 8) for j in range(4)]
            pack(tiles, g * ROWS + i * 8, to_left, to_right)
    pack([tile(own, ONS * ROWS + j * 8) for j in range(4)], OWN_ONS, to_left, to_right)
    for g in range(2):
        for i in range(4):
            tiles = [tile(chk, (8 * g + j) * ROWS + i * 8) for j in range(8)]
            pack(tiles, OWN_CHK + g * ROWS + i * 8, to_left, to_right)


def pack_edge_kernel(above, below, to_left, to_right):
    for side, ref in enumerate((above, below)):
        for g in range(GROUPS):
            for i in range(4):
                tiles = [tile(ref, (4 * g + j) * ROWS + i * 8) for j in range(4)]
                pack(tiles, g * 2 * HALO + side * HALO + i * 8, to_left, to_right)
        tiles = [tile(ref, ONS * ROWS + j * 8) for j in range(4)]
        pack(tiles, EDGE_ONS + side * 8, to_left, to_right)
        for g in range(2):
            for i in range(2):
                tiles = [tile(ref, MAIN + (8 * g + j) * FHALO + i * 8) for j in range(8)]
                pack(tiles, EDGE_CHK + g * 2 * FHALO + side * FHALO + i * 8, to_left, to_right)


def unpack_strip(right, left, lane, j, count):
    width = LANES // count
    mixed = jnp.where(lane // width == j, tile(*right), tile(*left))
    return pltpu.roll(mixed, (LANES - width * j) % LANES, 1) if j else mixed


class Strips:
    def __init__(self, own_right, own_left, edge_right, edge_left, lane):
        self.own, self.edge, self.lane = (own_right, own_left), (edge_right, edge_left), lane

    def unpack(self, refs, row, j, count):
        return unpack_strip((refs[0], row), (refs[1], row), self.lane, j, count)

    def plane(self, index, t):
        g, j = index // 4, index % 4
        if 4 <= t < 8:
            return self.unpack(self.own, g * ROWS + (t - 4) * 8, j, 4)
        return self.unpack(self.edge, g * 2 * HALO + (t if t < 4 else t - 4) * 8, j, 4)

    def onsite(self, t):
        if 4 <= t < 8:
            return self.unpack(self.own, OWN_ONS, t - 4, 4)
        return self.unpack(self.edge, EDGE_ONS + t // 8 * 8, t % 4, 4)

    def checkpoint(self, plane, t):
        g, j = plane // 8, plane % 8
        if 2 <= t < 6:
            return self.unpack(self.own, OWN_CHK + g * ROWS + (t - 2) * 8, j, 8)
        at = EDGE_CHK + g * 2 * FHALO + (t if t < 2 else t - 4) * 8
        return self.unpack(self.edge, at, j, 8)


SWAP_OWN, SWAP_EDGE = 2 * ROWS, 4 * HALO
SWAP_SIDE = SWAP_OWN + SWAP_EDGE
SWAP_MAIN = 2 * SWAP_SIDE


def swapped_strip(swapped, lane, e, t):
    g, j = e // 4, e % 4
    if 4 <= t < 8:
        row = g * ROWS + (t - 4) * 8
    else:
        row = SWAP_OWN + g * 2 * HALO + (t if t < 4 else t - 4) * 8
    return unpack_strip((swapped, row), (swapped, SWAP_SIDE + row), lane, j, 4)


def splats(coef, t_term):
    return [jnp.full((8, LANES), coef[t_term, e], F32) for e in range(2 * HALF)]


def weigh(factors, planes):
    terms = [value * factor for value, factor in zip(planes, factors)]
    while len(terms) > 1:
        terms = [x + y for x, y in zip(terms[::2], terms[1::2])]
    return terms[0]


def phase_tiles(phase):
    return phase, EXT // 8 - phase


def weights_kernel(coef, own, res_other, above, below, out):
    def residuals(t):
        planes = [main_tile(own, above, below, RES + e, t) for e in range(HALF)]
        if 4 <= t < 8:
            planes += [tile(res_other, e * ROWS + (t - 4) * 8) for e in range(HALF)]
        return planes

    for phase in range(4):
        lo, hi = phase_tiles(phase)

        def body(i, carry, phase=phase, lo=lo, hi=hi):
            t_term = TERMS - 8 * (phase + 1) + i
            factors = splats(coef, t_term)
            for t in range(lo, hi):
                out[t_term, pl.ds(t * 8, 8), :] = weigh(factors, residuals(t))
            return carry

        lax.fori_loop(0, 8, body, 0)


class Stencil:
    def __init__(self):
        lane, sub = lane_iota(), lax.broadcasted_iota(jnp.int32, (8, LANES), 0)
        self.lane = lane
        self.first_lane, self.last_lane = lane == 0, lane == LANES - 1
        self.first_sub, self.last_sub = sub == 0, sub == 7

    def tiles(self, cref, href, plane, lo, hi, count):
        def load(t):
            return cref[plane, pl.ds(t * 8, 8), :], href[plane, pl.ds(t * 8, 8), :]

        def rolled(pair, shift):
            return tuple(pltpu.roll(p, shift, 0) for p in pair)

        here = load(lo)
        here_up, here_down = rolled(here, 1), rolled(here, 7)
        prev_up = rolled(load(lo - 1), 1) if lo > 0 else here_up
        for t in range(lo, hi):
            after = load(t + 1) if t + 1 < count else here
            after_up, after_down = rolled(after, 1), rolled(after, 7)
            c, h = here
            cl, cr = pltpu.roll(c, 1, 1), pltpu.roll(c, LANES - 1, 1)
            hl, hr = pltpu.roll(h, 1, 1), pltpu.roll(h, LANES - 1, 1)
            side_c = jnp.where(self.first_lane, hl, cl) + jnp.where(self.last_lane, hr, cr)
            side_h = jnp.where(self.first_lane, cl, hl) + jnp.where(self.last_lane, cr, hr)
            vert = [
                jnp.where(self.first_sub, prev_up[k], here_up[k])
                + jnp.where(self.last_sub, after_down[k], here_down[k])
                for k in range(2)
            ]
            yield t, c, h, side_c + vert[0], side_h + vert[1]
            here, prev_up, here_up, here_down = after, here_up, after_up, after_down


def forward_kernel(
    scale, own, chk, above, below, own_right, own_left, edge_right, edge_left,
    vs, fc, fh, onc, onh,
):
    stencil = Stencil()
    strips = Strips(own_right, own_left, edge_right, edge_left, stencil.lane)
    s = jnp.full((8, LANES), scale[0], F32)
    for t in range(FEXT // 8):
        row = pl.ds(t * 8, 8)
        for plane in range(FPLANES):
            fc[plane, row, :] = fwd_tile(chk, above, below, plane, t)
            fh[plane, row, :] = strips.checkpoint(plane, t)
        e = t + (HALO - FHALO) // 8
        onc[row, :] = main_tile(own, above, below, ONS, e)
        onh[row, :] = strips.onsite(e)
    for segment in range(2):
        for which in range(2):
            for v in range(4):
                for i in range(4):
                    vs[segment * SEG + which, v, pl.ds(i * 8, 8), :] = tile(
                        chk, (segment * 8 + which * 4 + v) * ROWS + i * 8
                    )

    def forward(k, new, old, lo, hi):
        for segment in range(2):
            for v in range(4):
                p_new = segment * 8 + new * 4 + v
                p_old = segment * 8 + old * 4 + v
                for t, c, h, nc, nh in stencil.tiles(fc, fh, p_new, lo, hi, FEXT // 8):
                    row = pl.ds(t * 8, 8)
                    out_c = onc[row, :] * c - s * nc - fc[p_old, row, :]
                    out_h = onh[row, :] * h - s * nh - fh[p_old, row, :]
                    fc[p_old, row, :] = out_c
                    fh[p_old, row, :] = out_h
                    if 2 <= t < 6:
                        vs[segment * SEG + k, v, pl.ds((t - 2) * 8, 8), :] = out_c

    for start, stop, lo, hi in ((1, 4, 0, 8), (4, 8, 1, 7)):
        def body(i, carry, lo=lo, hi=hi):
            forward(2 * i, 1, 0, lo, hi)
            forward(2 * i + 1, 0, 1, lo, hi)
            return carry
        lax.fori_loop(start, stop, body, 0)


def adjoint_kernel(
    coef, scale, own, above, below, own_right, own_left, edge_right, edge_left, swapped, vs, wcs,
    adj_out, grad_out,
    xc, xh, sgc, sgh, rsh, onc, onh, whr, wcr,
):
    stencil = Stencil()
    strips = Strips(own_right, own_left, edge_right, edge_left, stencil.lane)
    s = jnp.full((8, LANES), scale[0], F32)

    for t in range(EXT // 8):
        row = pl.ds(t * 8, 8)
        for plane in range(8):
            xc[plane, row, :] = main_tile(own, above, below, plane, t)
            xh[plane, row, :] = strips.plane(plane, t)
        for v in range(4):
            sgc[v, row, :] = main_tile(own, above, below, SGN + v, t)
            sgh[v, row, :] = strips.plane(SGN + v, t)
        for e in range(HALF):
            rsh[e, row, :] = strips.plane(RES + e, t)
            rsh[HALF + e, row, :] = swapped_strip(swapped, stencil.lane, e, t)
        onc[row, :] = main_tile(own, above, below, ONS, t)
        onh[row, :] = strips.onsite(t)

    def adjoint(t_term, new, old, lo, hi, grads):
        grads = list(grads)
        factors = splats(coef, t_term)
        for t in range(lo, hi):
            row = pl.ds(t * 8, 8)
            whr[row, :] = weigh(factors, [rsh[e, row, :] for e in range(2 * HALF)])
            if not 4 <= t < 8:
                at = SWAP_MAIN + t * 8 + (0 if t < 4 else (HALF - 2) * ROWS)
                planes = [tile(swapped, at + e * ROWS) for e in range(HALF)]
                wcr[row, :] = wcs[t_term, row, :] + weigh(factors[HALF:], planes)
        for v in range(4):
            p_new, p_old = new * 4 + v, old * 4 + v
            for t, c, h, nc, nh in stencil.tiles(xc, xh, p_new, lo, hi, EXT // 8):
                row = pl.ds(t * 8, 8)
                if 4 <= t < 8:
                    grads[t - 4] = grads[t - 4] + c * vs[t_term, v, pl.ds((t - 4) * 8, 8), :]
                xc[p_old, row, :] = (
                    (wcs[t_term, row, :] if 4 <= t < 8 else wcr[row, :]) * sgc[v, row, :]
                    + (onc[row, :] * c - s * nc)
                    - xc[p_old, row, :]
                )
                xh[p_old, row, :] = (
                    whr[row, :] * sgh[v, row, :]
                    + (onh[row, :] * h - s * nh)
                    - xh[p_old, row, :]
                )
        return tuple(grads)

    grads = tuple(jnp.zeros((8, LANES), F32) for _ in range(4))
    for phase in range(4):
        lo, hi = phase_tiles(phase)
        def body(i, carry, phase=phase, lo=lo, hi=hi):
            t_term = TERMS - 1 - 8 * phase - 2 * i
            carry = adjoint(t_term, 0, 1, lo, hi, carry)
            return adjoint(t_term - 1, 1, 0, lo, hi, carry)
        grads = lax.fori_loop(0, 4, body, grads)
    for i in range(4):
        grad_out[pl.ds(i * 8, 8), :] = grads[i] * s
    for which in range(2):
        for v in range(4):
            for i in range(4):
                adj_out[which, v, pl.ds(i * 8, 8), :] = xc[which * 4 + v, pl.ds(HALO + i * 8, 8), :]


VMEM_SPEC = pl.BlockSpec(memory_space=pltpu.VMEM)
SMEM_SPEC = pl.BlockSpec(memory_space=pltpu.SMEM)
HBM_SPEC = pl.BlockSpec(memory_space=pltpu.HBM)


def params(mib):
    return pltpu.CompilerParams(vmem_limit_bytes=mib * 1024 * 1024)


def per_device(
    checkpoints,
    adjoints_in,
    vector_bits,
    potential_int,
    pot_scale,
    energies,
    residual,
    first_segment,
):
    core = lax.axis_index("vec") % 2
    coefs = window_coefs(first_segment, energies)
    coefs = jnp.where(core == 0, coefs, jnp.roll(coefs, HALF, axis=1))
    core = core[None]
    scale = 2.0 / (4.5 + QMAX * pot_scale)
    chk = checkpoints.reshape(FPLANES * ROWS, LANES)
    res = residual.reshape(2 * HALF * ROWS, LANES)
    send = jax.ShapeDtypeStruct((MAIN + FPLANES * FHALO, LANES), F32)
    own, to_above, chk, res_other = pl.pallas_call(
        prepare_kernel,
        out_shape=(
            send,
            send,
            jax.ShapeDtypeStruct((FPLANES * ROWS, LANES), F32),
            jax.ShapeDtypeStruct((HALF * ROWS, LANES), F32),
        ),
        in_specs=[SMEM_SPEC] * 2 + [HBM_SPEC] * 5,
        out_specs=(VMEM_SPEC,) * 4,
        scratch_shapes=[
            pltpu.VMEM((4 * ROWS, LANES), jnp.int32),
            pltpu.VMEM((ROWS, LANES), jnp.int32),
            pltpu.SemaphoreType.DMA((4 + 2 * (2 + FPLANES),)),
        ],
        compiler_params=params(4),
        name="prepare",
    )(
        core,
        pot_scale,
        *(
            pltpu.with_memory_space_constraint(value, pltpu.HBM)
            for value in (
                adjoints_in.reshape(8 * ROWS, LANES),
                vector_bits.reshape(4 * ROWS, LANES),
                potential_int,
                res,
                chk,
            )
        ),
    )

    def shift(value, axis, step):
        n = lax.axis_size(axis)
        return lax.ppermute(value, axis, [(i, (i + step) % n) for i in range(n)])

    def swap_cores(value):
        return lax.ppermute(value, "vec", [(0, 1), (1, 0), (2, 3), (3, 2)])

    above = shift(own, "row", 1)
    below = shift(to_above, "row", -1)

    def packed(kernel, rows, name, *values):
        shape = jax.ShapeDtypeStruct((rows, LANES), F32)
        to_left, to_right = pl.pallas_call(
            kernel,
            out_shape=(shape, shape),
            in_specs=[VMEM_SPEC] * len(values),
            out_specs=(VMEM_SPEC,) * 2,
            compiler_params=params(6),
            name=name,
        )(*values)
        return shift(to_left, "col", -1), shift(to_right, "col", 1)

    coefs, late_own, late_chk = lax.optimization_barrier((coefs, own, chk))
    own_strips = packed(pack_own_kernel, OWN_ROWS, "pack_own", late_own, late_chk)
    edge_strips = packed(pack_edge_kernel, EDGE_ROWS, "pack_edge", above, below)
    weights = pl.pallas_call(
        weights_kernel,
        out_shape=jax.ShapeDtypeStruct((TERMS, EXT, LANES), F32),
        in_specs=[SMEM_SPEC] + [VMEM_SPEC] * 4,
        out_specs=VMEM_SPEC,
        compiler_params=params(6),
        cost_estimate=pl.CostEstimate(flops=12_000_000, bytes_accessed=4_000_000, transcendentals=0),
        name="weights",
    )(coefs, own, res_other, above, below)

    weights, edge_strips = lax.optimization_barrier((weights, edge_strips))
    res_rows = slice(RES * ROWS, (RES + HALF) * ROWS)
    own_rows = slice(RES_GROUP * ROWS, GROUPS * ROWS)
    edge_rows = slice(RES_GROUP * 2 * HALO, GROUPS * 2 * HALO)
    swapped = swap_cores(
        jnp.concatenate(
            [
                own_strips[0][own_rows], edge_strips[0][edge_rows],
                own_strips[1][own_rows], edge_strips[1][edge_rows],
                above[res_rows], below[res_rows],
            ],
            axis=0,
        )
    )
    frame = (FPLANES, FEXT, LANES)
    states = pl.pallas_call(
        forward_kernel,
        out_shape=jax.ShapeDtypeStruct((TERMS, 4, ROWS, LANES), F32),
        in_specs=[SMEM_SPEC] + [VMEM_SPEC] * 8,
        out_specs=VMEM_SPEC,
        scratch_shapes=[
            pltpu.VMEM(frame, F32), pltpu.VMEM(frame, F32),
            pltpu.VMEM(frame[1:], F32), pltpu.VMEM(frame[1:], F32),
        ],
        compiler_params=params(8),
        cost_estimate=pl.CostEstimate(flops=20_000_000, bytes_accessed=6_000_000, transcendentals=0),
        name="forward",
    )(scale, own, chk, above, below, *own_strips, *edge_strips)

    ext = (EXT, LANES)
    adjoint_out, grad = pl.pallas_call(
        adjoint_kernel,
        out_shape=(
            jax.ShapeDtypeStruct((2, 4, ROWS, LANES), F32),
            jax.ShapeDtypeStruct((ROWS, LANES), F32),
        ),
        in_specs=[SMEM_SPEC, SMEM_SPEC] + [VMEM_SPEC] * 10,
        out_specs=(VMEM_SPEC, VMEM_SPEC),
        scratch_shapes=[
            pltpu.VMEM((8, *ext), F32), pltpu.VMEM((8, *ext), F32),
            pltpu.VMEM((4, *ext), F32), pltpu.VMEM((4, *ext), F32),
            pltpu.VMEM((2 * HALF, *ext), F32),
            pltpu.VMEM(ext, F32), pltpu.VMEM(ext, F32), pltpu.VMEM(ext, F32), pltpu.VMEM(ext, F32),
        ],
        compiler_params=params(10),
        name="adjoint",
    )(
        coefs, scale, own, above, below, *own_strips, *edge_strips, swapped, states, weights
    )

    grad = jnp.sum(lax.all_gather(grad, "vec"), axis=0)
    return grad, adjoint_out


def solution(mesh):
    return jax.shard_map(
        per_device,
        mesh=mesh,
        in_specs=(
            P(None, None, "vec", "row", "col"),
            P(None, "vec", "row", "col"),
            P("vec", "row", "col"),
            P("row", "col"),
            P(),
            P(),
            P(None, "row", "col"),
            P(),
        ),
        out_specs=(P("row", "col"), P(None, "vec", "row", "col")),
        check_vma=False,
    )
```

```python
import functools
import math

import jax
import jax.numpy as jnp
from jax import lax
from jax.experimental import pallas as pl
from jax.experimental.pallas import tpu as pltpu
from jax.sharding import PartitionSpec as P

SEG = 16
MOMENTS = 1024
QMAX = 32767
TERMS = 2 * SEG
NVEC = 16
F32 = jnp.float32

ADJ, SGN, RES, ONS = 0, 8, 12, 20
PLANES = 21
HALF = 8
ROWS = 32
HALO = 32
EXT = ROWS + 2 * HALO
FHALO = 16
FEXT = ROWS + 2 * FHALO
LANES = 128
FPLANES = 16
MAIN = PLANES * ROWS
WIDE = EXT // 8
GROUPS = 5
RES_GROUP = 3
OWN_ONS = GROUPS * ROWS
OWN_CHK = OWN_ONS + 8
OWN_ROWS = OWN_CHK + 2 * ROWS
EDGE_ONS = GROUPS * 2 * HALO
EDGE_CHK = EDGE_ONS + 16
EDGE_ROWS = EDGE_CHK + 4 * FHALO


def window_coefs(first_segment, energies):
    moment_order = first_segment[0] * SEG + jnp.arange(TERMS, dtype=jnp.int32)
    degree = moment_order.astype(jnp.float32)
    kernel_norm = float(MOMENTS + 1)
    angle_step = math.pi / kernel_norm
    jackson = (
        (kernel_norm - degree) * jnp.cos(angle_step * degree)
        + jnp.sin(angle_step * degree) * (math.cos(angle_step) / math.sin(angle_step))
    ) / kernel_norm
    factor = jnp.where(moment_order == 0, 1.0, 2.0).astype(jnp.float32)
    angles = jnp.arccos(energies)
    cosines = jnp.cos(degree[:, None] * angles[None, :])
    return (jackson * factor)[:, None] * cosines / (math.pi * jnp.sin(angles))[None, :]


def lane_iota():
    return lax.broadcasted_iota(jnp.int32, (8, LANES), 1)


def tile(ref, row):
    return ref[pl.ds(row, 8), :]


def main_tile(own, above, below, plane, t):
    section = (above, own, below)[t // 4]
    return tile(section, plane * ROWS + (t % 4) * 8)


def fwd_tile(chk, above, below, plane, t):
    if t < 2:
        return tile(above, MAIN + plane * FHALO + t * 8)
    if t < 6:
        return tile(chk, plane * ROWS + (t - 2) * 8)
    return tile(below, MAIN + plane * FHALO + (t - 6) * 8)


def prepare_kernel(
    core, scalar, adj, bits, pot, res, chk,
    to_below, to_above, chk_v, res_v, bits_v, pot_v, sems
):
    copies = []

    def start(src, dst):
        copy = pltpu.make_async_copy(src, dst, sems.at[len(copies)])
        copy.start()
        copies.append(copy)

    first_res = pl.multiple_of(core[0] * (HALF * ROWS), HALF * ROWS)
    start(bits, bits_v)
    start(pot, pot_v)
    for out, first in ((to_below, ROWS - FHALO), (to_above, 0)):
        start(adj, out.at[pl.ds(ADJ * ROWS, 8 * ROWS)])
        start(res.at[pl.ds(first_res, HALF * ROWS)], out.at[pl.ds(RES * ROWS, HALF * ROWS)])
        for plane in range(FPLANES):
            start(
                chk.at[pl.ds(plane * ROWS + first, FHALO)],
                out.at[pl.ds(MAIN + plane * FHALO, FHALO)],
            )
    start(chk, chk_v)
    start(res.at[pl.ds(pl.multiple_of(HALF * ROWS - first_res, HALF * ROWS), HALF * ROWS)], res_v)
    copies[0].wait()
    signs = (2 * bits_v[...] - 1).astype(F32) * (1.0 / NVEC)
    copies[1].wait()
    pot_factor = scalar[0]
    scale = 2.0 / (4.5 + QMAX * pot_factor)
    onsite = pot_v[...].astype(F32) * (pot_factor * scale)
    for out in (to_below, to_above):
        out[pl.ds(SGN * ROWS, 4 * ROWS), :] = signs
        out[pl.ds(ONS * ROWS, ROWS), :] = onsite
    for copy in copies[2:]:
        copy.wait()


def pack(tiles, row, to_left, to_right):
    lane = lane_iota()
    count = len(tiles)
    width = LANES // count
    group = lane // width
    left = right = None
    for j, value in enumerate(tiles):
        rolled = pltpu.roll(value, width * j, 1) if j else value
        left = rolled if j == 0 else jnp.where(group == j, rolled, left)
        right = rolled if j == 0 else jnp.where(group == (j + count - 1) % count, rolled, right)
    to_left[pl.ds(row, 8), :] = left
    to_right[pl.ds(row, 8), :] = right


def pack_own_kernel(own, chk, to_left, to_right):
    for g in range(GROUPS):
        for i in range(4):
            tiles = [tile(own, (4 * g + j) * ROWS + i * 8) for j in range(4)]
            pack(tiles, g * ROWS + i * 8, to_left, to_right)
    pack([tile(own, ONS * ROWS + j * 8) for j in range(4)], OWN_ONS, to_left, to_right)
    for g in range(2):
        for i in range(4):
            tiles = [tile(chk, (8 * g + j) * ROWS + i * 8) for j in range(8)]
            pack(tiles, OWN_CHK + g * ROWS + i * 8, to_left, to_right)


def pack_edge_kernel(above, below, to_left, to_right):
    for side, ref in enumerate((above, below)):
        for g in range(GROUPS):
            for i in range(4):
                tiles = [tile(ref, (4 * g + j) * ROWS + i * 8) for j in range(4)]
                pack(tiles, g * 2 * HALO + side * HALO + i * 8, to_left, to_right)
        tiles = [tile(ref, ONS * ROWS + j * 8) for j in range(4)]
        pack(tiles, EDGE_ONS + side * 8, to_left, to_right)
        for g in range(2):
            for i in range(2):
                tiles = [tile(ref, MAIN + (8 * g + j) * FHALO + i * 8) for j in range(8)]
                pack(tiles, EDGE_CHK + g * 2 * FHALO + side * FHALO + i * 8, to_left, to_right)


def unpack_strip(right, left, lane, j, count):
    width = LANES // count
    mixed = jnp.where(lane // width == j, tile(*right), tile(*left))
    return pltpu.roll(mixed, (LANES - width * j) % LANES, 1) if j else mixed


class Strips:
    def __init__(self, own_right, own_left, edge_right, edge_left, lane):
        self.own, self.edge, self.lane = (own_right, own_left), (edge_right, edge_left), lane

    def unpack(self, refs, row, j, count):
        return unpack_strip((refs[0], row), (refs[1], row), self.lane, j, count)

    def plane(self, index, t):
        g, j = index // 4, index % 4
        if 4 <= t < 8:
            return self.unpack(self.own, g * ROWS + (t - 4) * 8, j, 4)
        return self.unpack(self.edge, g * 2 * HALO + (t if t < 4 else t - 4) * 8, j, 4)

    def onsite(self, t):
        if 4 <= t < 8:
            return self.unpack(self.own, OWN_ONS, t - 4, 4)
        return self.unpack(self.edge, EDGE_ONS + t // 8 * 8, t % 4, 4)

    def checkpoint(self, plane, t):
        g, j = plane // 8, plane % 8
        if 2 <= t < 6:
            return self.unpack(self.own, OWN_CHK + g * ROWS + (t - 2) * 8, j, 8)
        at = EDGE_CHK + g * 2 * FHALO + (t if t < 2 else t - 4) * 8
        return self.unpack(self.edge, at, j, 8)


SWAP_OWN, SWAP_EDGE = 2 * ROWS, 4 * HALO
SWAP_SIDE = SWAP_OWN + SWAP_EDGE
SWAP_MAIN = 2 * SWAP_SIDE


def swapped_strip(swapped, lane, e, t):
    g, j = e // 4, e % 4
    if 4 <= t < 8:
        row = g * ROWS + (t - 4) * 8
    else:
        row = SWAP_OWN + g * 2 * HALO + (t if t < 4 else t - 4) * 8
    return unpack_strip((swapped, row), (swapped, SWAP_SIDE + row), lane, j, 4)


def splats(coef, t_term):
    return [jnp.full((8, LANES), coef[t_term, e], F32) for e in range(2 * HALF)]


def weigh(factors, planes):
    terms = [value * factor for value, factor in zip(planes, factors)]
    while len(terms) > 1:
        terms = [x + y for x, y in zip(terms[::2], terms[1::2])]
    return terms[0]


def phase_tiles(phase):
    return phase, EXT // 8 - phase


def weights_kernel(coef, own, res_other, out):
    def body(t_term, carry):
        factors = splats(coef, t_term)
        for i in range(4):
            planes = [tile(own, (RES + e) * ROWS + i * 8) for e in range(HALF)]
            planes += [tile(res_other, e * ROWS + i * 8) for e in range(HALF)]
            out[t_term, pl.ds(i * 8, 8), :] = weigh(factors, planes)
        return carry

    lax.fori_loop(0, TERMS, body, 0)


def weigh_stacks(high, low, stacks, out, t):
    first = TERMS - 8 * (min(t, 3) + 1)
    rows = slice(8 * first, 8 * TERMS)
    stack = jnp.concatenate([jnp.concatenate(stack, axis=0) for stack in stacks], axis=1)
    upper = stack.astype(jnp.bfloat16)
    lower = (stack - upper.astype(F32)).astype(jnp.bfloat16)

    def product(x, y):
        return jnp.dot(x[rows, :], y, preferred_element_type=F32)

    result = product(high, upper) + (product(high, lower) + product(low, upper))
    for n in range(first, TERMS):
        part = result[8 * (n - first) : 8 * (n - first) + 8]
        out[n, pl.ds(t * 8, 8), :] = part[:, :LANES]
        out[n, pl.ds(EXT - 8 - t * 8, 8), :] = part[:, LANES:]


class Stencil:
    def __init__(self):
        lane, sub = lane_iota(), lax.broadcasted_iota(jnp.int32, (8, LANES), 0)
        self.lane = lane
        self.first_lane, self.last_lane = lane == 0, lane == LANES - 1
        self.first_sub, self.last_sub = sub == 0, sub == 7

    def tiles(self, cref, href, plane, lo, hi, count):
        def load(t):
            return cref[plane, pl.ds(t * 8, 8), :], href[plane, pl.ds(t * 8, 8), :]

        def rolled(pair, shift):
            return tuple(pltpu.roll(p, shift, 0) for p in pair)

        here = load(lo)
        here_up, here_down = rolled(here, 1), rolled(here, 7)
        prev_up = rolled(load(lo - 1), 1) if lo > 0 else here_up
        for t in range(lo, hi):
            after = load(t + 1) if t + 1 < count else here
            after_up, after_down = rolled(after, 1), rolled(after, 7)
            c, h = here
            cl, cr = pltpu.roll(c, 1, 1), pltpu.roll(c, LANES - 1, 1)
            hl, hr = pltpu.roll(h, 1, 1), pltpu.roll(h, LANES - 1, 1)
            side_c = jnp.where(self.first_lane, hl, cl) + jnp.where(self.last_lane, hr, cr)
            side_h = jnp.where(self.first_lane, cl, hl) + jnp.where(self.last_lane, cr, hr)
            vert = [
                jnp.where(self.first_sub, prev_up[k], here_up[k])
                + jnp.where(self.last_sub, after_down[k], here_down[k])
                for k in range(2)
            ]
            yield t, c, h, side_c + vert[0], side_h + vert[1]
            here, prev_up, here_up, here_down = after, here_up, after_up, after_down


def forward_kernel(
    scale, own, chk, above, below, own_right, own_left, edge_right, edge_left,
    vs, fc, fh, onc, onh,
):
    stencil = Stencil()
    strips = Strips(own_right, own_left, edge_right, edge_left, stencil.lane)
    s = jnp.full((8, LANES), scale[0], F32)
    for t in range(FEXT // 8):
        row = pl.ds(t * 8, 8)
        for plane in range(FPLANES):
            fc[plane, row, :] = fwd_tile(chk, above, below, plane, t)
            fh[plane, row, :] = strips.checkpoint(plane, t)
        e = t + (HALO - FHALO) // 8
        onc[row, :] = main_tile(own, above, below, ONS, e)
        onh[row, :] = strips.onsite(e)
    for segment in range(2):
        for which in range(2):
            for v in range(4):
                for i in range(4):
                    vs[segment * SEG + which, v, pl.ds(i * 8, 8), :] = tile(
                        chk, (segment * 8 + which * 4 + v) * ROWS + i * 8
                    )

    def forward(k, new, old, lo, hi):
        for segment in range(2):
            for v in range(4):
                p_new = segment * 8 + new * 4 + v
                p_old = segment * 8 + old * 4 + v
                for t, c, h, nc, nh in stencil.tiles(fc, fh, p_new, lo, hi, FEXT // 8):
                    row = pl.ds(t * 8, 8)
                    out_c = onc[row, :] * c - s * nc - fc[p_old, row, :]
                    out_h = onh[row, :] * h - s * nh - fh[p_old, row, :]
                    fc[p_old, row, :] = out_c
                    fh[p_old, row, :] = out_h
                    if 2 <= t < 6:
                        vs[segment * SEG + k, v, pl.ds((t - 2) * 8, 8), :] = out_c

    for start, stop, lo, hi in ((1, 4, 0, 8), (4, 8, 1, 7)):
        def body(i, carry, lo=lo, hi=hi):
            forward(2 * i, 1, 0, lo, hi)
            forward(2 * i + 1, 0, 1, lo, hi)
            return carry
        lax.fori_loop(start, stop, body, 0)


def adjoint_kernel(
    scale, high, low, own, above, below, own_right, own_left, edge_right, edge_left, swapped,
    vs, own_weights,
    adj_out, grad_out,
    xc, xh, sgc, sgh, onc, onh, wcs, whs,
):
    stencil = Stencil()
    strips = Strips(own_right, own_left, edge_right, edge_left, stencil.lane)
    s = jnp.full((8, LANES), scale[0], F32)

    for t in range(EXT // 8):
        row = pl.ds(t * 8, 8)
        for plane in range(8):
            xc[plane, row, :] = main_tile(own, above, below, plane, t)
            xh[plane, row, :] = strips.plane(plane, t)
        for v in range(4):
            sgc[v, row, :] = main_tile(own, above, below, SGN + v, t)
            sgh[v, row, :] = strips.plane(SGN + v, t)
        onc[row, :] = main_tile(own, above, below, ONS, t)
        onh[row, :] = strips.onsite(t)

    def halo_stack(t):
        return [strips.plane(RES + e, t) for e in range(HALF)] + [
            swapped_strip(swapped, stencil.lane, e, t) for e in range(HALF)
        ]

    def centre_stack(t):
        at = SWAP_MAIN + t * 8 + (0 if t < 4 else (HALF - 2) * ROWS)
        return [main_tile(own, above, below, RES + e, t) for e in range(HALF)] + [
            tile(swapped, at + e * ROWS) for e in range(HALF)
        ]

    for t in range(EXT // 16):
        other = EXT // 8 - 1 - t
        weigh_stacks(high, low, (halo_stack(t), halo_stack(other)), whs, t)
        if t < 4:
            weigh_stacks(high, low, (centre_stack(t), centre_stack(other)), wcs, t)

    def adjoint(t_term, new, old, lo, hi, grads):
        grads = list(grads)
        for v in range(4):
            p_new, p_old = new * 4 + v, old * 4 + v
            for t, c, h, nc, nh in stencil.tiles(xc, xh, p_new, lo, hi, EXT // 8):
                row = pl.ds(t * 8, 8)
                if 4 <= t < 8:
                    weight = own_weights[t_term, pl.ds((t - 4) * 8, 8), :]
                    grads[t - 4] = grads[t - 4] + c * vs[t_term, v, pl.ds((t - 4) * 8, 8), :]
                else:
                    weight = wcs[t_term, row, :]
                xc[p_old, row, :] = (
                    weight * sgc[v, row, :]
                    + (onc[row, :] * c - s * nc)
                    - xc[p_old, row, :]
                )
                xh[p_old, row, :] = (
                    whs[t_term, row, :] * sgh[v, row, :]
                    + (onh[row, :] * h - s * nh)
                    - xh[p_old, row, :]
                )
        return tuple(grads)

    grads = tuple(jnp.zeros((8, LANES), F32) for _ in range(4))
    for phase in range(4):
        lo, hi = phase_tiles(phase)
        def body(i, carry, phase=phase, lo=lo, hi=hi):
            t_term = TERMS - 1 - 8 * phase - 2 * i
            carry = adjoint(t_term, 0, 1, lo, hi, carry)
            return adjoint(t_term - 1, 1, 0, lo, hi, carry)
        grads = lax.fori_loop(0, 4, body, grads)
    for i in range(4):
        grad_out[pl.ds(i * 8, 8), :] = grads[i] * s
    for which in range(2):
        for v in range(4):
            for i in range(4):
                adj_out[which, v, pl.ds(i * 8, 8), :] = xc[which * 4 + v, pl.ds(HALO + i * 8, 8), :]


VMEM_SPEC = pl.BlockSpec(memory_space=pltpu.VMEM)
SMEM_SPEC = pl.BlockSpec(memory_space=pltpu.SMEM)
HBM_SPEC = pl.BlockSpec(memory_space=pltpu.HBM)


def params(mib):
    return pltpu.CompilerParams(vmem_limit_bytes=mib * 1024 * 1024)


def per_device(
    checkpoints,
    adjoints_in,
    vector_bits,
    potential_int,
    pot_scale,
    energies,
    residual,
    first_segment,
):
    core = lax.axis_index("vec") % 2
    coefs = window_coefs(first_segment, energies)
    coefs = jnp.where(core == 0, coefs, jnp.roll(coefs, HALF, axis=1))
    core = core[None]
    scale = 2.0 / (4.5 + QMAX * pot_scale)
    chk = checkpoints.reshape(FPLANES * ROWS, LANES)
    res = residual.reshape(2 * HALF * ROWS, LANES)
    send = jax.ShapeDtypeStruct((MAIN + FPLANES * FHALO, LANES), F32)
    own, to_above, chk, res_other = pl.pallas_call(
        prepare_kernel,
        out_shape=(
            send,
            send,
            jax.ShapeDtypeStruct((FPLANES * ROWS, LANES), F32),
            jax.ShapeDtypeStruct((HALF * ROWS, LANES), F32),
        ),
        in_specs=[SMEM_SPEC] * 2 + [HBM_SPEC] * 5,
        out_specs=(VMEM_SPEC,) * 4,
        scratch_shapes=[
            pltpu.VMEM((4 * ROWS, LANES), jnp.int32),
            pltpu.VMEM((ROWS, LANES), jnp.int32),
            pltpu.SemaphoreType.DMA((4 + 2 * (2 + FPLANES),)),
        ],
        compiler_params=params(4),
        name="prepare",
    )(
        core,
        pot_scale,
        *(
            pltpu.with_memory_space_constraint(value, pltpu.HBM)
            for value in (
                adjoints_in.reshape(8 * ROWS, LANES),
                vector_bits.reshape(4 * ROWS, LANES),
                potential_int,
                res,
                chk,
            )
        ),
    )

    def shift(value, axis, step):
        n = lax.axis_size(axis)
        return lax.ppermute(value, axis, [(i, (i + step) % n) for i in range(n)])

    def swap_cores(value):
        return lax.ppermute(value, "vec", [(0, 1), (1, 0), (2, 3), (3, 2)])

    above = shift(own, "row", 1)
    below = shift(to_above, "row", -1)

    def packed(kernel, rows, name, *values):
        shape = jax.ShapeDtypeStruct((rows, LANES), F32)
        to_left, to_right = pl.pallas_call(
            kernel,
            out_shape=(shape, shape),
            in_specs=[VMEM_SPEC] * len(values),
            out_specs=(VMEM_SPEC,) * 2,
            compiler_params=params(6),
            name=name,
        )(*values)
        return shift(to_left, "col", -1), shift(to_right, "col", 1)

    spread = (coefs[:, None, :, None] * jnp.eye(8, dtype=F32)[None, :, None, :]).reshape(
        8 * TERMS, 16 * HALF
    )
    rounded = lax.reduce_precision(spread, exponent_bits=8, mantissa_bits=7)
    high, low = rounded.astype(jnp.bfloat16), (spread - rounded).astype(jnp.bfloat16)
    coefs, high, low, late_own, late_chk = lax.optimization_barrier((coefs, high, low, own, chk))
    own_strips = packed(pack_own_kernel, OWN_ROWS, "pack_own", late_own, late_chk)
    edge_strips = packed(pack_edge_kernel, EDGE_ROWS, "pack_edge", above, below)
    weights = pl.pallas_call(
        weights_kernel,
        out_shape=jax.ShapeDtypeStruct((TERMS, ROWS, LANES), F32),
        in_specs=[SMEM_SPEC] + [VMEM_SPEC] * 2,
        out_specs=VMEM_SPEC,
        compiler_params=params(4),
        cost_estimate=pl.CostEstimate(flops=4_000_000, bytes_accessed=1_000_000, transcendentals=0),
        name="weights",
    )(coefs, late_own, res_other)

    weights, edge_strips = lax.optimization_barrier((weights, edge_strips))
    res_rows = slice(RES * ROWS, (RES + HALF) * ROWS)
    own_rows = slice(RES_GROUP * ROWS, GROUPS * ROWS)
    edge_rows = slice(RES_GROUP * 2 * HALO, GROUPS * 2 * HALO)
    swapped = swap_cores(
        jnp.concatenate(
            [
                own_strips[0][own_rows], edge_strips[0][edge_rows],
                own_strips[1][own_rows], edge_strips[1][edge_rows],
                above[res_rows], below[res_rows],
            ],
            axis=0,
        )
    )
    frame = (FPLANES, FEXT, LANES)
    states = pl.pallas_call(
        forward_kernel,
        out_shape=jax.ShapeDtypeStruct((TERMS, 4, ROWS, LANES), F32),
        in_specs=[SMEM_SPEC] + [VMEM_SPEC] * 8,
        out_specs=VMEM_SPEC,
        scratch_shapes=[
            pltpu.VMEM(frame, F32), pltpu.VMEM(frame, F32),
            pltpu.VMEM(frame[1:], F32), pltpu.VMEM(frame[1:], F32),
        ],
        compiler_params=params(8),
        cost_estimate=pl.CostEstimate(flops=20_000_000, bytes_accessed=6_000_000, transcendentals=0),
        name="forward",
    )(scale, own, chk, above, below, *own_strips, *edge_strips)

    ext = (EXT, LANES)
    adjoint_out, grad = pl.pallas_call(
        adjoint_kernel,
        out_shape=(
            jax.ShapeDtypeStruct((2, 4, ROWS, LANES), F32),
            jax.ShapeDtypeStruct((ROWS, LANES), F32),
        ),
        in_specs=[SMEM_SPEC] + [VMEM_SPEC] * 12,
        out_specs=(VMEM_SPEC, VMEM_SPEC),
        scratch_shapes=[
            pltpu.VMEM((8, *ext), F32), pltpu.VMEM((8, *ext), F32),
            pltpu.VMEM((4, *ext), F32), pltpu.VMEM((4, *ext), F32),
            pltpu.VMEM(ext, F32), pltpu.VMEM(ext, F32),
            pltpu.VMEM((TERMS, *ext), F32), pltpu.VMEM((TERMS, *ext), F32),
        ],
        compiler_params=params(10),
        name="adjoint",
    )(
        scale, high, low, own, above, below, *own_strips, *edge_strips, swapped, states, weights
    )

    grad = jnp.sum(lax.all_gather(grad, "vec"), axis=0)
    return grad, adjoint_out


def solution(mesh):
    return jax.shard_map(
        per_device,
        mesh=mesh,
        in_specs=(
            P(None, None, "vec", "row", "col"),
            P(None, "vec", "row", "col"),
            P("vec", "row", "col"),
            P("row", "col"),
            P(),
            P(),
            P(None, "row", "col"),
            P(),
        ),
        out_specs=(P("row", "col"), P(None, "vec", "row", "col")),
        check_vma=False,
    )
```

```python
import functools
import math

import jax
import jax.numpy as jnp
from jax import lax
from jax.experimental import pallas as pl
from jax.experimental.pallas import tpu as pltpu
from jax.sharding import PartitionSpec as P

SEG = 16
MOMENTS = 1024
QMAX = 32767
TERMS = 2 * SEG
NVEC = 16
F32 = jnp.float32

ADJ, SGN, RES, ONS = 0, 8, 12, 20
PLANES = 21
HALF = 8
ROWS = 32
HALO = 32
EXT = ROWS + 2 * HALO
FHALO = 16
FEXT = ROWS + 2 * FHALO
LANES = 128
FPLANES = 16
MAIN = PLANES * ROWS
WIDE = EXT // 8
GROUPS = 5
RES_GROUP = 3
OWN_ONS = GROUPS * ROWS
OWN_CHK = OWN_ONS + 8
OWN_ROWS = OWN_CHK + 2 * ROWS
EDGE_ONS = GROUPS * 2 * HALO
EDGE_CHK = EDGE_ONS + 16
EDGE_ROWS = EDGE_CHK + 4 * FHALO


def window_coefs(first_segment, energies):
    moment_order = first_segment[0] * SEG + jnp.arange(TERMS, dtype=jnp.int32)
    degree = moment_order.astype(jnp.float32)
    kernel_norm = float(MOMENTS + 1)
    angle_step = math.pi / kernel_norm
    jackson = (
        (kernel_norm - degree) * jnp.cos(angle_step * degree)
        + jnp.sin(angle_step * degree) * (math.cos(angle_step) / math.sin(angle_step))
    ) / kernel_norm
    factor = jnp.where(moment_order == 0, 1.0, 2.0).astype(jnp.float32)
    angles = jnp.arccos(energies)
    cosines = jnp.cos(degree[:, None] * angles[None, :])
    return (jackson * factor)[:, None] * cosines / (math.pi * jnp.sin(angles))[None, :]


def lane_iota():
    return lax.broadcasted_iota(jnp.int32, (8, LANES), 1)


def tile(ref, row):
    return ref[pl.ds(row, 8), :]


def main_tile(own, above, below, plane, t):
    section = (above, own, below)[t // 4]
    return tile(section, plane * ROWS + (t % 4) * 8)


def fwd_tile(chk, above, below, plane, t):
    if t < 2:
        return tile(above, MAIN + plane * FHALO + t * 8)
    if t < 6:
        return tile(chk, plane * ROWS + (t - 2) * 8)
    return tile(below, MAIN + plane * FHALO + (t - 6) * 8)


def prepare_kernel(
    core, scalar, adj, bits, pot, res, chk,
    to_below, to_above, chk_v, res_v, bits_v, pot_v, sems
):
    copies = []

    def start(src, dst):
        copy = pltpu.make_async_copy(src, dst, sems.at[len(copies)])
        copy.start()
        copies.append(copy)

    first_res = pl.multiple_of(core[0] * (HALF * ROWS), HALF * ROWS)
    start(bits, bits_v)
    start(pot, pot_v)
    for out, first in ((to_below, ROWS - FHALO), (to_above, 0)):
        start(adj, out.at[pl.ds(ADJ * ROWS, 8 * ROWS)])
        start(res.at[pl.ds(first_res, HALF * ROWS)], out.at[pl.ds(RES * ROWS, HALF * ROWS)])
        for plane in range(FPLANES):
            start(
                chk.at[pl.ds(plane * ROWS + first, FHALO)],
                out.at[pl.ds(MAIN + plane * FHALO, FHALO)],
            )
    start(chk, chk_v)
    start(res.at[pl.ds(pl.multiple_of(HALF * ROWS - first_res, HALF * ROWS), HALF * ROWS)], res_v)
    copies[0].wait()
    signs = (2 * bits_v[...] - 1).astype(F32) * (1.0 / NVEC)
    copies[1].wait()
    pot_factor = scalar[0]
    scale = 2.0 / (4.5 + QMAX * pot_factor)
    onsite = pot_v[...].astype(F32) * (pot_factor * scale)
    for out in (to_below, to_above):
        out[pl.ds(SGN * ROWS, 4 * ROWS), :] = signs
        out[pl.ds(ONS * ROWS, ROWS), :] = onsite
    for copy in copies[2:]:
        copy.wait()


def pack(tiles, row, to_left, to_right):
    lane = lane_iota()
    count = len(tiles)
    width = LANES // count
    group = lane // width
    left = right = None
    for j, value in enumerate(tiles):
        rolled = pltpu.roll(value, width * j, 1) if j else value
        left = rolled if j == 0 else jnp.where(group == j, rolled, left)
        right = rolled if j == 0 else jnp.where(group == (j + count - 1) % count, rolled, right)
    to_left[pl.ds(row, 8), :] = left
    to_right[pl.ds(row, 8), :] = right


def pack_own_kernel(own, chk, to_left, to_right):
    for g in range(GROUPS):
        for i in range(4):
            tiles = [tile(own, (4 * g + j) * ROWS + i * 8) for j in range(4)]
            pack(tiles, g * ROWS + i * 8, to_left, to_right)
    pack([tile(own, ONS * ROWS + j * 8) for j in range(4)], OWN_ONS, to_left, to_right)
    for g in range(2):
        for i in range(4):
            tiles = [tile(chk, (8 * g + j) * ROWS + i * 8) for j in range(8)]
            pack(tiles, OWN_CHK + g * ROWS + i * 8, to_left, to_right)


def pack_edge_kernel(above, below, to_left, to_right):
    for side, ref in enumerate((above, below)):
        for g in range(GROUPS):
            for i in range(4):
                tiles = [tile(ref, (4 * g + j) * ROWS + i * 8) for j in range(4)]
                pack(tiles, g * 2 * HALO + side * HALO + i * 8, to_left, to_right)
        tiles = [tile(ref, ONS * ROWS + j * 8) for j in range(4)]
        pack(tiles, EDGE_ONS + side * 8, to_left, to_right)
        for g in range(2):
            for i in range(2):
                tiles = [tile(ref, MAIN + (8 * g + j) * FHALO + i * 8) for j in range(8)]
                pack(tiles, EDGE_CHK + g * 2 * FHALO + side * FHALO + i * 8, to_left, to_right)


def unpack_strip(right, left, lane, j, count, turns=(0,)):
    width = LANES // count
    mixed = jnp.where(lane // width == j, tile(*right), tile(*left))
    shifts = [(LANES - width * j + turn * (LANES // 2)) % LANES for turn in turns]
    return [pltpu.roll(mixed, shift, 1) if shift else mixed for shift in shifts]


class Strips:
    def __init__(self, own_right, own_left, edge_right, edge_left, lane):
        self.own, self.edge, self.lane = (own_right, own_left), (edge_right, edge_left), lane

    def unpack(self, refs, row, j, count, turns):
        return unpack_strip((refs[0], row), (refs[1], row), self.lane, j, count, turns)

    def plane(self, index, t, turns=(0, 1)):
        g, j = index // 4, index % 4
        if 4 <= t < 8:
            return self.unpack(self.own, g * ROWS + (t - 4) * 8, j, 4, turns)
        return self.unpack(self.edge, g * 2 * HALO + (t if t < 4 else t - 4) * 8, j, 4, turns)

    def onsite(self, t, turns=(0, 1)):
        if 4 <= t < 8:
            return self.unpack(self.own, OWN_ONS, t - 4, 4, turns)
        return self.unpack(self.edge, EDGE_ONS + t // 8 * 8, t % 4, 4, turns)

    def checkpoint(self, plane, t, turns):
        g, j = plane // 8, plane % 8
        if 2 <= t < 6:
            return self.unpack(self.own, OWN_CHK + g * ROWS + (t - 2) * 8, j, 8, turns)
        at = EDGE_CHK + g * 2 * FHALO + (t if t < 2 else t - 4) * 8
        return self.unpack(self.edge, at, j, 8, turns)


SWAP_OWN, SWAP_EDGE = 2 * ROWS, 4 * HALO
SWAP_SIDE = SWAP_OWN + SWAP_EDGE
SWAP_MAIN = 2 * SWAP_SIDE


def swapped_strip(swapped, lane, e, t):
    g, j = e // 4, e % 4
    if 4 <= t < 8:
        row = g * ROWS + (t - 4) * 8
    else:
        row = SWAP_OWN + g * 2 * HALO + (t if t < 4 else t - 4) * 8
    return unpack_strip((swapped, row), (swapped, SWAP_SIDE + row), lane, j, 4, (0, 1))


def splats(coef, t_term):
    return [jnp.full((8, LANES), coef[t_term, e], F32) for e in range(2 * HALF)]


def weigh(factors, planes):
    terms = [value * factor for value, factor in zip(planes, factors)]
    while len(terms) > 1:
        terms = [x + y for x, y in zip(terms[::2], terms[1::2])]
    return terms[0]


def phase_tiles(phase):
    return phase, EXT // 8 - phase


def weights_kernel(coef, own, res_other, out):
    def body(t_term, carry):
        factors = splats(coef, t_term)
        for i in range(4):
            planes = [tile(own, (RES + e) * ROWS + i * 8) for e in range(HALF)]
            planes += [tile(res_other, e * ROWS + i * 8) for e in range(HALF)]
            value = weigh(factors, planes)
            out[0, t_term, pl.ds(i * 8, 8), :] = value
            out[1, t_term, pl.ds(i * 8, 8), :] = turned(value)
        return carry

    lax.fori_loop(0, TERMS, body, 0)


def weigh_stacks(high, low, stacks, out, out_turned, t):
    first = TERMS - 8 * (min(t, 3) + 1)
    rows = slice(8 * first, 8 * TERMS)
    stack = jnp.concatenate([jnp.concatenate(stack, axis=0) for stack in stacks], axis=1)
    upper = stack.astype(jnp.bfloat16)
    lower = (stack - upper.astype(F32)).astype(jnp.bfloat16)

    def product(x, y):
        return jnp.dot(x[rows, :], y, preferred_element_type=F32)

    result = product(high, upper) + (product(high, lower) + product(low, upper))
    for n in range(first, TERMS):
        part = result[8 * (n - first) : 8 * (n - first) + 8]
        for at, value in ((t * 8, part[:, :LANES]), (EXT - 8 - t * 8, part[:, LANES:])):
            out[n, pl.ds(at, 8), :] = value
            if out_turned is not None:
                out_turned[n, pl.ds(at, 8), :] = turned(value)


def turned(value):
    return pltpu.roll(value, LANES // 2, 1)


def maybe_turned(value, turn):
    return turned(value) if turn else value


def paired(first, second_turned, lane):
    inner = (lane >= HALO) & (lane < LANES - HALO)
    return jnp.where(inner, second_turned, first)


class Stencil:
    def __init__(self):
        lane, sub = lane_iota(), lax.broadcasted_iota(jnp.int32, (8, LANES), 0)
        self.lane = lane
        self.seam = {p: lane == p for p in (0, LANES // 2 - 1, LANES // 2, LANES - 1)}
        self.first_sub, self.last_sub = sub == 0, sub == 7

    def side(self, values, shift, at_a, at_b):
        a, b, h = (pltpu.roll(v, shift, 1) for v in values)
        seam_a, seam_b = self.seam[at_a], self.seam[at_b]
        return (
            jnp.where(seam_a, h, a),
            jnp.where(seam_b, h, b),
            jnp.where(seam_a, a, jnp.where(seam_b, b, h)),
        )

    def tiles(self, refs, lo, hi, count):
        def load(t):
            return [ref[pl.ds(t * 8, 8), :] for ref in refs]

        def rolled(values, shift):
            return [pltpu.roll(v, shift, 0) for v in values]

        half = LANES // 2
        here = load(lo)
        here_up, here_down = rolled(here, 1), rolled(here, 7)
        prev_up = rolled(load(lo - 1), 1) if lo > 0 else here_up
        for t in range(lo, hi):
            after = load(t + 1) if t + 1 < count else here
            after_up, after_down = rolled(after, 1), rolled(after, 7)
            left = self.side(here, 1, 0, half)
            right = self.side(here, LANES - 1, LANES - 1, half - 1)
            sums = [
                (left[m] + right[m])
                + (
                    jnp.where(self.first_sub, prev_up[m], here_up[m])
                    + jnp.where(self.last_sub, after_down[m], here_down[m])
                )
                for m in range(3)
            ]
            yield t, here, sums
            here, prev_up, here_up, here_down = after, here_up, after_up, after_down


def forward_kernel(
    scale, own, chk, above, below, own_right, own_left, edge_right, edge_left,
    vs, fc, fh, on,
):
    stencil = Stencil()
    lane = stencil.lane
    strips = Strips(own_right, own_left, edge_right, edge_left, lane)
    s = jnp.full((8, LANES), scale[0], F32)
    for t in range(FEXT // 8):
        row = pl.ds(t * 8, 8)
        for plane in range(FPLANES):
            value = maybe_turned(fwd_tile(chk, above, below, plane, t), plane % 2)
            fc[plane, row, :] = value
            if 2 <= t < 6:
                segment, which, v = plane // 8, plane // 4 % 2, plane % 4
                vs[segment * SEG + which, v, pl.ds((t - 2) * 8, 8), :] = value
            if plane % 2:
                fh[plane // 2, row, :] = paired(
                    *strips.checkpoint(plane - 1, t, (0,)), *strips.checkpoint(plane, t, (1,)), lane
                )
        e = t + (HALO - FHALO) // 8
        centre, edge = main_tile(own, above, below, ONS, e), strips.onsite(e)
        on[0, row, :] = centre
        on[1, row, :] = turned(centre)
        on[2, row, :] = paired(*edge, lane)

    def group(segment, which, pair):
        at = segment * 4 + which * 2 + pair
        return [fc.at[2 * at], fc.at[2 * at + 1], fh.at[at]]

    def forward(k, new, old, lo, hi):
        for segment in range(2):
            for pair in range(2):
                target = group(segment, old, pair)
                for t, values, sums in stencil.tiles(group(segment, new, pair), lo, hi, FEXT // 8):
                    row = pl.ds(t * 8, 8)
                    for m in range(3):
                        value = on[m, row, :] * values[m] - s * sums[m] - target[m][row, :]
                        target[m][row, :] = value
                        if m < 2 and 2 <= t < 6:
                            vs[segment * SEG + k, 2 * pair + m, pl.ds((t - 2) * 8, 8), :] = value

    for start, stop, lo, hi in ((1, 4, 0, 8), (4, 8, 1, 7)):
        def body(i, carry, lo=lo, hi=hi):
            forward(2 * i, 1, 0, lo, hi)
            forward(2 * i + 1, 0, 1, lo, hi)
            return carry
        lax.fori_loop(start, stop, body, 0)


def adjoint_kernel(
    scale, high, low, own, above, below, own_right, own_left, edge_right, edge_left, swapped,
    vs, own_weights,
    adj_out, grad_out,
    xc, xh, sg, on, wcs, wts, whs,
):
    stencil = Stencil()
    lane = stencil.lane
    strips = Strips(own_right, own_left, edge_right, edge_left, lane)
    s = jnp.full((8, LANES), scale[0], F32)

    for t in range(EXT // 8):
        row = pl.ds(t * 8, 8)
        for plane in range(8):
            xc[plane, row, :] = maybe_turned(main_tile(own, above, below, plane, t), plane % 2)
        for at in range(4):
            xh[at, row, :] = paired(
                *strips.plane(2 * at, t, (0,)), *strips.plane(2 * at + 1, t, (1,)), lane
            )
        for pair in range(2):
            first = SGN + 2 * pair
            for m in range(2):
                sg[3 * pair + m, row, :] = maybe_turned(
                    main_tile(own, above, below, first + m, t), m
                )
            sg[3 * pair + 2, row, :] = paired(
                *strips.plane(first, t, (0,)), *strips.plane(first + 1, t, (1,)), lane
            )
        centre, edge = main_tile(own, above, below, ONS, t), strips.onsite(t)
        on[0, row, :] = centre
        on[1, row, :] = turned(centre)
        on[2, row, :] = paired(*edge, lane)

    def halo_stack(t):
        values = [strips.plane(RES + e, t) for e in range(HALF)]
        values += [swapped_strip(swapped, lane, e, t) for e in range(HALF)]
        return [paired(*value, lane) for value in values]

    def centre_stack(t):
        at = SWAP_MAIN + t * 8 + (0 if t < 4 else (HALF - 2) * ROWS)
        return [main_tile(own, above, below, RES + e, t) for e in range(HALF)] + [
            tile(swapped, at + e * ROWS) for e in range(HALF)
        ]

    for t in range(EXT // 16):
        other = EXT // 8 - 1 - t
        weigh_stacks(high, low, (halo_stack(t), halo_stack(other)), whs, None, t)
        if t < 4:
            weigh_stacks(high, low, (centre_stack(t), centre_stack(other)), wcs, wts, t)

    def group(which, pair):
        at = which * 2 + pair
        return [xc.at[2 * at], xc.at[2 * at + 1], xh.at[at]]

    def weights_of(t_term, t):
        row = pl.ds(t * 8, 8)
        if 4 <= t < 8:
            local = pl.ds((t - 4) * 8, 8)
            centre = [own_weights[m, t_term, local, :] for m in range(2)]
        else:
            centre = [wcs[t_term, row, :], wts[t_term, row, :]]
        return centre + [whs[t_term, row, :]]

    def adjoint(t_term, new, old, lo, hi, grads):
        grads = list(grads)
        for pair in range(2):
            target = group(old, pair)
            for t, values, sums in stencil.tiles(group(new, pair), lo, hi, EXT // 8):
                row = pl.ds(t * 8, 8)
                if 4 <= t < 8:
                    for m in range(2):
                        at = 4 * m + t - 4
                        state = vs[t_term, 2 * pair + m, pl.ds((t - 4) * 8, 8), :]
                        grads[at] = grads[at] + values[m] * state
                weights = weights_of(t_term, t)
                for m in range(3):
                    target[m][row, :] = (
                        weights[m] * sg[3 * pair + m, row, :]
                        + (on[m, row, :] * values[m] - s * sums[m])
                        - target[m][row, :]
                    )
        return tuple(grads)

    grads = tuple(jnp.zeros((8, LANES), F32) for _ in range(8))
    for phase in range(4):
        lo, hi = phase_tiles(phase)
        def body(i, carry, phase=phase, lo=lo, hi=hi):
            t_term = TERMS - 1 - 8 * phase - 2 * i
            carry = adjoint(t_term, 0, 1, lo, hi, carry)
            return adjoint(t_term - 1, 1, 0, lo, hi, carry)
        grads = lax.fori_loop(0, 4, body, grads)
    for i in range(4):
        grad_out[pl.ds(i * 8, 8), :] = (grads[i] + turned(grads[4 + i])) * s
    for which in range(2):
        for v in range(4):
            for i in range(4):
                value = xc[which * 4 + v, pl.ds(HALO + i * 8, 8), :]
                adj_out[which, v, pl.ds(i * 8, 8), :] = maybe_turned(value, v % 2)


VMEM_SPEC = pl.BlockSpec(memory_space=pltpu.VMEM)
SMEM_SPEC = pl.BlockSpec(memory_space=pltpu.SMEM)
HBM_SPEC = pl.BlockSpec(memory_space=pltpu.HBM)


def params(mib):
    return pltpu.CompilerParams(vmem_limit_bytes=mib * 1024 * 1024)


def per_device(
    checkpoints,
    adjoints_in,
    vector_bits,
    potential_int,
    pot_scale,
    energies,
    residual,
    first_segment,
):
    core = lax.axis_index("vec") % 2
    coefs = window_coefs(first_segment, energies)
    coefs = jnp.where(core == 0, coefs, jnp.roll(coefs, HALF, axis=1))
    core = core[None]
    scale = 2.0 / (4.5 + QMAX * pot_scale)
    chk = checkpoints.reshape(FPLANES * ROWS, LANES)
    res = residual.reshape(2 * HALF * ROWS, LANES)
    send = jax.ShapeDtypeStruct((MAIN + FPLANES * FHALO, LANES), F32)
    own, to_above, chk, res_other = pl.pallas_call(
        prepare_kernel,
        out_shape=(
            send,
            send,
            jax.ShapeDtypeStruct((FPLANES * ROWS, LANES), F32),
            jax.ShapeDtypeStruct((HALF * ROWS, LANES), F32),
        ),
        in_specs=[SMEM_SPEC] * 2 + [HBM_SPEC] * 5,
        out_specs=(VMEM_SPEC,) * 4,
        scratch_shapes=[
            pltpu.VMEM((4 * ROWS, LANES), jnp.int32),
            pltpu.VMEM((ROWS, LANES), jnp.int32),
            pltpu.SemaphoreType.DMA((4 + 2 * (2 + FPLANES),)),
        ],
        compiler_params=params(4),
        name="prepare",
    )(
        core,
        pot_scale,
        *(
            pltpu.with_memory_space_constraint(value, pltpu.HBM)
            for value in (
                adjoints_in.reshape(8 * ROWS, LANES),
                vector_bits.reshape(4 * ROWS, LANES),
                potential_int,
                res,
                chk,
            )
        ),
    )

    def shift(value, axis, step):
        n = lax.axis_size(axis)
        return lax.ppermute(value, axis, [(i, (i + step) % n) for i in range(n)])

    def swap_cores(value):
        return lax.ppermute(value, "vec", [(0, 1), (1, 0), (2, 3), (3, 2)])

    above = shift(own, "row", 1)
    below = shift(to_above, "row", -1)

    def packed(kernel, rows, name, *values):
        shape = jax.ShapeDtypeStruct((rows, LANES), F32)
        to_left, to_right = pl.pallas_call(
            kernel,
            out_shape=(shape, shape),
            in_specs=[VMEM_SPEC] * len(values),
            out_specs=(VMEM_SPEC,) * 2,
            compiler_params=params(6),
            name=name,
        )(*values)
        return shift(to_left, "col", -1), shift(to_right, "col", 1)

    spread = (coefs[:, None, :, None] * jnp.eye(8, dtype=F32)[None, :, None, :]).reshape(
        8 * TERMS, 16 * HALF
    )
    rounded = lax.reduce_precision(spread, exponent_bits=8, mantissa_bits=7)
    high, low = rounded.astype(jnp.bfloat16), (spread - rounded).astype(jnp.bfloat16)
    coefs, high, low, late_own, late_chk = lax.optimization_barrier((coefs, high, low, own, chk))
    own_strips = packed(pack_own_kernel, OWN_ROWS, "pack_own", late_own, late_chk)
    edge_strips = packed(pack_edge_kernel, EDGE_ROWS, "pack_edge", above, below)
    weights = pl.pallas_call(
        weights_kernel,
        out_shape=jax.ShapeDtypeStruct((2, TERMS, ROWS, LANES), F32),
        in_specs=[SMEM_SPEC] + [VMEM_SPEC] * 2,
        out_specs=VMEM_SPEC,
        compiler_params=params(4),
        cost_estimate=pl.CostEstimate(flops=4_000_000, bytes_accessed=1_000_000, transcendentals=0),
        name="weights",
    )(coefs, late_own, res_other)

    weights, edge_strips = lax.optimization_barrier((weights, edge_strips))
    res_rows = slice(RES * ROWS, (RES + HALF) * ROWS)
    own_rows = slice(RES_GROUP * ROWS, GROUPS * ROWS)
    edge_rows = slice(RES_GROUP * 2 * HALO, GROUPS * 2 * HALO)
    swapped = swap_cores(
        jnp.concatenate(
            [
                own_strips[0][own_rows], edge_strips[0][edge_rows],
                own_strips[1][own_rows], edge_strips[1][edge_rows],
                above[res_rows], below[res_rows],
            ],
            axis=0,
        )
    )
    frame = (FPLANES, FEXT, LANES)
    states = pl.pallas_call(
        forward_kernel,
        out_shape=jax.ShapeDtypeStruct((TERMS, 4, ROWS, LANES), F32),
        in_specs=[SMEM_SPEC] + [VMEM_SPEC] * 8,
        out_specs=VMEM_SPEC,
        scratch_shapes=[
            pltpu.VMEM(frame, F32), pltpu.VMEM((FPLANES // 2, *frame[1:]), F32),
            pltpu.VMEM((3, *frame[1:]), F32),
        ],
        compiler_params=params(8),
        cost_estimate=pl.CostEstimate(flops=20_000_000, bytes_accessed=6_000_000, transcendentals=0),
        name="forward",
    )(scale, own, chk, above, below, *own_strips, *edge_strips)

    ext = (EXT, LANES)
    adjoint_out, grad = pl.pallas_call(
        adjoint_kernel,
        out_shape=(
            jax.ShapeDtypeStruct((2, 4, ROWS, LANES), F32),
            jax.ShapeDtypeStruct((ROWS, LANES), F32),
        ),
        in_specs=[SMEM_SPEC] + [VMEM_SPEC] * 12,
        out_specs=(VMEM_SPEC, VMEM_SPEC),
        scratch_shapes=[
            pltpu.VMEM((8, *ext), F32), pltpu.VMEM((4, *ext), F32),
            pltpu.VMEM((6, *ext), F32), pltpu.VMEM((3, *ext), F32),
            pltpu.VMEM((TERMS, *ext), F32), pltpu.VMEM((TERMS, *ext), F32),
            pltpu.VMEM((TERMS, *ext), F32),
        ],
        compiler_params=params(12),
        name="adjoint",
    )(
        scale, high, low, own, above, below, *own_strips, *edge_strips, swapped, states, weights
    )

    grad = jnp.sum(lax.all_gather(grad, "vec"), axis=0)
    return grad, adjoint_out


def solution(mesh):
    return jax.shard_map(
        per_device,
        mesh=mesh,
        in_specs=(
            P(None, None, "vec", "row", "col"),
            P(None, "vec", "row", "col"),
            P("vec", "row", "col"),
            P("row", "col"),
            P(),
            P(),
            P(None, "row", "col"),
            P(),
        ),
        out_specs=(P("row", "col"), P(None, "vec", "row", "col")),
        check_vma=False,
    )
```

```python
import functools
import math

import jax
import jax.numpy as jnp
from jax import lax
from jax.experimental import pallas as pl
from jax.experimental.pallas import tpu as pltpu
from jax.sharding import PartitionSpec as P

SEG = 16
MOMENTS = 1024
QMAX = 32767
TERMS = 2 * SEG
NVEC = 16
F32 = jnp.float32

ADJ, SGN, RES, ONS = 0, 8, 12, 20
PLANES = 21
HALF = 8
ROWS = 32
HALO = 32
EXT = ROWS + 2 * HALO
FHALO = 16
FEXT = ROWS + 2 * FHALO
LANES = 128
FPLANES = 16
MAIN = PLANES * ROWS
WIDE = EXT // 8
GROUPS = 5
RES_GROUP = 3
OWN_ONS = GROUPS * ROWS
OWN_CHK = OWN_ONS + 8
OWN_ROWS = OWN_CHK + 2 * ROWS
EDGE_FAR = GROUPS * HALO
FAR_GROUPS = ((ADJ, 8), (RES, 8), (SGN, 4))
EDGE_ONS = EDGE_FAR + len(FAR_GROUPS) * HALO
EDGE_CHK = EDGE_ONS + 8
EDGE_ROWS = EDGE_CHK + 4 * FHALO


def near_index(t):
    return t - 2 if t < 4 else t - 6


def far_index(t):
    return t if t < 2 else t - 8


def window_coefs(first_segment, energies):
    moment_order = first_segment[0] * SEG + jnp.arange(TERMS, dtype=jnp.int32)
    degree = moment_order.astype(jnp.float32)
    kernel_norm = float(MOMENTS + 1)
    angle_step = math.pi / kernel_norm
    jackson = (
        (kernel_norm - degree) * jnp.cos(angle_step * degree)
        + jnp.sin(angle_step * degree) * (math.cos(angle_step) / math.sin(angle_step))
    ) / kernel_norm
    factor = jnp.where(moment_order == 0, 1.0, 2.0).astype(jnp.float32)
    angles = jnp.arccos(energies)
    cosines = jnp.cos(degree[:, None] * angles[None, :])
    return (jackson * factor)[:, None] * cosines / (math.pi * jnp.sin(angles))[None, :]


def lane_iota():
    return lax.broadcasted_iota(jnp.int32, (8, LANES), 1)


def tile(ref, row):
    return ref[pl.ds(row, 8), :]


def main_tile(own, above, below, plane, t):
    section = (above, own, below)[t // 4]
    return tile(section, plane * ROWS + (t % 4) * 8)


def fwd_tile(chk, above, below, plane, t):
    if t < 2:
        return tile(above, MAIN + plane * FHALO + t * 8)
    if t < 6:
        return tile(chk, plane * ROWS + (t - 2) * 8)
    return tile(below, MAIN + plane * FHALO + (t - 6) * 8)


def prepare_kernel(
    core, scalar, adj, bits, pot, res, chk,
    to_below, to_above, chk_v, res_v, bits_v, pot_v, sems
):
    copies = []

    def start(src, dst):
        copy = pltpu.make_async_copy(src, dst, sems.at[len(copies)])
        copy.start()
        copies.append(copy)

    first_res = pl.multiple_of(core[0] * (HALF * ROWS), HALF * ROWS)
    start(bits, bits_v)
    start(pot, pot_v)
    for out, first in ((to_below, ROWS - FHALO), (to_above, 0)):
        start(adj, out.at[pl.ds(ADJ * ROWS, 8 * ROWS)])
        start(res.at[pl.ds(first_res, HALF * ROWS)], out.at[pl.ds(RES * ROWS, HALF * ROWS)])
        for plane in range(FPLANES):
            start(
                chk.at[pl.ds(plane * ROWS + first, FHALO)],
                out.at[pl.ds(MAIN + plane * FHALO, FHALO)],
            )
    start(chk, chk_v)
    start(res.at[pl.ds(pl.multiple_of(HALF * ROWS - first_res, HALF * ROWS), HALF * ROWS)], res_v)
    copies[0].wait()
    signs = (2 * bits_v[...] - 1).astype(F32) * (1.0 / NVEC)
    copies[1].wait()
    pot_factor = scalar[0]
    scale = 2.0 / (4.5 + QMAX * pot_factor)
    onsite = pot_v[...].astype(F32) * (pot_factor * scale)
    for out in (to_below, to_above):
        out[pl.ds(SGN * ROWS, 4 * ROWS), :] = signs
        out[pl.ds(ONS * ROWS, ROWS), :] = onsite
    for copy in copies[2:]:
        copy.wait()


def pack(tiles, row, to_left, to_right):
    lane = lane_iota()
    count = len(tiles)
    width = LANES // count
    group = lane // width
    left = right = None
    for j, value in enumerate(tiles):
        rolled = pltpu.roll(value, width * j, 1) if j else value
        left = rolled if j == 0 else jnp.where(group == j, rolled, left)
        right = rolled if j == 0 else jnp.where(group == (j + count - 1) % count, rolled, right)
    to_left[pl.ds(row, 8), :] = left
    to_right[pl.ds(row, 8), :] = right


def pack_own_kernel(own, chk, to_left, to_right):
    for g in range(GROUPS):
        for i in range(4):
            tiles = [tile(own, (4 * g + j) * ROWS + i * 8) for j in range(4)]
            pack(tiles, g * ROWS + i * 8, to_left, to_right)
    pack([tile(own, ONS * ROWS + j * 8) for j in range(4)], OWN_ONS, to_left, to_right)
    for g in range(2):
        for i in range(4):
            tiles = [tile(chk, (8 * g + j) * ROWS + i * 8) for j in range(8)]
            pack(tiles, OWN_CHK + g * ROWS + i * 8, to_left, to_right)


def pack_edge_kernel(above, below, to_left, to_right):
    def at(plane, t):
        return main_tile(None, above, below, plane, t)

    near, far = (2, 3, 8, 9), (0, 1, 10, 11)
    for t in near:
        for g in range(GROUPS):
            tiles = [at(4 * g + j, t) for j in range(4)]
            pack(tiles, g * HALO + near_index(t) * 8, to_left, to_right)
    for t in far:
        for g, (first, count) in enumerate(FAR_GROUPS):
            tiles = [at(first + j, t) for j in range(count)]
            tiles += [at(ONS, t)] * (8 - count)
            pack(tiles, EDGE_FAR + g * HALO + far_index(t) * 8, to_left, to_right)
    pack([at(ONS, t) for t in near], EDGE_ONS, to_left, to_right)
    for side, ref in enumerate((above, below)):
        for g in range(2):
            for i in range(2):
                tiles = [tile(ref, MAIN + (8 * g + j) * FHALO + i * 8) for j in range(8)]
                pack(tiles, EDGE_CHK + g * 2 * FHALO + side * FHALO + i * 8, to_left, to_right)


def unpack_strip(right, left, lane, j, count, turns=(0,)):
    width = LANES // count
    mixed = jnp.where(lane // width == j, tile(*right), tile(*left))
    shifts = [(LANES - width * j + turn * (LANES // 2)) % LANES for turn in turns]
    return [pltpu.roll(mixed, shift, 1) if shift else mixed for shift in shifts]


class Strips:
    def __init__(self, own_right, own_left, edge_right, edge_left, lane):
        self.own, self.edge, self.lane = (own_right, own_left), (edge_right, edge_left), lane

    def unpack(self, refs, row, j, count, turns):
        return unpack_strip((refs[0], row), (refs[1], row), self.lane, j, count, turns)

    def plane(self, index, t, turns=(0, 1)):
        g, j = index // 4, index % 4
        if 4 <= t < 8:
            return self.unpack(self.own, g * ROWS + (t - 4) * 8, j, 4, turns)
        if 2 <= t < 10:
            return self.unpack(self.edge, g * HALO + near_index(t) * 8, j, 4, turns)
        for g, (first, count) in enumerate(FAR_GROUPS):
            if first <= index < first + count:
                row = EDGE_FAR + g * HALO + far_index(t) * 8
                return self.unpack(self.edge, row, index - first, 8, turns)

    def onsite(self, t, turns=(0, 1)):
        if 4 <= t < 8:
            return self.unpack(self.own, OWN_ONS, t - 4, 4, turns)
        if 2 <= t < 10:
            return self.unpack(self.edge, EDGE_ONS, near_index(t), 4, turns)
        return self.unpack(self.edge, EDGE_FAR + 2 * HALO + far_index(t) * 8, 4, 8, turns)

    def checkpoint(self, plane, t, turns):
        g, j = plane // 8, plane % 8
        if 2 <= t < 6:
            return self.unpack(self.own, OWN_CHK + g * ROWS + (t - 2) * 8, j, 8, turns)
        at = EDGE_CHK + g * 2 * FHALO + (t if t < 2 else t - 4) * 8
        return self.unpack(self.edge, at, j, 8, turns)


SWAP_NEAR, SWAP_FAR = 2 * ROWS, 2 * ROWS + 2 * HALO
SWAP_SIDE = SWAP_FAR + HALO
SWAP_MAIN = 2 * SWAP_SIDE


def swapped_strip(swapped, lane, e, t):
    g, j, count = e // 4, e % 4, 4
    if 4 <= t < 8:
        row = g * ROWS + (t - 4) * 8
    elif 2 <= t < 10:
        row = SWAP_NEAR + g * HALO + near_index(t) * 8
    else:
        row, j, count = SWAP_FAR + far_index(t) * 8, e, 8
    return unpack_strip((swapped, row), (swapped, SWAP_SIDE + row), lane, j, count, (0, 1))


def splats(coef, t_term):
    return [jnp.full((8, LANES), coef[t_term, e], F32) for e in range(2 * HALF)]


def weigh(factors, planes):
    terms = [value * factor for value, factor in zip(planes, factors)]
    while len(terms) > 1:
        terms = [x + y for x, y in zip(terms[::2], terms[1::2])]
    return terms[0]


def phase_tiles(phase):
    return phase, EXT // 8 - phase


def weights_kernel(coef, own, res_other, out):
    def body(t_term, carry):
        factors = splats(coef, t_term)
        for i in range(4):
            planes = [tile(own, (RES + e) * ROWS + i * 8) for e in range(HALF)]
            planes += [tile(res_other, e * ROWS + i * 8) for e in range(HALF)]
            value = weigh(factors, planes)
            out[0, t_term, pl.ds(i * 8, 8), :] = value
            out[1, t_term, pl.ds(i * 8, 8), :] = turned(value)
        return carry

    lax.fori_loop(0, TERMS, body, 0)


def weigh_stacks(high, low, stacks, out, out_turned, t):
    first = TERMS - 8 * (min(t, 3) + 1)
    rows = slice(8 * first, 8 * TERMS)
    stack = jnp.concatenate([jnp.concatenate(stack, axis=0) for stack in stacks], axis=1)
    upper = stack.astype(jnp.bfloat16)
    lower = (stack - upper.astype(F32)).astype(jnp.bfloat16)

    def product(x, y):
        return jnp.dot(x[rows, :], y, preferred_element_type=F32)

    result = product(high, upper) + (product(high, lower) + product(low, upper))
    for n in range(first, TERMS):
        part = result[8 * (n - first) : 8 * (n - first) + 8]
        for at, value in ((t * 8, part[:, :LANES]), (EXT - 8 - t * 8, part[:, LANES:])):
            out[n, pl.ds(at, 8), :] = value
            if out_turned is not None:
                out_turned[n, pl.ds(at, 8), :] = turned(value)


def turned(value):
    return pltpu.roll(value, LANES // 2, 1)


def maybe_turned(value, turn):
    return turned(value) if turn else value


def paired(first, second_turned, lane):
    inner = (lane >= HALO) & (lane < LANES - HALO)
    return jnp.where(inner, second_turned, first)


class Stencil:
    def __init__(self):
        lane, sub = lane_iota(), lax.broadcasted_iota(jnp.int32, (8, LANES), 0)
        self.lane = lane
        self.seam = {p: lane == p for p in (0, LANES // 2 - 1, LANES // 2, LANES - 1)}
        self.first_sub, self.last_sub = sub == 0, sub == 7

    def side(self, values, shift, at_a, at_b):
        a, b, h = (pltpu.roll(v, shift, 1) for v in values)
        seam_a, seam_b = self.seam[at_a], self.seam[at_b]
        return (
            jnp.where(seam_a, h, a),
            jnp.where(seam_b, h, b),
            jnp.where(seam_a, a, jnp.where(seam_b, b, h)),
        )

    def tiles(self, refs, lo, hi, count):
        def load(t):
            return [ref[pl.ds(t * 8, 8), :] for ref in refs]

        def rolled(values, shift):
            return [pltpu.roll(v, shift, 0) for v in values]

        half = LANES // 2
        here = load(lo)
        here_up, here_down = rolled(here, 1), rolled(here, 7)
        prev_up = rolled(load(lo - 1), 1) if lo > 0 else here_up
        for t in range(lo, hi):
            after = load(t + 1) if t + 1 < count else here
            after_up, after_down = rolled(after, 1), rolled(after, 7)
            left = self.side(here, 1, 0, half)
            right = self.side(here, LANES - 1, LANES - 1, half - 1)
            sums = [
                (left[m] + right[m])
                + (
                    jnp.where(self.first_sub, prev_up[m], here_up[m])
                    + jnp.where(self.last_sub, after_down[m], here_down[m])
                )
                for m in range(3)
            ]
            yield t, here, sums
            here, prev_up, here_up, here_down = after, here_up, after_up, after_down


def forward_kernel(
    scale, own, chk, above, below, own_right, own_left, edge_right, edge_left,
    vs, fc, fh, on,
):
    stencil = Stencil()
    lane = stencil.lane
    strips = Strips(own_right, own_left, edge_right, edge_left, lane)
    s = jnp.full((8, LANES), scale[0], F32)
    for t in range(FEXT // 8):
        row = pl.ds(t * 8, 8)
        for plane in range(FPLANES):
            value = maybe_turned(fwd_tile(chk, above, below, plane, t), plane % 2)
            fc[plane, row, :] = value
            if 2 <= t < 6:
                segment, which, v = plane // 8, plane // 4 % 2, plane % 4
                vs[segment * SEG + which, v, pl.ds((t - 2) * 8, 8), :] = value
            if plane % 2:
                fh[plane // 2, row, :] = paired(
                    *strips.checkpoint(plane - 1, t, (0,)), *strips.checkpoint(plane, t, (1,)), lane
                )
        e = t + (HALO - FHALO) // 8
        centre, edge = main_tile(own, above, below, ONS, e), strips.onsite(e)
        on[0, row, :] = centre
        on[1, row, :] = turned(centre)
        on[2, row, :] = paired(*edge, lane)

    def group(segment, which, pair):
        at = segment * 4 + which * 2 + pair
        return [fc.at[2 * at], fc.at[2 * at + 1], fh.at[at]]

    def forward(k, new, old, lo, hi):
        for segment in range(2):
            for pair in range(2):
                target = group(segment, old, pair)
                for t, values, sums in stencil.tiles(group(segment, new, pair), lo, hi, FEXT // 8):
                    row = pl.ds(t * 8, 8)
                    for m in range(3):
                        value = on[m, row, :] * values[m] - s * sums[m] - target[m][row, :]
                        target[m][row, :] = value
                        if m < 2 and 2 <= t < 6:
                            vs[segment * SEG + k, 2 * pair + m, pl.ds((t - 2) * 8, 8), :] = value

    for start, stop, lo, hi in ((1, 4, 0, 8), (4, 8, 1, 7)):
        def body(i, carry, lo=lo, hi=hi):
            forward(2 * i, 1, 0, lo, hi)
            forward(2 * i + 1, 0, 1, lo, hi)
            return carry
        lax.fori_loop(start, stop, body, 0)


def adjoint_kernel(
    scale, high, low, own, above, below, own_right, own_left, edge_right, edge_left, swapped,
    vs, own_weights,
    adj_out, grad_out,
    xc, xh, sg, on, wcs, wts, whs,
):
    stencil = Stencil()
    lane = stencil.lane
    strips = Strips(own_right, own_left, edge_right, edge_left, lane)
    s = jnp.full((8, LANES), scale[0], F32)

    for t in range(EXT // 8):
        row = pl.ds(t * 8, 8)
        for plane in range(8):
            xc[plane, row, :] = maybe_turned(main_tile(own, above, below, plane, t), plane % 2)
        for at in range(4):
            xh[at, row, :] = paired(
                *strips.plane(2 * at, t, (0,)), *strips.plane(2 * at + 1, t, (1,)), lane
            )
        for pair in range(2):
            first = SGN + 2 * pair
            for m in range(2):
                sg[3 * pair + m, row, :] = maybe_turned(
                    main_tile(own, above, below, first + m, t), m
                )
            sg[3 * pair + 2, row, :] = paired(
                *strips.plane(first, t, (0,)), *strips.plane(first + 1, t, (1,)), lane
            )
        centre, edge = main_tile(own, above, below, ONS, t), strips.onsite(t)
        on[0, row, :] = centre
        on[1, row, :] = turned(centre)
        on[2, row, :] = paired(*edge, lane)

    def halo_stack(t):
        values = [strips.plane(RES + e, t) for e in range(HALF)]
        values += [swapped_strip(swapped, lane, e, t) for e in range(HALF)]
        return [paired(*value, lane) for value in values]

    def centre_stack(t):
        at = SWAP_MAIN + t * 8 + (0 if t < 4 else (HALF - 2) * ROWS)
        return [main_tile(own, above, below, RES + e, t) for e in range(HALF)] + [
            tile(swapped, at + e * ROWS) for e in range(HALF)
        ]

    for t in range(EXT // 16):
        other = EXT // 8 - 1 - t
        weigh_stacks(high, low, (halo_stack(t), halo_stack(other)), whs, None, t)
        if t < 4:
            weigh_stacks(high, low, (centre_stack(t), centre_stack(other)), wcs, wts, t)

    def group(which, pair):
        at = which * 2 + pair
        return [xc.at[2 * at], xc.at[2 * at + 1], xh.at[at]]

    def weights_of(t_term, t):
        row = pl.ds(t * 8, 8)
        if 4 <= t < 8:
            local = pl.ds((t - 4) * 8, 8)
            centre = [own_weights[m, t_term, local, :] for m in range(2)]
        else:
            centre = [wcs[t_term, row, :], wts[t_term, row, :]]
        return centre + [whs[t_term, row, :]]

    def adjoint(t_term, new, old, lo, hi, grads):
        grads = list(grads)
        for pair in range(2):
            target = group(old, pair)
            for t, values, sums in stencil.tiles(group(new, pair), lo, hi, EXT // 8):
                row = pl.ds(t * 8, 8)
                if 4 <= t < 8:
                    for m in range(2):
                        at = 4 * m + t - 4
                        state = vs[t_term, 2 * pair + m, pl.ds((t - 4) * 8, 8), :]
                        grads[at] = grads[at] + values[m] * state
                weights = weights_of(t_term, t)
                for m in range(3):
                    target[m][row, :] = (
                        weights[m] * sg[3 * pair + m, row, :]
                        + (on[m, row, :] * values[m] - s * sums[m])
                        - target[m][row, :]
                    )
        return tuple(grads)

    grads = tuple(jnp.zeros((8, LANES), F32) for _ in range(8))
    for phase in range(4):
        lo, hi = phase_tiles(phase)
        def body(i, carry, phase=phase, lo=lo, hi=hi):
            t_term = TERMS - 1 - 8 * phase - 2 * i
            carry = adjoint(t_term, 0, 1, lo, hi, carry)
            return adjoint(t_term - 1, 1, 0, lo, hi, carry)
        grads = lax.fori_loop(0, 4, body, grads)
    for i in range(4):
        grad_out[pl.ds(i * 8, 8), :] = (grads[i] + turned(grads[4 + i])) * s
    for which in range(2):
        for v in range(4):
            for i in range(4):
                value = xc[which * 4 + v, pl.ds(HALO + i * 8, 8), :]
                adj_out[which, v, pl.ds(i * 8, 8), :] = maybe_turned(value, v % 2)


VMEM_SPEC = pl.BlockSpec(memory_space=pltpu.VMEM)
SMEM_SPEC = pl.BlockSpec(memory_space=pltpu.SMEM)
HBM_SPEC = pl.BlockSpec(memory_space=pltpu.HBM)


def params(mib):
    return pltpu.CompilerParams(vmem_limit_bytes=mib * 1024 * 1024)


def per_device(
    checkpoints,
    adjoints_in,
    vector_bits,
    potential_int,
    pot_scale,
    energies,
    residual,
    first_segment,
):
    core = lax.axis_index("vec") % 2
    coefs = window_coefs(first_segment, energies)
    coefs = jnp.where(core == 0, coefs, jnp.roll(coefs, HALF, axis=1))
    core = core[None]
    scale = 2.0 / (4.5 + QMAX * pot_scale)
    chk = checkpoints.reshape(FPLANES * ROWS, LANES)
    res = residual.reshape(2 * HALF * ROWS, LANES)
    send = jax.ShapeDtypeStruct((MAIN + FPLANES * FHALO, LANES), F32)
    own, to_above, chk, res_other = pl.pallas_call(
        prepare_kernel,
        out_shape=(
            send,
            send,
            jax.ShapeDtypeStruct((FPLANES * ROWS, LANES), F32),
            jax.ShapeDtypeStruct((HALF * ROWS, LANES), F32),
        ),
        in_specs=[SMEM_SPEC] * 2 + [HBM_SPEC] * 5,
        out_specs=(VMEM_SPEC,) * 4,
        scratch_shapes=[
            pltpu.VMEM((4 * ROWS, LANES), jnp.int32),
            pltpu.VMEM((ROWS, LANES), jnp.int32),
            pltpu.SemaphoreType.DMA((4 + 2 * (2 + FPLANES),)),
        ],
        compiler_params=params(4),
        name="prepare",
    )(
        core,
        pot_scale,
        *(
            pltpu.with_memory_space_constraint(value, pltpu.HBM)
            for value in (
                adjoints_in.reshape(8 * ROWS, LANES),
                vector_bits.reshape(4 * ROWS, LANES),
                potential_int,
                res,
                chk,
            )
        ),
    )

    def shift(value, axis, step):
        n = lax.axis_size(axis)
        return lax.ppermute(value, axis, [(i, (i + step) % n) for i in range(n)])

    def swap_cores(value):
        return lax.ppermute(value, "vec", [(0, 1), (1, 0), (2, 3), (3, 2)])

    above = shift(own, "row", 1)
    below = shift(to_above, "row", -1)

    def packed(kernel, rows, name, *values):
        shape = jax.ShapeDtypeStruct((rows, LANES), F32)
        to_left, to_right = pl.pallas_call(
            kernel,
            out_shape=(shape, shape),
            in_specs=[VMEM_SPEC] * len(values),
            out_specs=(VMEM_SPEC,) * 2,
            compiler_params=params(6),
            name=name,
        )(*values)
        return shift(to_left, "col", -1), shift(to_right, "col", 1)

    spread = (coefs[:, None, :, None] * jnp.eye(8, dtype=F32)[None, :, None, :]).reshape(
        8 * TERMS, 16 * HALF
    )
    rounded = lax.reduce_precision(spread, exponent_bits=8, mantissa_bits=7)
    high, low = rounded.astype(jnp.bfloat16), (spread - rounded).astype(jnp.bfloat16)
    coefs, high, low, late_own, late_chk = lax.optimization_barrier((coefs, high, low, own, chk))
    own_strips = packed(pack_own_kernel, OWN_ROWS, "pack_own", late_own, late_chk)
    edge_strips = packed(pack_edge_kernel, EDGE_ROWS, "pack_edge", above, below)
    weights = pl.pallas_call(
        weights_kernel,
        out_shape=jax.ShapeDtypeStruct((2, TERMS, ROWS, LANES), F32),
        in_specs=[SMEM_SPEC] + [VMEM_SPEC] * 2,
        out_specs=VMEM_SPEC,
        compiler_params=params(4),
        cost_estimate=pl.CostEstimate(flops=4_000_000, bytes_accessed=1_000_000, transcendentals=0),
        name="weights",
    )(coefs, late_own, res_other)

    weights, edge_strips = lax.optimization_barrier((weights, edge_strips))
    res_rows = slice(RES * ROWS, (RES + HALF) * ROWS)
    own_rows = slice(RES_GROUP * ROWS, GROUPS * ROWS)
    near_rows = slice(RES_GROUP * HALO, GROUPS * HALO)
    far_rows = slice(EDGE_FAR + HALO, EDGE_FAR + 2 * HALO)
    pieces = []
    for mine, edge in zip(own_strips, edge_strips):
        pieces += [mine[own_rows], edge[near_rows], edge[far_rows]]
    pieces += [above[res_rows], below[res_rows]]
    swapped = swap_cores(jnp.concatenate(pieces, axis=0))
    frame = (FPLANES, FEXT, LANES)
    states = pl.pallas_call(
        forward_kernel,
        out_shape=jax.ShapeDtypeStruct((TERMS, 4, ROWS, LANES), F32),
        in_specs=[SMEM_SPEC] + [VMEM_SPEC] * 8,
        out_specs=VMEM_SPEC,
        scratch_shapes=[
            pltpu.VMEM(frame, F32), pltpu.VMEM((FPLANES // 2, *frame[1:]), F32),
            pltpu.VMEM((3, *frame[1:]), F32),
        ],
        compiler_params=params(8),
        cost_estimate=pl.CostEstimate(flops=20_000_000, bytes_accessed=6_000_000, transcendentals=0),
        name="forward",
    )(scale, own, chk, above, below, *own_strips, *edge_strips)

    ext = (EXT, LANES)
    adjoint_out, grad = pl.pallas_call(
        adjoint_kernel,
        out_shape=(
            jax.ShapeDtypeStruct((2, 4, ROWS, LANES), F32),
            jax.ShapeDtypeStruct((ROWS, LANES), F32),
        ),
        in_specs=[SMEM_SPEC] + [VMEM_SPEC] * 12,
        out_specs=(VMEM_SPEC, VMEM_SPEC),
        scratch_shapes=[
            pltpu.VMEM((8, *ext), F32), pltpu.VMEM((4, *ext), F32),
            pltpu.VMEM((6, *ext), F32), pltpu.VMEM((3, *ext), F32),
            pltpu.VMEM((TERMS, *ext), F32), pltpu.VMEM((TERMS, *ext), F32),
            pltpu.VMEM((TERMS, *ext), F32),
        ],
        compiler_params=params(12),
        name="adjoint",
    )(
        scale, high, low, own, above, below, *own_strips, *edge_strips, swapped, states, weights
    )

    grad = jnp.sum(lax.all_gather(grad, "vec"), axis=0)
    return grad, adjoint_out


def solution(mesh):
    return jax.shard_map(
        per_device,
        mesh=mesh,
        in_specs=(
            P(None, None, "vec", "row", "col"),
            P(None, "vec", "row", "col"),
            P("vec", "row", "col"),
            P("row", "col"),
            P(),
            P(),
            P(None, "row", "col"),
            P(),
        ),
        out_specs=(P("row", "col"), P(None, "vec", "row", "col")),
        check_vma=False,
    )
```

```python
import functools
import math

import jax
import jax.numpy as jnp
from jax import lax
from jax.experimental import pallas as pl
from jax.experimental.pallas import tpu as pltpu
from jax.sharding import PartitionSpec as P

SEG = 16
MOMENTS = 1024
QMAX = 32767
TERMS = 2 * SEG
NVEC = 16
F32 = jnp.float32

ADJ, SGN, RES, ONS = 0, 8, 12, 20
PLANES = 21
HALF = 8
ROWS = 32
HALO = 32
EXT = ROWS + 2 * HALO
FHALO = 16
FEXT = ROWS + 2 * FHALO
LANES = 128
FPLANES = 16
MAIN = PLANES * ROWS
WIDE = EXT // 8
GROUPS = 5
RES_GROUP = 3
OWN_ONS = GROUPS * ROWS
OWN_CHK = OWN_ONS + 8
OWN_ROWS = OWN_CHK + 2 * ROWS
EDGE_FAR = GROUPS * HALO
FAR_GROUPS = ((ADJ, 8), (RES, 8), (SGN, 4))
EDGE_ONS = EDGE_FAR + len(FAR_GROUPS) * HALO
EDGE_CHK = EDGE_ONS + 8
EDGE_ROWS = EDGE_CHK + 4 * FHALO


def near_index(t):
    return t - 2 if t < 4 else t - 6


def far_index(t):
    return t if t < 2 else t - 8


def window_coefs(first_segment, energies):
    moment_order = first_segment[0] * SEG + jnp.arange(TERMS, dtype=jnp.int32)
    degree = moment_order.astype(jnp.float32)
    kernel_norm = float(MOMENTS + 1)
    angle_step = math.pi / kernel_norm
    jackson = (
        (kernel_norm - degree) * jnp.cos(angle_step * degree)
        + jnp.sin(angle_step * degree) * (math.cos(angle_step) / math.sin(angle_step))
    ) / kernel_norm
    factor = jnp.where(moment_order == 0, 1.0, 2.0).astype(jnp.float32)
    angles = jnp.arccos(energies)
    cosines = jnp.cos(degree[:, None] * angles[None, :])
    return (jackson * factor)[:, None] * cosines / (math.pi * jnp.sin(angles))[None, :]


def lane_iota():
    return lax.broadcasted_iota(jnp.int32, (8, LANES), 1)


def tile(ref, row):
    return ref[pl.ds(row, 8), :]


def main_tile(own, above, below, plane, t):
    section = (above, own, below)[t // 4]
    return tile(section, plane * ROWS + (t % 4) * 8)


def fwd_tile(chk, above, below, plane, t):
    if t < 2:
        return tile(above, MAIN + plane * FHALO + t * 8)
    if t < 6:
        return tile(chk, plane * ROWS + (t - 2) * 8)
    return tile(below, MAIN + plane * FHALO + (t - 6) * 8)


def prepare_kernel(
    core, scalar, adj, bits, pot, res, chk,
    to_below, to_above, chk_v, res_v, bits_v, pot_v, sems
):
    copies = []

    def start(src, dst):
        copy = pltpu.make_async_copy(src, dst, sems.at[len(copies)])
        copy.start()
        copies.append(copy)

    first_res = pl.multiple_of(core[0] * (HALF * ROWS), HALF * ROWS)
    start(bits, bits_v)
    start(pot, pot_v)
    for out, first in ((to_below, ROWS - FHALO), (to_above, 0)):
        start(adj, out.at[pl.ds(ADJ * ROWS, 8 * ROWS)])
        start(res.at[pl.ds(first_res, HALF * ROWS)], out.at[pl.ds(RES * ROWS, HALF * ROWS)])
        for plane in range(FPLANES):
            start(
                chk.at[pl.ds(plane * ROWS + first, FHALO)],
                out.at[pl.ds(MAIN + plane * FHALO, FHALO)],
            )
    start(chk, chk_v)
    start(res.at[pl.ds(pl.multiple_of(HALF * ROWS - first_res, HALF * ROWS), HALF * ROWS)], res_v)
    copies[0].wait()
    signs = (2 * bits_v[...] - 1).astype(F32) * (1.0 / NVEC)
    copies[1].wait()
    pot_factor = scalar[0]
    scale = 2.0 / (4.5 + QMAX * pot_factor)
    onsite = pot_v[...].astype(F32) * (pot_factor * scale)
    for out in (to_below, to_above):
        out[pl.ds(SGN * ROWS, 4 * ROWS), :] = signs
        out[pl.ds(ONS * ROWS, ROWS), :] = onsite
    for copy in copies[2:]:
        copy.wait()


def pack(tiles, row, to_left, to_right):
    lane = lane_iota()
    count = len(tiles)
    width = LANES // count
    group = lane // width
    left = right = None
    for j, value in enumerate(tiles):
        rolled = pltpu.roll(value, width * j, 1) if j else value
        left = rolled if j == 0 else jnp.where(group == j, rolled, left)
        right = rolled if j == 0 else jnp.where(group == (j + count - 1) % count, rolled, right)
    to_left[pl.ds(row, 8), :] = left
    to_right[pl.ds(row, 8), :] = right


def pack_own_kernel(own, chk, to_left, to_right):
    for g in range(GROUPS):
        for i in range(4):
            tiles = [tile(own, (4 * g + j) * ROWS + i * 8) for j in range(4)]
            pack(tiles, g * ROWS + i * 8, to_left, to_right)
    pack([tile(own, ONS * ROWS + j * 8) for j in range(4)], OWN_ONS, to_left, to_right)
    for g in range(2):
        for i in range(4):
            tiles = [tile(chk, (8 * g + j) * ROWS + i * 8) for j in range(8)]
            pack(tiles, OWN_CHK + g * ROWS + i * 8, to_left, to_right)


def pack_edge_kernel(above, below, to_left, to_right):
    def at(plane, t):
        return main_tile(None, above, below, plane, t)

    near, far = (2, 3, 8, 9), (0, 1, 10, 11)
    for t in near:
        for g in range(GROUPS):
            tiles = [at(4 * g + j, t) for j in range(4)]
            pack(tiles, g * HALO + near_index(t) * 8, to_left, to_right)
    for t in far:
        for g, (first, count) in enumerate(FAR_GROUPS):
            tiles = [at(first + j, t) for j in range(count)]
            tiles += [at(ONS, t)] * (8 - count)
            pack(tiles, EDGE_FAR + g * HALO + far_index(t) * 8, to_left, to_right)
    pack([at(ONS, t) for t in near], EDGE_ONS, to_left, to_right)
    for side, ref in enumerate((above, below)):
        for g in range(2):
            for i in range(2):
                tiles = [tile(ref, MAIN + (8 * g + j) * FHALO + i * 8) for j in range(8)]
                pack(tiles, EDGE_CHK + g * 2 * FHALO + side * FHALO + i * 8, to_left, to_right)


def unpack_strip(right, left, lane, j, count, turns=(0,)):
    width = LANES // count
    mixed = jnp.where(lane // width == j, tile(*right), tile(*left))
    shifts = [(LANES - width * j + turn * (LANES // 2)) % LANES for turn in turns]
    return [pltpu.roll(mixed, shift, 1) if shift else mixed for shift in shifts]


class Strips:
    def __init__(self, own_right, own_left, edge_right, edge_left, lane):
        self.own, self.edge, self.lane = (own_right, own_left), (edge_right, edge_left), lane

    def unpack(self, refs, row, j, count, turns):
        return unpack_strip((refs[0], row), (refs[1], row), self.lane, j, count, turns)

    def plane(self, index, t, turns=(0, 1)):
        g, j = index // 4, index % 4
        if 4 <= t < 8:
            return self.unpack(self.own, g * ROWS + (t - 4) * 8, j, 4, turns)
        if 2 <= t < 10:
            return self.unpack(self.edge, g * HALO + near_index(t) * 8, j, 4, turns)
        for g, (first, count) in enumerate(FAR_GROUPS):
            if first <= index < first + count:
                row = EDGE_FAR + g * HALO + far_index(t) * 8
                return self.unpack(self.edge, row, index - first, 8, turns)

    def onsite(self, t, turns=(0, 1)):
        if 4 <= t < 8:
            return self.unpack(self.own, OWN_ONS, t - 4, 4, turns)
        if 2 <= t < 10:
            return self.unpack(self.edge, EDGE_ONS, near_index(t), 4, turns)
        return self.unpack(self.edge, EDGE_FAR + 2 * HALO + far_index(t) * 8, 4, 8, turns)

    def checkpoint(self, plane, t, turns):
        g, j = plane // 8, plane % 8
        if 2 <= t < 6:
            return self.unpack(self.own, OWN_CHK + g * ROWS + (t - 2) * 8, j, 8, turns)
        at = EDGE_CHK + g * 2 * FHALO + (t if t < 2 else t - 4) * 8
        return self.unpack(self.edge, at, j, 8, turns)


SWAP_NEAR, SWAP_FAR = 2 * ROWS, 2 * ROWS + 2 * HALO
SWAP_SIDE = SWAP_FAR + HALO
SWAP_MAIN = 2 * SWAP_SIDE


def swapped_strip(swapped, lane, e, t):
    g, j, count = e // 4, e % 4, 4
    if 4 <= t < 8:
        row = g * ROWS + (t - 4) * 8
    elif 2 <= t < 10:
        row = SWAP_NEAR + g * HALO + near_index(t) * 8
    else:
        row, j, count = SWAP_FAR + far_index(t) * 8, e, 8
    return unpack_strip((swapped, row), (swapped, SWAP_SIDE + row), lane, j, count, (0, 1))


def splats(coef, t_term):
    return [jnp.full((8, LANES), coef[t_term, e], F32) for e in range(2 * HALF)]


def weigh(factors, planes):
    terms = [value * factor for value, factor in zip(planes, factors)]
    while len(terms) > 1:
        terms = [x + y for x, y in zip(terms[::2], terms[1::2])]
    return terms[0]


def phase_tiles(phase):
    return phase, EXT // 8 - phase


def weights_kernel(coef, own, res_other, out):
    def body(t_term, carry):
        factors = splats(coef, t_term)
        for i in range(4):
            planes = [tile(own, (RES + e) * ROWS + i * 8) for e in range(HALF)]
            planes += [tile(res_other, e * ROWS + i * 8) for e in range(HALF)]
            value = weigh(factors, planes)
            out[0, t_term, pl.ds(i * 8, 8), :] = value
            out[1, t_term, pl.ds(i * 8, 8), :] = turned(value)
        return carry

    lax.fori_loop(0, TERMS, body, 0)


def weigh_stacks(high, low, stacks, out, out_turned, t):
    first = TERMS - 8 * (min(t, 3) + 1)
    rows = slice(8 * first, 8 * TERMS)
    stack = jnp.concatenate([jnp.concatenate(stack, axis=0) for stack in stacks], axis=1)
    upper = stack.astype(jnp.bfloat16)
    lower = (stack - upper.astype(F32)).astype(jnp.bfloat16)

    def product(x, y):
        return jnp.dot(x[rows, :], y, preferred_element_type=F32)

    result = product(high, upper) + (product(high, lower) + product(low, upper))
    for n in range(first, TERMS):
        part = result[8 * (n - first) : 8 * (n - first) + 8]
        for at, value in ((t * 8, part[:, :LANES]), (EXT - 8 - t * 8, part[:, LANES:])):
            out[n, pl.ds(at, 8), :] = value
            if out_turned is not None:
                out_turned[n, pl.ds(at, 8), :] = turned(value)


def turned(value):
    return pltpu.roll(value, LANES // 2, 1)


def maybe_turned(value, turn):
    return turned(value) if turn else value


def paired(first, second_turned, lane):
    inner = (lane >= HALO) & (lane < LANES - HALO)
    return jnp.where(inner, second_turned, first)


class Stencil:
    def __init__(self):
        lane, sub = lane_iota(), lax.broadcasted_iota(jnp.int32, (8, LANES), 0)
        self.lane = lane
        self.seam = {p: lane == p for p in (0, LANES // 2 - 1, LANES // 2, LANES - 1)}
        self.first_sub, self.last_sub = sub == 0, sub == 7

    def side(self, values, shift, at_a, at_b):
        a, b, h = (pltpu.roll(v, shift, 1) for v in values)
        seam_a, seam_b = self.seam[at_a], self.seam[at_b]
        return (
            jnp.where(seam_a, h, a),
            jnp.where(seam_b, h, b),
            jnp.where(seam_a, a, jnp.where(seam_b, b, h)),
        )

    def tiles(self, refs, lo, hi, count):
        def load(t):
            return [ref[pl.ds(t * 8, 8), :] for ref in refs]

        def rolled(values, shift):
            return [pltpu.roll(v, shift, 0) for v in values]

        half = LANES // 2
        here = load(lo)
        here_up, here_down = rolled(here, 1), rolled(here, 7)
        prev_up = rolled(load(lo - 1), 1) if lo > 0 else here_up
        for t in range(lo, hi):
            after = load(t + 1) if t + 1 < count else here
            after_up, after_down = rolled(after, 1), rolled(after, 7)
            left = self.side(here, 1, 0, half)
            right = self.side(here, LANES - 1, LANES - 1, half - 1)
            sums = [
                (left[m] + right[m])
                + (
                    jnp.where(self.first_sub, prev_up[m], here_up[m])
                    + jnp.where(self.last_sub, after_down[m], here_down[m])
                )
                for m in range(3)
            ]
            yield t, here, sums
            here, prev_up, here_up, here_down = after, here_up, after_up, after_down


def forward_kernel(
    scale, own, chk, above, below, own_right, own_left, edge_right, edge_left,
    vs, fc, fh, on,
):
    stencil = Stencil()
    lane = stencil.lane
    strips = Strips(own_right, own_left, edge_right, edge_left, lane)
    s = jnp.full((8, LANES), scale[0], F32)
    for t in range(FEXT // 8):
        row = pl.ds(t * 8, 8)
        for plane in range(FPLANES):
            value = maybe_turned(fwd_tile(chk, above, below, plane, t), plane % 2)
            fc[plane, row, :] = value
            if 2 <= t < 6:
                segment, which, v = plane // 8, plane // 4 % 2, plane % 4
                vs[segment * SEG + which, v, pl.ds((t - 2) * 8, 8), :] = value
            if plane % 2:
                fh[plane // 2, row, :] = paired(
                    *strips.checkpoint(plane - 1, t, (0,)), *strips.checkpoint(plane, t, (1,)), lane
                )
        e = t + (HALO - FHALO) // 8
        centre, edge = main_tile(own, above, below, ONS, e), strips.onsite(e)
        on[0, row, :] = centre
        on[1, row, :] = turned(centre)
        on[2, row, :] = paired(*edge, lane)

    def group(segment, which, pair):
        at = segment * 4 + which * 2 + pair
        return [fc.at[2 * at], fc.at[2 * at + 1], fh.at[at]]

    def forward(k, new, old, lo, hi, planes=3):
        for segment in range(2):
            for pair in range(2):
                target = group(segment, old, pair)
                for t, values, sums in stencil.tiles(group(segment, new, pair), lo, hi, FEXT // 8):
                    row = pl.ds(t * 8, 8)
                    for m in range(planes):
                        value = on[m, row, :] * values[m] - s * sums[m] - target[m][row, :]
                        target[m][row, :] = value
                        if m < 2 and 2 <= t < 6:
                            vs[segment * SEG + k, 2 * pair + m, pl.ds((t - 2) * 8, 8), :] = value

    for start, stop, lo, hi in ((1, 3, 0, 8), (4, 7, 1, 7)):
        def body(i, carry, lo=lo, hi=hi):
            forward(2 * i, 1, 0, lo, hi)
            forward(2 * i + 1, 0, 1, lo, hi)
            return carry
        lax.fori_loop(start, stop, body, 0)
        forward(2 * stop, 1, 0, lo, hi)
        forward(2 * stop + 1, 0, 1, lo + 1, hi - 1, 3 if lo == 0 else 2)


def adjoint_kernel(
    scale, high, low, own, above, below, own_right, own_left, edge_right, edge_left, swapped,
    vs, own_weights,
    adj_out, grad_out,
    xc, xh, sg, on, wcs, wts, whs,
):
    stencil = Stencil()
    lane = stencil.lane
    strips = Strips(own_right, own_left, edge_right, edge_left, lane)
    s = jnp.full((8, LANES), scale[0], F32)

    for t in range(EXT // 8):
        row = pl.ds(t * 8, 8)
        for plane in range(8):
            xc[plane, row, :] = maybe_turned(main_tile(own, above, below, plane, t), plane % 2)
        for at in range(4):
            xh[at, row, :] = paired(
                *strips.plane(2 * at, t, (0,)), *strips.plane(2 * at + 1, t, (1,)), lane
            )
        for pair in range(2):
            first = SGN + 2 * pair
            for m in range(2):
                sg[3 * pair + m, row, :] = maybe_turned(
                    main_tile(own, above, below, first + m, t), m
                )
            sg[3 * pair + 2, row, :] = paired(
                *strips.plane(first, t, (0,)), *strips.plane(first + 1, t, (1,)), lane
            )
        centre, edge = main_tile(own, above, below, ONS, t), strips.onsite(t)
        on[0, row, :] = centre
        on[1, row, :] = turned(centre)
        on[2, row, :] = paired(*edge, lane)

    def halo_stack(t):
        values = [strips.plane(RES + e, t) for e in range(HALF)]
        values += [swapped_strip(swapped, lane, e, t) for e in range(HALF)]
        return [paired(*value, lane) for value in values]

    def centre_stack(t):
        at = SWAP_MAIN + t * 8 + (0 if t < 4 else (HALF - 2) * ROWS)
        return [main_tile(own, above, below, RES + e, t) for e in range(HALF)] + [
            tile(swapped, at + e * ROWS) for e in range(HALF)
        ]

    for t in range(EXT // 16):
        other = EXT // 8 - 1 - t
        weigh_stacks(high, low, (halo_stack(t), halo_stack(other)), whs, None, t)
        if t < 4:
            weigh_stacks(high, low, (centre_stack(t), centre_stack(other)), wcs, wts, t)

    def group(which, pair):
        at = which * 2 + pair
        return [xc.at[2 * at], xc.at[2 * at + 1], xh.at[at]]

    def weights_of(t_term, t):
        row = pl.ds(t * 8, 8)
        if 4 <= t < 8:
            local = pl.ds((t - 4) * 8, 8)
            centre = [own_weights[m, t_term, local, :] for m in range(2)]
        else:
            centre = [wcs[t_term, row, :], wts[t_term, row, :]]
        return centre + [whs[t_term, row, :]]

    def adjoint(t_term, new, old, lo, hi, grads, planes=3):
        grads = list(grads)
        for pair in range(2):
            target = group(old, pair)
            for t, values, sums in stencil.tiles(group(new, pair), lo, hi, EXT // 8):
                row = pl.ds(t * 8, 8)
                if 4 <= t < 8:
                    for m in range(2):
                        at = 4 * m + t - 4
                        state = vs[t_term, 2 * pair + m, pl.ds((t - 4) * 8, 8), :]
                        grads[at] = grads[at] + values[m] * state
                weights = weights_of(t_term, t)
                for m in range(planes):
                    target[m][row, :] = (
                        weights[m] * sg[3 * pair + m, row, :]
                        + (on[m, row, :] * values[m] - s * sums[m])
                        - target[m][row, :]
                    )
        return tuple(grads)

    grads = tuple(jnp.zeros((8, LANES), F32) for _ in range(8))
    for phase in range(4):
        lo, hi = phase_tiles(phase)
        def body(i, carry, phase=phase, lo=lo, hi=hi):
            t_term = TERMS - 1 - 8 * phase - 2 * i
            carry = adjoint(t_term, 0, 1, lo, hi, carry)
            return adjoint(t_term - 1, 1, 0, lo, hi, carry)
        grads = lax.fori_loop(0, 3, body, grads)
        last = TERMS - 8 * (phase + 1)
        grads = adjoint(last + 1, 0, 1, lo, hi, grads)
        grads = adjoint(last, 1, 0, lo + 1, hi - 1, grads, 3 if phase < 3 else 2)
    for i in range(4):
        grad_out[pl.ds(i * 8, 8), :] = (grads[i] + turned(grads[4 + i])) * s
    for which in range(2):
        for v in range(4):
            for i in range(4):
                value = xc[which * 4 + v, pl.ds(HALO + i * 8, 8), :]
                adj_out[which, v, pl.ds(i * 8, 8), :] = maybe_turned(value, v % 2)


VMEM_SPEC = pl.BlockSpec(memory_space=pltpu.VMEM)
SMEM_SPEC = pl.BlockSpec(memory_space=pltpu.SMEM)
HBM_SPEC = pl.BlockSpec(memory_space=pltpu.HBM)


def params(mib):
    return pltpu.CompilerParams(vmem_limit_bytes=mib * 1024 * 1024)


def per_device(
    checkpoints,
    adjoints_in,
    vector_bits,
    potential_int,
    pot_scale,
    energies,
    residual,
    first_segment,
):
    core = lax.axis_index("vec") % 2
    coefs = window_coefs(first_segment, energies)
    coefs = jnp.where(core == 0, coefs, jnp.roll(coefs, HALF, axis=1))
    core = core[None]
    scale = 2.0 / (4.5 + QMAX * pot_scale)
    chk = checkpoints.reshape(FPLANES * ROWS, LANES)
    res = residual.reshape(2 * HALF * ROWS, LANES)
    send = jax.ShapeDtypeStruct((MAIN + FPLANES * FHALO, LANES), F32)
    own, to_above, chk, res_other = pl.pallas_call(
        prepare_kernel,
        out_shape=(
            send,
            send,
            jax.ShapeDtypeStruct((FPLANES * ROWS, LANES), F32),
            jax.ShapeDtypeStruct((HALF * ROWS, LANES), F32),
        ),
        in_specs=[SMEM_SPEC] * 2 + [HBM_SPEC] * 5,
        out_specs=(VMEM_SPEC,) * 4,
        scratch_shapes=[
            pltpu.VMEM((4 * ROWS, LANES), jnp.int32),
            pltpu.VMEM((ROWS, LANES), jnp.int32),
            pltpu.SemaphoreType.DMA((4 + 2 * (2 + FPLANES),)),
        ],
        compiler_params=params(4),
        name="prepare",
    )(
        core,
        pot_scale,
        *(
            pltpu.with_memory_space_constraint(value, pltpu.HBM)
            for value in (
                adjoints_in.reshape(8 * ROWS, LANES),
                vector_bits.reshape(4 * ROWS, LANES),
                potential_int,
                res,
                chk,
            )
        ),
    )

    def shift(value, axis, step):
        n = lax.axis_size(axis)
        return lax.ppermute(value, axis, [(i, (i + step) % n) for i in range(n)])

    def swap_cores(value):
        return lax.ppermute(value, "vec", [(0, 1), (1, 0), (2, 3), (3, 2)])

    above = shift(own, "row", 1)
    below = shift(to_above, "row", -1)

    def packed(kernel, rows, name, *values):
        shape = jax.ShapeDtypeStruct((rows, LANES), F32)
        to_left, to_right = pl.pallas_call(
            kernel,
            out_shape=(shape, shape),
            in_specs=[VMEM_SPEC] * len(values),
            out_specs=(VMEM_SPEC,) * 2,
            compiler_params=params(6),
            name=name,
        )(*values)
        return shift(to_left, "col", -1), shift(to_right, "col", 1)

    spread = (coefs[:, None, :, None] * jnp.eye(8, dtype=F32)[None, :, None, :]).reshape(
        8 * TERMS, 16 * HALF
    )
    rounded = lax.reduce_precision(spread, exponent_bits=8, mantissa_bits=7)
    high, low = rounded.astype(jnp.bfloat16), (spread - rounded).astype(jnp.bfloat16)
    coefs, high, low, late_own, late_chk = lax.optimization_barrier((coefs, high, low, own, chk))
    own_strips = packed(pack_own_kernel, OWN_ROWS, "pack_own", late_own, late_chk)
    edge_strips = packed(pack_edge_kernel, EDGE_ROWS, "pack_edge", above, below)
    weights = pl.pallas_call(
        weights_kernel,
        out_shape=jax.ShapeDtypeStruct((2, TERMS, ROWS, LANES), F32),
        in_specs=[SMEM_SPEC] + [VMEM_SPEC] * 2,
        out_specs=VMEM_SPEC,
        compiler_params=params(4),
        cost_estimate=pl.CostEstimate(flops=4_000_000, bytes_accessed=1_000_000, transcendentals=0),
        name="weights",
    )(coefs, late_own, res_other)

    weights, edge_strips = lax.optimization_barrier((weights, edge_strips))
    res_rows = slice(RES * ROWS, (RES + HALF) * ROWS)
    own_rows = slice(RES_GROUP * ROWS, GROUPS * ROWS)
    near_rows = slice(RES_GROUP * HALO, GROUPS * HALO)
    far_rows = slice(EDGE_FAR + HALO, EDGE_FAR + 2 * HALO)
    pieces = []
    for mine, edge in zip(own_strips, edge_strips):
        pieces += [mine[own_rows], edge[near_rows], edge[far_rows]]
    pieces += [above[res_rows], below[res_rows]]
    swapped = swap_cores(jnp.concatenate(pieces, axis=0))
    frame = (FPLANES, FEXT, LANES)
    states = pl.pallas_call(
        forward_kernel,
        out_shape=jax.ShapeDtypeStruct((TERMS, 4, ROWS, LANES), F32),
        in_specs=[SMEM_SPEC] + [VMEM_SPEC] * 8,
        out_specs=VMEM_SPEC,
        scratch_shapes=[
            pltpu.VMEM(frame, F32), pltpu.VMEM((FPLANES // 2, *frame[1:]), F32),
            pltpu.VMEM((3, *frame[1:]), F32),
        ],
        compiler_params=params(8),
        cost_estimate=pl.CostEstimate(flops=20_000_000, bytes_accessed=6_000_000, transcendentals=0),
        name="forward",
    )(scale, own, chk, above, below, *own_strips, *edge_strips)

    ext = (EXT, LANES)
    adjoint_out, grad = pl.pallas_call(
        adjoint_kernel,
        out_shape=(
            jax.ShapeDtypeStruct((2, 4, ROWS, LANES), F32),
            jax.ShapeDtypeStruct((ROWS, LANES), F32),
        ),
        in_specs=[SMEM_SPEC] + [VMEM_SPEC] * 12,
        out_specs=(VMEM_SPEC, VMEM_SPEC),
        scratch_shapes=[
            pltpu.VMEM((8, *ext), F32), pltpu.VMEM((4, *ext), F32),
            pltpu.VMEM((6, *ext), F32), pltpu.VMEM((3, *ext), F32),
            pltpu.VMEM((TERMS, *ext), F32), pltpu.VMEM((TERMS, *ext), F32),
            pltpu.VMEM((TERMS, *ext), F32),
        ],
        compiler_params=params(12),
        name="adjoint",
    )(
        scale, high, low, own, above, below, *own_strips, *edge_strips, swapped, states, weights
    )

    grad = jnp.sum(lax.all_gather(grad, "vec"), axis=0)
    return grad, adjoint_out


def solution(mesh):
    return jax.shard_map(
        per_device,
        mesh=mesh,
        in_specs=(
            P(None, None, "vec", "row", "col"),
            P(None, "vec", "row", "col"),
            P("vec", "row", "col"),
            P("row", "col"),
            P(),
            P(),
            P(None, "row", "col"),
            P(),
        ),
        out_specs=(P("row", "col"), P(None, "vec", "row", "col")),
        check_vma=False,
    )
```

```python
import functools
import math

import jax
import jax.numpy as jnp
from jax import lax
from jax.experimental import pallas as pl
from jax.experimental.pallas import tpu as pltpu
from jax.sharding import PartitionSpec as P

SEG = 16
MOMENTS = 1024
QMAX = 32767
TERMS = 2 * SEG
NVEC = 16
F32 = jnp.float32

ADJ, SGN, RES, ONS = 0, 8, 12, 20
PLANES = 21
HALF = 8
ROWS = 32
HALO = 32
EXT = ROWS + 2 * HALO
FHALO = 16
FEXT = ROWS + 2 * FHALO
LANES = 128
FPLANES = 16
MAIN = PLANES * ROWS
WIDE = EXT // 8
GROUPS = 5
RES_GROUP = 3
OWN_ONS = GROUPS * ROWS
OWN_CHK = OWN_ONS + 8
OWN_ROWS = OWN_CHK + 2 * ROWS
EDGE_FAR = GROUPS * HALO
FAR_GROUPS = ((ADJ, 8), (RES, 8), (SGN, 4))
EDGE_ONS = EDGE_FAR + len(FAR_GROUPS) * HALO
EDGE_CHK = EDGE_ONS + 8
EDGE_ROWS = EDGE_CHK + 4 * FHALO


def near_index(t):
    return t - 2 if t < 4 else t - 6


def far_index(t):
    return t if t < 2 else t - 8


def window_coefs(first_segment, energies):
    moment_order = first_segment[0] * SEG + jnp.arange(TERMS, dtype=jnp.int32)
    degree = moment_order.astype(jnp.float32)
    kernel_norm = float(MOMENTS + 1)
    angle_step = math.pi / kernel_norm
    jackson = (
        (kernel_norm - degree) * jnp.cos(angle_step * degree)
        + jnp.sin(angle_step * degree) * (math.cos(angle_step) / math.sin(angle_step))
    ) / kernel_norm
    factor = jnp.where(moment_order == 0, 1.0, 2.0).astype(jnp.float32)
    angles = jnp.arccos(energies)
    cosines = jnp.cos(degree[:, None] * angles[None, :])
    return (jackson * factor)[:, None] * cosines / (math.pi * jnp.sin(angles))[None, :]


def lane_iota():
    return lax.broadcasted_iota(jnp.int32, (8, LANES), 1)


def tile(ref, row):
    return ref[pl.ds(row, 8), :]


def main_tile(own, above, below, plane, t):
    section = (above, own, below)[t // 4]
    return tile(section, plane * ROWS + (t % 4) * 8)


def fwd_tile(chk, above, below, plane, t):
    if t < 2:
        return tile(above, MAIN + plane * FHALO + t * 8)
    if t < 6:
        return tile(chk, plane * ROWS + (t - 2) * 8)
    return tile(below, MAIN + plane * FHALO + (t - 6) * 8)


def prepare_kernel(
    core, scalar, adj, bits, pot, res, chk,
    to_below, to_above, chk_v, res_v, bits_v, pot_v, sems
):
    copies = []

    def start(src, dst):
        copy = pltpu.make_async_copy(src, dst, sems.at[len(copies)])
        copy.start()
        copies.append(copy)

    first_res = pl.multiple_of(core[0] * (HALF * ROWS), HALF * ROWS)
    start(bits, bits_v)
    start(pot, pot_v)
    for out, first in ((to_below, ROWS - FHALO), (to_above, 0)):
        start(adj, out.at[pl.ds(ADJ * ROWS, 8 * ROWS)])
        start(res.at[pl.ds(first_res, HALF * ROWS)], out.at[pl.ds(RES * ROWS, HALF * ROWS)])
        start(
            chk.reshape(FPLANES, ROWS, LANES).at[:, pl.ds(first, FHALO)],
            out.at[pl.ds(MAIN, FPLANES * FHALO)].reshape(FPLANES, FHALO, LANES),
        )
    start(chk, chk_v)
    start(res.at[pl.ds(pl.multiple_of(HALF * ROWS - first_res, HALF * ROWS), HALF * ROWS)], res_v)
    copies[0].wait()
    signs = (2 * bits_v[...] - 1).astype(F32) * (1.0 / NVEC)
    copies[1].wait()
    pot_factor = scalar[0]
    scale = 2.0 / (4.5 + QMAX * pot_factor)
    onsite = pot_v[...].astype(F32) * (pot_factor * scale)
    for out in (to_below, to_above):
        out[pl.ds(SGN * ROWS, 4 * ROWS), :] = signs
        out[pl.ds(ONS * ROWS, ROWS), :] = onsite
    for copy in copies[2:]:
        copy.wait()


def pack(tiles, row, to_left, to_right):
    lane = lane_iota()
    count = len(tiles)
    width = LANES // count
    group = lane // width
    left = right = None
    for j, value in enumerate(tiles):
        rolled = pltpu.roll(value, width * j, 1) if j else value
        left = rolled if j == 0 else jnp.where(group == j, rolled, left)
        right = rolled if j == 0 else jnp.where(group == (j + count - 1) % count, rolled, right)
    to_left[pl.ds(row, 8), :] = left
    to_right[pl.ds(row, 8), :] = right


def pack_own_kernel(own, chk, to_left, to_right):
    for g in range(GROUPS):
        for i in range(4):
            tiles = [tile(own, (4 * g + j) * ROWS + i * 8) for j in range(4)]
            pack(tiles, g * ROWS + i * 8, to_left, to_right)
    pack([tile(own, ONS * ROWS + j * 8) for j in range(4)], OWN_ONS, to_left, to_right)
    for g in range(2):
        for i in range(4):
            tiles = [tile(chk, (8 * g + j) * ROWS + i * 8) for j in range(8)]
            pack(tiles, OWN_CHK + g * ROWS + i * 8, to_left, to_right)


def pack_edge_kernel(above, below, to_left, to_right):
    def at(plane, t):
        return main_tile(None, above, below, plane, t)

    near, far = (2, 3, 8, 9), (0, 1, 10, 11)
    for t in near:
        for g in range(GROUPS):
            tiles = [at(4 * g + j, t) for j in range(4)]
            pack(tiles, g * HALO + near_index(t) * 8, to_left, to_right)
    for t in far:
        for g, (first, count) in enumerate(FAR_GROUPS):
            tiles = [at(first + j, t) for j in range(count)]
            tiles += [at(ONS, t)] * (8 - count)
            pack(tiles, EDGE_FAR + g * HALO + far_index(t) * 8, to_left, to_right)
    pack([at(ONS, t) for t in near], EDGE_ONS, to_left, to_right)
    for side, ref in enumerate((above, below)):
        for g in range(2):
            for i in range(2):
                tiles = [tile(ref, MAIN + (8 * g + j) * FHALO + i * 8) for j in range(8)]
                pack(tiles, EDGE_CHK + g * 2 * FHALO + side * FHALO + i * 8, to_left, to_right)


def unpack_strip(right, left, lane, j, count, turns=(0,)):
    width = LANES // count
    mixed = jnp.where(lane // width == j, tile(*right), tile(*left))
    shifts = [(LANES - width * j + turn * (LANES // 2)) % LANES for turn in turns]
    return [pltpu.roll(mixed, shift, 1) if shift else mixed for shift in shifts]


class Strips:
    def __init__(self, own_right, own_left, edge_right, edge_left, lane):
        self.own, self.edge, self.lane = (own_right, own_left), (edge_right, edge_left), lane

    def unpack(self, refs, row, j, count, turns):
        return unpack_strip((refs[0], row), (refs[1], row), self.lane, j, count, turns)

    def plane(self, index, t, turns=(0, 1)):
        g, j = index // 4, index % 4
        if 4 <= t < 8:
            return self.unpack(self.own, g * ROWS + (t - 4) * 8, j, 4, turns)
        if 2 <= t < 10:
            return self.unpack(self.edge, g * HALO + near_index(t) * 8, j, 4, turns)
        for g, (first, count) in enumerate(FAR_GROUPS):
            if first <= index < first + count:
                row = EDGE_FAR + g * HALO + far_index(t) * 8
                return self.unpack(self.edge, row, index - first, 8, turns)

    def onsite(self, t, turns=(0, 1)):
        if 4 <= t < 8:
            return self.unpack(self.own, OWN_ONS, t - 4, 4, turns)
        if 2 <= t < 10:
            return self.unpack(self.edge, EDGE_ONS, near_index(t), 4, turns)
        return self.unpack(self.edge, EDGE_FAR + 2 * HALO + far_index(t) * 8, 4, 8, turns)

    def checkpoint(self, plane, t, turns):
        g, j = plane // 8, plane % 8
        if 2 <= t < 6:
            return self.unpack(self.own, OWN_CHK + g * ROWS + (t - 2) * 8, j, 8, turns)
        at = EDGE_CHK + g * 2 * FHALO + (t if t < 2 else t - 4) * 8
        return self.unpack(self.edge, at, j, 8, turns)


SWAP_NEAR, SWAP_FAR = 2 * ROWS, 2 * ROWS + 2 * HALO
SWAP_SIDE = SWAP_FAR + HALO
SWAP_MAIN = 2 * SWAP_SIDE


def swapped_strip(swapped, lane, e, t):
    g, j, count = e // 4, e % 4, 4
    if 4 <= t < 8:
        row = g * ROWS + (t - 4) * 8
    elif 2 <= t < 10:
        row = SWAP_NEAR + g * HALO + near_index(t) * 8
    else:
        row, j, count = SWAP_FAR + far_index(t) * 8, e, 8
    return unpack_strip((swapped, row), (swapped, SWAP_SIDE + row), lane, j, count, (0, 1))


def splats(coef, t_term):
    return [jnp.full((8, LANES), coef[t_term, e], F32) for e in range(2 * HALF)]


def weigh(factors, planes):
    terms = [value * factor for value, factor in zip(planes, factors)]
    while len(terms) > 1:
        terms = [x + y for x, y in zip(terms[::2], terms[1::2])]
    return terms[0]


def phase_tiles(phase):
    return phase, EXT // 8 - phase


def weights_kernel(coef, own, res_other, out):
    def body(t_term, carry):
        factors = splats(coef, t_term)
        for i in range(4):
            planes = [tile(own, (RES + e) * ROWS + i * 8) for e in range(HALF)]
            planes += [tile(res_other, e * ROWS + i * 8) for e in range(HALF)]
            value = weigh(factors, planes)
            out[0, t_term, pl.ds(i * 8, 8), :] = value
            out[1, t_term, pl.ds(i * 8, 8), :] = turned(value)
        return carry

    lax.fori_loop(0, TERMS, body, 0)


def weigh_stacks(high, low, stacks, out, out_turned, t):
    first = TERMS - 8 * (min(t, 3) + 1)
    rows = slice(8 * first, 8 * TERMS)
    stack = jnp.concatenate([jnp.concatenate(stack, axis=0) for stack in stacks], axis=1)
    upper = stack.astype(jnp.bfloat16)
    lower = (stack - upper.astype(F32)).astype(jnp.bfloat16)

    def product(x, y):
        return jnp.dot(x[rows, :], y, preferred_element_type=F32)

    result = product(high, upper) + (product(high, lower) + product(low, upper))
    for n in range(first, TERMS):
        part = result[8 * (n - first) : 8 * (n - first) + 8]
        for at, value in ((t * 8, part[:, :LANES]), (EXT - 8 - t * 8, part[:, LANES:])):
            out[n, pl.ds(at, 8), :] = value
            if out_turned is not None:
                out_turned[n, pl.ds(at, 8), :] = turned(value)


def turned(value):
    return pltpu.roll(value, LANES // 2, 1)


def maybe_turned(value, turn):
    return turned(value) if turn else value


def paired(first, second_turned, lane):
    inner = (lane >= HALO) & (lane < LANES - HALO)
    return jnp.where(inner, second_turned, first)


class Stencil:
    def __init__(self):
        lane, sub = lane_iota(), lax.broadcasted_iota(jnp.int32, (8, LANES), 0)
        self.lane = lane
        self.seam = {p: lane == p for p in (0, LANES // 2 - 1, LANES // 2, LANES - 1)}
        self.first_sub, self.last_sub = sub == 0, sub == 7

    def side(self, values, shift, at_a, at_b):
        a, b, h = (pltpu.roll(v, shift, 1) for v in values)
        seam_a, seam_b = self.seam[at_a], self.seam[at_b]
        return (
            jnp.where(seam_a, h, a),
            jnp.where(seam_b, h, b),
            jnp.where(seam_a, a, jnp.where(seam_b, b, h)),
        )

    def tiles(self, refs, lo, hi, count):
        def load(t):
            return [ref[pl.ds(t * 8, 8), :] for ref in refs]

        def rolled(values, shift):
            return [pltpu.roll(v, shift, 0) for v in values]

        half = LANES // 2
        here = load(lo)
        here_up, here_down = rolled(here, 1), rolled(here, 7)
        prev_up = rolled(load(lo - 1), 1) if lo > 0 else here_up
        for t in range(lo, hi):
            after = load(t + 1) if t + 1 < count else here
            after_up, after_down = rolled(after, 1), rolled(after, 7)
            left = self.side(here, 1, 0, half)
            right = self.side(here, LANES - 1, LANES - 1, half - 1)
            sums = [
                (left[m] + right[m])
                + (
                    jnp.where(self.first_sub, prev_up[m], here_up[m])
                    + jnp.where(self.last_sub, after_down[m], here_down[m])
                )
                for m in range(3)
            ]
            yield t, here, sums
            here, prev_up, here_up, here_down = after, here_up, after_up, after_down


def forward_kernel(
    scale, own, chk, above, below, own_right, own_left, edge_right, edge_left,
    vs, fc, fh, on,
):
    stencil = Stencil()
    lane = stencil.lane
    strips = Strips(own_right, own_left, edge_right, edge_left, lane)
    s = jnp.full((8, LANES), scale[0], F32)
    for t in range(FEXT // 8):
        row = pl.ds(t * 8, 8)
        for plane in range(FPLANES):
            value = maybe_turned(fwd_tile(chk, above, below, plane, t), plane % 2)
            fc[plane, row, :] = value
            if 2 <= t < 6:
                segment, which, v = plane // 8, plane // 4 % 2, plane % 4
                vs[segment * SEG + which, v, pl.ds((t - 2) * 8, 8), :] = value
            if plane % 2:
                fh[plane // 2, row, :] = paired(
                    *strips.checkpoint(plane - 1, t, (0,)), *strips.checkpoint(plane, t, (1,)), lane
                )
        e = t + (HALO - FHALO) // 8
        centre, edge = main_tile(own, above, below, ONS, e), strips.onsite(e)
        on[0, row, :] = centre
        on[1, row, :] = turned(centre)
        on[2, row, :] = paired(*edge, lane)

    def group(segment, which, pair):
        at = segment * 4 + which * 2 + pair
        return [fc.at[2 * at], fc.at[2 * at + 1], fh.at[at]]

    def forward(k, new, old, lo, hi, planes=3):
        for segment in range(2):
            for pair in range(2):
                target = group(segment, old, pair)
                for t, values, sums in stencil.tiles(group(segment, new, pair), lo, hi, FEXT // 8):
                    row = pl.ds(t * 8, 8)
                    for m in range(planes):
                        value = on[m, row, :] * values[m] - s * sums[m] - target[m][row, :]
                        target[m][row, :] = value
                        if m < 2 and 2 <= t < 6:
                            vs[segment * SEG + k, 2 * pair + m, pl.ds((t - 2) * 8, 8), :] = value

    for start, stop, lo, hi in ((1, 3, 0, 8), (4, 7, 1, 7)):
        def body(i, carry, lo=lo, hi=hi):
            forward(2 * i, 1, 0, lo, hi)
            forward(2 * i + 1, 0, 1, lo, hi)
            return carry
        lax.fori_loop(start, stop, body, 0)
        forward(2 * stop, 1, 0, lo, hi)
        forward(2 * stop + 1, 0, 1, lo + 1, hi - 1, 3 if lo == 0 else 2)


def adjoint_kernel(
    scale, high, low, own, above, below, own_right, own_left, edge_right, edge_left, swapped,
    vs, own_weights,
    adj_out, grad_out,
    xc, xh, sg, on, wcs, wts, whs,
):
    stencil = Stencil()
    lane = stencil.lane
    strips = Strips(own_right, own_left, edge_right, edge_left, lane)
    s = jnp.full((8, LANES), scale[0], F32)

    for t in range(EXT // 8):
        row = pl.ds(t * 8, 8)
        for plane in range(8):
            xc[plane, row, :] = maybe_turned(main_tile(own, above, below, plane, t), plane % 2)
        for at in range(4):
            xh[at, row, :] = paired(
                *strips.plane(2 * at, t, (0,)), *strips.plane(2 * at + 1, t, (1,)), lane
            )
        for pair in range(2):
            first = SGN + 2 * pair
            for m in range(2):
                sg[3 * pair + m, row, :] = maybe_turned(
                    main_tile(own, above, below, first + m, t), m
                )
            sg[3 * pair + 2, row, :] = paired(
                *strips.plane(first, t, (0,)), *strips.plane(first + 1, t, (1,)), lane
            )
        centre, edge = main_tile(own, above, below, ONS, t), strips.onsite(t)
        on[0, row, :] = centre
        on[1, row, :] = turned(centre)
        on[2, row, :] = paired(*edge, lane)

    def halo_stack(t):
        values = [strips.plane(RES + e, t) for e in range(HALF)]
        values += [swapped_strip(swapped, lane, e, t) for e in range(HALF)]
        return [paired(*value, lane) for value in values]

    def centre_stack(t):
        at = SWAP_MAIN + t * 8 + (0 if t < 4 else (HALF - 2) * ROWS)
        return [main_tile(own, above, below, RES + e, t) for e in range(HALF)] + [
            tile(swapped, at + e * ROWS) for e in range(HALF)
        ]

    for t in range(EXT // 16):
        other = EXT // 8 - 1 - t
        weigh_stacks(high, low, (halo_stack(t), halo_stack(other)), whs, None, t)
        if t < 4:
            weigh_stacks(high, low, (centre_stack(t), centre_stack(other)), wcs, wts, t)

    def group(which, pair):
        at = which * 2 + pair
        return [xc.at[2 * at], xc.at[2 * at + 1], xh.at[at]]

    def weights_of(t_term, t):
        row = pl.ds(t * 8, 8)
        if 4 <= t < 8:
            local = pl.ds((t - 4) * 8, 8)
            centre = [own_weights[m, t_term, local, :] for m in range(2)]
        else:
            centre = [wcs[t_term, row, :], wts[t_term, row, :]]
        return centre + [whs[t_term, row, :]]

    def adjoint(t_term, new, old, lo, hi, grads, planes=3):
        grads = list(grads)
        for pair in range(2):
            target = group(old, pair)
            for t, values, sums in stencil.tiles(group(new, pair), lo, hi, EXT // 8):
                row = pl.ds(t * 8, 8)
                if 4 <= t < 8:
                    for m in range(2):
                        at = 4 * m + t - 4
                        state = vs[t_term, 2 * pair + m, pl.ds((t - 4) * 8, 8), :]
                        grads[at] = grads[at] + values[m] * state
                weights = weights_of(t_term, t)
                for m in range(planes):
                    target[m][row, :] = (
                        weights[m] * sg[3 * pair + m, row, :]
                        + (on[m, row, :] * values[m] - s * sums[m])
                        - target[m][row, :]
                    )
        return tuple(grads)

    grads = tuple(jnp.zeros((8, LANES), F32) for _ in range(8))
    for phase in range(4):
        lo, hi = phase_tiles(phase)
        def body(i, carry, phase=phase, lo=lo, hi=hi):
            t_term = TERMS - 1 - 8 * phase - 2 * i
            carry = adjoint(t_term, 0, 1, lo, hi, carry)
            return adjoint(t_term - 1, 1, 0, lo, hi, carry)
        grads = lax.fori_loop(0, 3, body, grads)
        last = TERMS - 8 * (phase + 1)
        grads = adjoint(last + 1, 0, 1, lo, hi, grads)
        grads = adjoint(last, 1, 0, lo + 1, hi - 1, grads, 3 if phase < 3 else 2)
    for i in range(4):
        grad_out[pl.ds(i * 8, 8), :] = (grads[i] + turned(grads[4 + i])) * s
    for which in range(2):
        for v in range(4):
            for i in range(4):
                value = xc[which * 4 + v, pl.ds(HALO + i * 8, 8), :]
                adj_out[which, v, pl.ds(i * 8, 8), :] = maybe_turned(value, v % 2)


VMEM_SPEC = pl.BlockSpec(memory_space=pltpu.VMEM)
SMEM_SPEC = pl.BlockSpec(memory_space=pltpu.SMEM)
HBM_SPEC = pl.BlockSpec(memory_space=pltpu.HBM)


def params(mib):
    return pltpu.CompilerParams(vmem_limit_bytes=mib * 1024 * 1024)


def per_device(
    checkpoints,
    adjoints_in,
    vector_bits,
    potential_int,
    pot_scale,
    energies,
    residual,
    first_segment,
):
    core = lax.axis_index("vec") % 2
    coefs = window_coefs(first_segment, energies)
    coefs = jnp.where(core == 0, coefs, jnp.roll(coefs, HALF, axis=1))
    core = core[None]
    scale = 2.0 / (4.5 + QMAX * pot_scale)
    chk = checkpoints.reshape(FPLANES * ROWS, LANES)
    res = residual.reshape(2 * HALF * ROWS, LANES)
    send = jax.ShapeDtypeStruct((MAIN + FPLANES * FHALO, LANES), F32)
    own, to_above, chk, res_other = pl.pallas_call(
        prepare_kernel,
        out_shape=(
            send,
            send,
            jax.ShapeDtypeStruct((FPLANES * ROWS, LANES), F32),
            jax.ShapeDtypeStruct((HALF * ROWS, LANES), F32),
        ),
        in_specs=[SMEM_SPEC] * 2 + [HBM_SPEC] * 5,
        out_specs=(VMEM_SPEC,) * 4,
        scratch_shapes=[
            pltpu.VMEM((4 * ROWS, LANES), jnp.int32),
            pltpu.VMEM((ROWS, LANES), jnp.int32),
            pltpu.SemaphoreType.DMA((10,)),
        ],
        compiler_params=params(4),
        name="prepare",
    )(
        core,
        pot_scale,
        *(
            pltpu.with_memory_space_constraint(value, pltpu.HBM)
            for value in (
                adjoints_in.reshape(8 * ROWS, LANES),
                vector_bits.reshape(4 * ROWS, LANES),
                potential_int,
                res,
                chk,
            )
        ),
    )

    def shift(value, axis, step):
        n = lax.axis_size(axis)
        return lax.ppermute(value, axis, [(i, (i + step) % n) for i in range(n)])

    def swap_cores(value):
        return lax.ppermute(value, "vec", [(0, 1), (1, 0), (2, 3), (3, 2)])

    above = shift(own, "row", 1)
    below = shift(to_above, "row", -1)

    def packed(kernel, rows, name, *values):
        shape = jax.ShapeDtypeStruct((rows, LANES), F32)
        to_left, to_right = pl.pallas_call(
            kernel,
            out_shape=(shape, shape),
            in_specs=[VMEM_SPEC] * len(values),
            out_specs=(VMEM_SPEC,) * 2,
            compiler_params=params(6),
            name=name,
        )(*values)
        return shift(to_left, "col", -1), shift(to_right, "col", 1)

    spread = (coefs[:, None, :, None] * jnp.eye(8, dtype=F32)[None, :, None, :]).reshape(
        8 * TERMS, 16 * HALF
    )
    rounded = lax.reduce_precision(spread, exponent_bits=8, mantissa_bits=7)
    high, low = rounded.astype(jnp.bfloat16), (spread - rounded).astype(jnp.bfloat16)
    coefs, high, low, late_own, late_chk = lax.optimization_barrier((coefs, high, low, own, chk))
    own_strips = packed(pack_own_kernel, OWN_ROWS, "pack_own", late_own, late_chk)
    edge_strips = packed(pack_edge_kernel, EDGE_ROWS, "pack_edge", above, below)
    weights = pl.pallas_call(
        weights_kernel,
        out_shape=jax.ShapeDtypeStruct((2, TERMS, ROWS, LANES), F32),
        in_specs=[SMEM_SPEC] + [VMEM_SPEC] * 2,
        out_specs=VMEM_SPEC,
        compiler_params=params(4),
        cost_estimate=pl.CostEstimate(flops=4_000_000, bytes_accessed=1_000_000, transcendentals=0),
        name="weights",
    )(coefs, late_own, res_other)

    weights, edge_strips = lax.optimization_barrier((weights, edge_strips))
    res_rows = slice(RES * ROWS, (RES + HALF) * ROWS)
    own_rows = slice(RES_GROUP * ROWS, GROUPS * ROWS)
    near_rows = slice(RES_GROUP * HALO, GROUPS * HALO)
    far_rows = slice(EDGE_FAR + HALO, EDGE_FAR + 2 * HALO)
    pieces = []
    for mine, edge in zip(own_strips, edge_strips):
        pieces += [mine[own_rows], edge[near_rows], edge[far_rows]]
    pieces += [above[res_rows], below[res_rows]]
    swapped = swap_cores(jnp.concatenate(pieces, axis=0))
    frame = (FPLANES, FEXT, LANES)
    states = pl.pallas_call(
        forward_kernel,
        out_shape=jax.ShapeDtypeStruct((TERMS, 4, ROWS, LANES), F32),
        in_specs=[SMEM_SPEC] + [VMEM_SPEC] * 8,
        out_specs=VMEM_SPEC,
        scratch_shapes=[
            pltpu.VMEM(frame, F32), pltpu.VMEM((FPLANES // 2, *frame[1:]), F32),
            pltpu.VMEM((3, *frame[1:]), F32),
        ],
        compiler_params=params(8),
        cost_estimate=pl.CostEstimate(flops=20_000_000, bytes_accessed=6_000_000, transcendentals=0),
        name="forward",
    )(scale, own, chk, above, below, *own_strips, *edge_strips)

    ext = (EXT, LANES)
    adjoint_out, grad = pl.pallas_call(
        adjoint_kernel,
        out_shape=(
            jax.ShapeDtypeStruct((2, 4, ROWS, LANES), F32),
            jax.ShapeDtypeStruct((ROWS, LANES), F32),
        ),
        in_specs=[SMEM_SPEC] + [VMEM_SPEC] * 12,
        out_specs=(VMEM_SPEC, VMEM_SPEC),
        scratch_shapes=[
            pltpu.VMEM((8, *ext), F32), pltpu.VMEM((4, *ext), F32),
            pltpu.VMEM((6, *ext), F32), pltpu.VMEM((3, *ext), F32),
            pltpu.VMEM((TERMS, *ext), F32), pltpu.VMEM((TERMS, *ext), F32),
            pltpu.VMEM((TERMS, *ext), F32),
        ],
        compiler_params=params(12),
        name="adjoint",
    )(
        scale, high, low, own, above, below, *own_strips, *edge_strips, swapped, states, weights
    )

    grad = jnp.sum(lax.all_gather(grad, "vec"), axis=0)
    return grad, adjoint_out


def solution(mesh):
    return jax.shard_map(
        per_device,
        mesh=mesh,
        in_specs=(
            P(None, None, "vec", "row", "col"),
            P(None, "vec", "row", "col"),
            P("vec", "row", "col"),
            P("row", "col"),
            P(),
            P(),
            P(None, "row", "col"),
            P(),
        ),
        out_specs=(P("row", "col"), P(None, "vec", "row", "col")),
        check_vma=False,
    )
```
